32 devices in a mesh: fsdp: 2 (over y), ctx: 4 (over z), tp: 4 (over x, core).
Axes of the slice: x: 2, y: 2, z: 4, core: 2. Of those that a mesh axis runs over, the one named last changes fastest.
Arguments:
- block_input: bfloat16 [4, 4096, 1280], P('fsdp', 'ctx', 'tp'), may hold values from -6 to 6
- cotangent: bfloat16 [4, 4096, 1280], P('fsdp', 'ctx', 'tp'), may hold values from -6 to 6
- norm1_gain: float32 [1280], replicated, may hold values from 0.25 to 1.75
- norm1_shift: float32 [1280], replicated, may hold values from -1.75 to 1.75
- w_qkv: bfloat16 [1280, 3, 1280], P('fsdp', None, 'tp'), may hold values from -0.15625 to 0.15625
- table_rows: bfloat16 [127, 80], replicated, may hold values from -0.5 to 0.5
- table_cols: bfloat16 [127, 80], replicated, may hold values from -0.5 to 0.5
- w_proj: bfloat16 [1280, 1280], P('tp', 'fsdp'), may hold values from -3.5 to 3.5
- norm2_gain: float32 [1280], replicated, may hold values from 0.25 to 1.75
- norm2_shift: float32 [1280], replicated, may hold values from -1.75 to 1.75
- w_fc1: bfloat16 [1280, 5120], P('fsdp', 'tp'), may hold values from -0.15625 to 0.15625
- w_fc2: bfloat16 [5120, 1280], P('tp', 'fsdp'), may hold values from -0.078125 to 0.078125
- index_rows: int32 [64, 64], replicated, may hold values from 0 to 126, as said below
- index_cols: int32 [64, 64], replicated, may hold values from 0 to 126, as said below
Outputs:
- block_output: bfloat16 [4, 4096, 1280], P('fsdp', 'ctx', 'tp')
- input_grad: float32 [4, 4096, 1280], P('fsdp', 'ctx', 'tp')
- grad_norm1_gain: float32 [1280], replicated
- grad_norm1_shift: float32 [1280], replicated
- grad_w_qkv: float32 [1280, 3, 1280], P(('fsdp', 'ctx'), None, 'tp')
- grad_table_rows: float32 [127, 80], replicated
- grad_table_cols: float32 [127, 80], replicated
- grad_w_proj: float32 [1280, 1280], P('tp', ('fsdp', 'ctx'))
- grad_norm2_gain: float32 [1280], replicated
- grad_norm2_shift: float32 [1280], replicated
- grad_w_fc1: float32 [1280, 5120], P(('fsdp', 'ctx'), 'tp')
- grad_w_fc2: float32 [5120, 1280], P('tp', ('fsdp', 'ctx'))
The draws below stay inside these ranges and needn't reach their ends.
Inputs may be any that keep to these rules, and one draw needn't show every extreme that they name: index_rows[y, k] depends only on y - k, and different offsets give different entries. index_cols[x, k] depends only on x - k, and different offsets give different entries.
All inputs are finite; a program needn't handle non-finite values.
Results may differ from the reference program's by a relative error of at most 0.022.
Values may be sent and summed in bfloat16 or wider, within the bound.
A program may use at most 256 MiB of HBM per device.

```python
import jax
import jax.numpy as jnp
from jax import lax

D = 1280
HEADS = 16
HD = 80
FF = 5120
GRID = 64
SEQ = 4096
TAB = 127
IMAGES = 4


def offset_table(key, salt_value):
    row_order = jax.random.permutation(jax.random.fold_in(key, salt_value), TAB).astype(jnp.int32)
    grid_places = jnp.arange(GRID, dtype=jnp.int32)
    return row_order[grid_places[:, None] - grid_places[None, :] + GRID - 1].astype(jnp.int32)


def draw_index_rows(key, part):
    return offset_table(key, 11)


def draw_index_cols(key, part):
    return offset_table(key, 23)


def shard_levels(rng, shape, split, least, high):
    level, own = 1.0, jax.random.fold_in(rng, 6)
    for position, parts in split:
        heights = jnp.exp(jax.random.uniform(jax.random.fold_in(own, position), (parts,), jnp.float32, least / len(split), high / len(split)))
        level = level * jnp.repeat(heights, shape[position] // parts).reshape([-1 if axis == position else 1 for axis in range(len(shape))])
    return level


def centred(stream_key, shape, deviation, reach, cuts=(), held_as=jnp.bfloat16):
    drawn = deviation * jax.random.normal(stream_key, shape, jnp.float32)
    if cuts:
        drawn = drawn * shard_levels(stream_key, shape, cuts, -0.22, 0.18)
    return jnp.clip(drawn, -reach, reach).astype(held_as)


def setup_inputs(seed: int = 0) -> dict:
    seeds = jax.random.split(jax.random.key(seed), 15)
    return {
        "block_input": centred(seeds[0], (IMAGES, SEQ, D), 1.0, 6.0, ((0, 2), (1, 4), (2, 4))),
        "cotangent": centred(seeds[1], (IMAGES, SEQ, D), 1.0, 6.0, ((0, 2), (1, 4), (2, 4))),
        "norm1_gain": jnp.clip(1.0 + 0.15 * jax.random.normal(seeds[2], (D,), jnp.float32), 0.25, 1.75),
        "norm1_shift": centred(seeds[3], (D,), 0.3, 1.75, (), jnp.float32),
        "w_qkv": centred(seeds[4], (D, 3, D), D ** -0.5, 0.15625, ((0, 2), (2, 4))),
        "table_rows": centred(seeds[5], (TAB, HD), 0.08, 0.5),
        "table_cols": centred(seeds[6], (TAB, HD), 0.08, 0.5),
        "w_proj": centred(seeds[7], (D, D), 0.6, 3.5, ((0, 4), (1, 2))),
        "norm2_gain": jnp.clip(1.0 + 0.15 * jax.random.normal(seeds[8], (D,), jnp.float32), 0.25, 1.75),
        "norm2_shift": centred(seeds[9], (D,), 0.3, 1.75, (), jnp.float32),
        "w_fc1": centred(seeds[10], (D, FF), D ** -0.5, 0.15625, ((0, 2), (1, 4))),
        "w_fc2": centred(seeds[11], (FF, D), FF ** -0.5, 0.078125, ((0, 4), (1, 2))),
        "index_rows": draw_index_rows(jax.random.fold_in(seeds[14], 71), 0),
        "index_cols": draw_index_cols(jax.random.fold_in(seeds[14], 71), 0),
    }


epsilon = 1e-06
highest = lax.Precision.HIGHEST

@jax.custom_vjp
def low(v):
    return lax.optimization_barrier(v.astype(jnp.bfloat16)).astype(jnp.float32)

@jax.custom_vjp
def low_back(v):
    return v

def low_keep(v):
    return (low(v), None)

def low_pass(kept, grad):
    return (grad,)

def back_keep(v):
    return (v, None)

def back_low(kept, grad):
    return (low(grad),)
low.defvjp(low_keep, low_pass)
low_back.defvjp(back_keep, back_low)

def layer_norm(values, gain_vec, shift_vec):
    center = values - lax.optimization_barrier(jnp.mean(values, axis=-1, keepdims=True))
    return center * lax.rsqrt(lax.optimization_barrier(jnp.mean(center * center, axis=-1, keepdims=True)) + epsilon) * gain_vec + shift_vec

def gelu_exact(values):
    return 0.5 * values * (1.0 + lax.erf(values * 0.7071067811865476))

def attend_block(queries, rows_term, cols_term, key_part, value_part):
    scores = jnp.einsum('qhc,khc->hqk', queries, key_part, precision=highest) * HD ** (-0.5)
    rel_bias = (rows_term[:, :, :, None] + cols_term[:, :, None, :]).reshape(queries.shape[0], HEADS, SEQ)
    scores = low_back(scores + jnp.transpose(rel_bias, (1, 0, 2)))
    exp_scores = jnp.exp(scores - lax.optimization_barrier(jnp.max(scores, axis=-1, keepdims=True)))
    soft_probs = exp_scores / lax.optimization_barrier(jnp.sum(exp_scores, axis=-1, keepdims=True))
    return jnp.einsum('hqk,khc->qhc', low(soft_probs), value_part, precision=highest)

def image_forward(tokens, params, hot_rows, hot_cols):
    gain_one, shift_one, weight_qkv, rows_tab, cols_tab, weight_proj, gain_two, shift_two, weight_up, weight_down = params
    normed = low(layer_norm(tokens, gain_one, shift_one))
    mixed_qkv = jnp.dot(normed, weight_qkv.reshape(D, 3 * D), precision=highest)
    mixed_qkv = low(low_back(mixed_qkv)).reshape(SEQ, 3, HEADS, HD)
    queries = mixed_qkv[:, 0]
    key_part = mixed_qkv[:, 1]
    value_part = mixed_qkv[:, 2]
    rows_table = jnp.dot(hot_rows, rows_tab, precision=highest).reshape(GRID, GRID, HD)
    cols_table = jnp.dot(hot_cols, cols_tab, precision=highest).reshape(GRID, GRID, HD)
    shaped = queries.reshape(GRID, GRID, HEADS, HD)
    rows_term = jnp.einsum('yxhc,ykc->yxhk', shaped, rows_table, precision=highest).reshape(SEQ, HEADS, GRID)
    cols_term = jnp.einsum('yxhc,xkc->yxhk', shaped, cols_table, precision=highest).reshape(SEQ, HEADS, GRID)
    block_span = min(512, SEQ)
    block_count = SEQ // block_span

    def one_block(pieces):
        return attend_block(pieces[0], pieces[1], pieces[2], key_part, value_part)
    attended = lax.map(jax.checkpoint(one_block), (queries.reshape(block_count, block_span, HEADS, HD), rows_term.reshape(block_count, block_span, HEADS, GRID), cols_term.reshape(block_count, block_span, HEADS, GRID)))
    attended = low(low_back(attended.reshape(SEQ, D)))
    middle = tokens + low_back(jnp.dot(attended, weight_proj, precision=highest))
    second = low(layer_norm(middle, gain_two, shift_two))
    hidden = low(gelu_exact(low_back(jnp.dot(second, weight_up, precision=highest))))
    return middle + low_back(jnp.dot(hidden, weight_down, precision=highest))

def reference(block_input, cotangent, norm1_gain, norm1_shift, w_qkv, table_rows, table_cols, w_proj, norm2_gain, norm2_shift, w_fc1, w_fc2, index_rows, index_cols):
    levels = jnp.arange(TAB, dtype=jnp.int32)
    hot_rows = (index_rows.reshape(-1)[:, None] == levels[None, :]).astype(jnp.float32)
    hot_cols = (index_cols.reshape(-1)[:, None] == levels[None, :]).astype(jnp.float32)
    params = (norm1_gain.astype(jnp.float32), norm1_shift.astype(jnp.float32), w_qkv.astype(jnp.float32), table_rows.astype(jnp.float32), table_cols.astype(jnp.float32), w_proj.astype(jnp.float32), norm2_gain.astype(jnp.float32), norm2_shift.astype(jnp.float32), w_fc1.astype(jnp.float32), w_fc2.astype(jnp.float32))

    def run_forward(tokens, weights):
        return image_forward(tokens, weights, hot_rows, hot_cols)

    def per_image(totals, pieces):
        one_image, one_grad = pieces
        result, pullback = jax.vjp(run_forward, one_image.astype(jnp.float32), params)
        grad_tokens, grad_weights = pullback(one_grad.astype(jnp.float32))
        totals = jax.tree.map(lambda earlier, adding: earlier + adding, totals, grad_weights)
        return (totals, (result.astype(jnp.bfloat16), grad_tokens))
    zero_grads = jax.tree.map(jnp.zeros_like, params)
    totals, (outputs, input_grads) = lax.scan(per_image, zero_grads, (block_input, cotangent))
    return (outputs, input_grads, totals[0], totals[1], totals[2], totals[3], totals[4], totals[5], totals[6], totals[7], totals[8], totals[9])
```

```python
import functools
import math

import jax
import jax.numpy as jnp
from jax import lax
from jax.experimental import pallas as pl
from jax.experimental.pallas import tpu as pltpu
from jax.sharding import PartitionSpec as P

MICRO = 2


epsilon = 1e-06
highest = lax.Precision.HIGHEST
block_rows = 512
lowest = -1e30


def layer_norm(values, gain_vec, shift_vec):
    center = values - jnp.mean(values, axis=-1, keepdims=True)
    inv_std = lax.rsqrt(jnp.mean(center * center, axis=-1, keepdims=True) + epsilon)
    normed = center * inv_std
    return (normed * gain_vec + shift_vec, normed, inv_std)


def norm_back(upstream, normed, inv_std, gain_vec):
    scaled = upstream * gain_vec
    inner = (
        scaled
        - jnp.mean(scaled, axis=-1, keepdims=True)
        - normed * jnp.mean(scaled * normed, axis=-1, keepdims=True)
    )
    return inner * inv_std


def gelu_pair(values):
    normal_cdf = 0.5 * (1.0 + lax.erf(values * 0.7071067811865476))
    normal_pdf = jnp.exp(-0.5 * values * values) * 0.3989422804014327
    return (values * normal_cdf, normal_cdf + values * normal_pdf)


def rel_terms(queries, band_table, cols_table, grid_side):
    shape_in = queries.shape
    shaped = queries.astype(jnp.float32).reshape(
        shape_in[0], shape_in[1] // grid_side, grid_side, shape_in[2], shape_in[3]
    )
    rows_term = jnp.einsum("byxhc,ykc->byxhk", shaped, band_table, precision=highest)
    cols_term = jnp.einsum("byxhc,xkc->byxhk", shaped, cols_table, precision=highest)
    return (
        rows_term.reshape(shape_in[:3] + (grid_side,)),
        cols_term.reshape(shape_in[:3] + (grid_side,)),
    )


def key_bias(rows_term, cols_term, first_key, key_count, grid_side):
    picked = lax.dynamic_slice_in_dim(rows_term, first_key // grid_side, key_count // grid_side, 3)
    joined = picked[..., :, None] + cols_term[..., None, :]
    return joined.reshape(picked.shape[:3] + (key_count,))


def bias_back(grad_logits, first_key, key_count, grid_side):
    split = grad_logits.reshape(grad_logits.shape[:3] + (key_count // grid_side, grid_side))
    empty = jnp.zeros(grad_logits.shape[:3] + (grid_side,), jnp.float32)
    rows_part = lax.dynamic_update_slice_in_dim(
        empty, jnp.sum(split, axis=4), first_key // grid_side, 3
    )
    return (rows_part, jnp.sum(split, axis=3))


def scores_of(queries, key_blk, rows_term, cols_term, first_key, score_scale, grid_side):
    raw_dots = jnp.einsum("brhc,bkhc->bhrk", queries, key_blk, preferred_element_type=jnp.float32)
    return raw_dots * score_scale + key_bias(
        rows_term, cols_term, first_key, key_blk.shape[1], grid_side
    )


def plain_device(
    block_input,
    cotangent,
    norm1_gain,
    norm1_shift,
    w_qkv,
    table_rows,
    table_cols,
    w_proj,
    norm2_gain,
    norm2_shift,
    w_fc1,
    w_fc2,
    index_rows,
    index_cols,
):
    grid_side = index_rows.shape[0]
    table_len = table_rows.shape[0]
    head_dim = table_rows.shape[1]
    model_width = norm1_gain.shape[0]
    band_len = block_input.shape[1]
    band_grid = band_len // grid_side
    local_heads = w_proj.shape[0] // head_dim
    hidden_local = w_fc1.shape[1]
    per_micro = block_input.shape[0] // MICRO
    score_scale = head_dim ** (-0.5)
    ctx_place = lax.axis_index("ctx")
    whole_seq = band_len * lax.axis_size("ctx")
    levels = jnp.arange(table_len, dtype=jnp.int32)
    hot_rows = (index_rows.reshape(-1)[:, None] == levels[None, :]).astype(jnp.float32)
    hot_cols = (index_cols.reshape(-1)[:, None] == levels[None, :]).astype(jnp.float32)
    rows_table = jnp.dot(hot_rows, table_rows.astype(jnp.float32), precision=highest).reshape(
        grid_side, grid_side, head_dim
    )
    cols_table = jnp.dot(hot_cols, table_cols.astype(jnp.float32), precision=highest).reshape(
        grid_side, grid_side, head_dim
    )
    band_table = lax.dynamic_slice_in_dim(rows_table, ctx_place * band_grid, band_grid, 0)
    band_hot = lax.dynamic_slice_in_dim(
        hot_rows.reshape(grid_side, grid_side, table_len), ctx_place * band_grid, band_grid, 0
    )
    cols_hot = hot_cols.reshape(grid_side, grid_side, table_len)
    over_rows = (((0,), (0,)), ((), ()))
    over_cols = (((1,), (1,)), ((), ()))
    qkv_width = 3 * local_heads * head_dim
    grad_qkv = jnp.zeros((model_width, qkv_width), jnp.float32)
    grad_proj = jnp.zeros((local_heads * head_dim, model_width), jnp.float32)
    grad_up = jnp.zeros((model_width, hidden_local), jnp.float32)
    grad_down = jnp.zeros((hidden_local, model_width), jnp.float32)
    gain_one = jnp.zeros((model_width,), jnp.float32)
    shift_one = jnp.zeros((model_width,), jnp.float32)
    gain_two = jnp.zeros((model_width,), jnp.float32)
    shift_two = jnp.zeros((model_width,), jnp.float32)
    grad_rows_tab = jnp.zeros((table_len, head_dim), jnp.float32)
    grad_cols_tab = jnp.zeros((table_len, head_dim), jnp.float32)
    outputs = []
    input_grads = []
    for micro_step in range(MICRO):
        input_part = block_input[micro_step * per_micro : (micro_step + 1) * per_micro]
        grad_part = cotangent[micro_step * per_micro : (micro_step + 1) * per_micro]
        images = input_part.shape[0]
        tokens = images * band_len
        full_qkv, full_proj, full_up, full_down = (
            lax.all_gather(w_qkv, "fsdp", axis=0, tiled=True),
            lax.all_gather(w_proj, "fsdp", axis=1, tiled=True),
            lax.all_gather(w_fc1, "fsdp", axis=0, tiled=True),
            lax.all_gather(w_fc2, "fsdp", axis=1, tiled=True),
        )
        flat_qkv = full_qkv.reshape(model_width, qkv_width)
        input_full, grad_out_full = (
            lax.all_gather(input_part, "tp", axis=2, tiled=True),
            lax.all_gather(grad_part, "tp", axis=2, tiled=True),
        )
        normed_in, normed1, inv_std1 = layer_norm(
            input_full.astype(jnp.float32), norm1_gain, norm1_shift
        )
        first_act = normed_in.astype(jnp.bfloat16).reshape(tokens, model_width)
        mixed_qkv = jnp.dot(first_act, flat_qkv, preferred_element_type=jnp.float32).astype(
            jnp.bfloat16
        )
        mixed_qkv = mixed_qkv.reshape(images, band_len, 3, local_heads, head_dim)
        queries = mixed_qkv[:, :, 0]
        key_part = mixed_qkv[:, :, 1]
        value_part = mixed_qkv[:, :, 2]
        rows_term, cols_term = rel_terms(queries, band_table, cols_table, grid_side)
        rows_swap = jnp.transpose(rows_term, (0, 2, 1, 3))
        cols_swap = jnp.transpose(cols_term, (0, 2, 1, 3))
        fold_init = (
            jnp.full((images, local_heads, band_len), lowest, jnp.float32),
            jnp.zeros((images, local_heads, band_len), jnp.float32),
            jnp.zeros((images, local_heads, band_len, head_dim), jnp.float32),
        )
        key_piece = lax.all_gather(key_part, "ctx", axis=1, tiled=True)
        value_piece = lax.all_gather(value_part, "ctx", axis=1, tiled=True)
        piece_len = key_piece.shape[1]
        sub_len = math.gcd(piece_len, block_rows)

        def forward_advance(block_idx, state):
            running, denom_sum, acc_out = state
            offset = block_idx * sub_len
            key_blk = lax.dynamic_slice_in_dim(key_piece, offset, sub_len, 1)
            value_blk = lax.dynamic_slice_in_dim(value_piece, offset, sub_len, 1)
            logits = scores_of(
                queries, key_blk, rows_swap, cols_swap, offset, score_scale, grid_side
            )
            new_peak = jnp.maximum(running, jnp.max(logits, axis=-1))
            rescale = jnp.exp(running - new_peak)
            weights = jnp.exp(logits - new_peak[..., None])
            denom_sum = denom_sum * rescale + jnp.sum(weights, axis=-1)
            acc_out = acc_out * rescale[..., None] + jnp.einsum(
                "bhrk,bkhc->bhrc",
                weights.astype(jnp.bfloat16),
                value_blk,
                preferred_element_type=jnp.float32,
            )
            return (new_peak, denom_sum, acc_out)

        peak_all, denom_all, acc_all = lax.fori_loop(
            0, piece_len // sub_len, forward_advance, fold_init
        )
        attn_exact = jnp.transpose(acc_all / denom_all[..., None], (0, 2, 1, 3))
        log_total = peak_all + jnp.log(denom_all)
        attn_low = attn_exact.astype(jnp.bfloat16).reshape(tokens, local_heads * head_dim)
        attn_branch = jnp.dot(attn_low, full_proj, preferred_element_type=jnp.float32).reshape(
            images, band_len, model_width
        )
        attn_share = lax.psum_scatter(
            attn_branch.astype(jnp.bfloat16), "tp", scatter_dimension=2, tiled=True
        ).astype(jnp.float32)
        middle_share = input_part.astype(jnp.float32) + attn_share
        middle_full = lax.all_gather(
            middle_share.astype(jnp.bfloat16), "tp", axis=2, tiled=True
        ).astype(middle_share.dtype)
        normed_mid, normed2, inv_std2 = layer_norm(middle_full, norm2_gain, norm2_shift)
        second_act = normed_mid.astype(jnp.bfloat16).reshape(tokens, model_width)
        pre_act = jnp.dot(second_act, full_up, preferred_element_type=jnp.float32)
        gelu_out, gelu_slope = gelu_pair(pre_act)
        hidden_low = gelu_out.astype(jnp.bfloat16)
        mlp_branch = jnp.dot(hidden_low, full_down, preferred_element_type=jnp.float32).reshape(
            images, band_len, model_width
        )
        mlp_share = lax.psum_scatter(
            mlp_branch.astype(jnp.bfloat16), "tp", scatter_dimension=2, tiled=True
        ).astype(jnp.float32)
        outputs.append((middle_share + mlp_share).astype(jnp.bfloat16))
        grad_out_flat = grad_out_full.reshape(tokens, model_width)
        grad_down = grad_down + lax.dot_general(
            hidden_low, grad_out_flat, over_rows, preferred_element_type=jnp.float32
        )
        grad_hidden = lax.dot_general(
            grad_out_flat, full_down, over_cols, preferred_element_type=jnp.float32
        )
        grad_pre = (grad_hidden * gelu_slope).astype(jnp.bfloat16)
        grad_up = grad_up + lax.dot_general(
            second_act, grad_pre, over_rows, preferred_element_type=jnp.float32
        )
        grad_second = lax.dot_general(
            grad_pre, full_up, over_cols, preferred_element_type=jnp.float32
        ).reshape(images, band_len, model_width)
        gain_two = gain_two + jnp.sum(grad_second * normed2, axis=(0, 1))
        shift_two = shift_two + jnp.sum(grad_second, axis=(0, 1))
        grad_middle = grad_part.astype(jnp.float32) + lax.psum_scatter(
            norm_back(grad_second, normed2, inv_std2, norm2_gain).astype(jnp.bfloat16),
            "tp",
            scatter_dimension=2,
            tiled=True,
        ).astype(jnp.float32)
        grad_branch = lax.all_gather(
            grad_middle.astype(jnp.bfloat16), "tp", axis=2, tiled=True
        ).reshape(tokens, model_width)
        grad_proj = grad_proj + lax.dot_general(
            attn_low, grad_branch, over_rows, preferred_element_type=jnp.float32
        )
        grad_attn = lax.dot_general(
            grad_branch, full_proj, over_cols, preferred_element_type=jnp.float32
        ).astype(jnp.bfloat16)
        grad_attn = grad_attn.reshape(images, band_len, local_heads, head_dim)
        delta_rows = jnp.sum(grad_attn.astype(jnp.float32) * attn_exact, axis=-1)
        delta_swap = jnp.transpose(delta_rows, (0, 2, 1))
        query_zero = jnp.zeros((images, local_heads, band_len, head_dim), jnp.float32)
        rel_zero = jnp.zeros((images, local_heads, band_len, grid_side), jnp.float32)
        whole_zero = jnp.zeros((images, whole_seq, local_heads, head_dim), jnp.float32)
        back_init = (query_zero, rel_zero, rel_zero, whole_zero, whole_zero)
        back_key_piece = lax.all_gather(key_part, "ctx", axis=1, tiled=True)
        back_value_piece = lax.all_gather(value_part, "ctx", axis=1, tiled=True)
        back_piece_len = back_key_piece.shape[1]
        back_sub_len = math.gcd(back_piece_len, block_rows)

        def back_advance(block_idx, state):
            offset = block_idx * back_sub_len
            key_blk = lax.dynamic_slice_in_dim(back_key_piece, offset, back_sub_len, 1)
            value_blk = lax.dynamic_slice_in_dim(back_value_piece, offset, back_sub_len, 1)
            logits = scores_of(
                queries, key_blk, rows_swap, cols_swap, offset, score_scale, grid_side
            )
            probs = jnp.exp(logits - log_total[..., None])
            grad_probs = jnp.einsum(
                "brhc,bkhc->bhrk", grad_attn, value_blk, preferred_element_type=jnp.float32
            )
            grad_logits = (probs * (grad_probs - delta_swap[..., None])).astype(jnp.bfloat16)
            grad_query = state[0] + jnp.einsum(
                "bhrk,bkhc->bhrc", grad_logits, key_blk, preferred_element_type=jnp.float32
            )
            add_rows, add_cols = bias_back(
                grad_logits.astype(jnp.float32), offset, back_sub_len, grid_side
            )
            grad_key_blk = (
                jnp.einsum(
                    "bhrk,brhc->bkhc", grad_logits, queries, preferred_element_type=jnp.float32
                )
                * score_scale
            )
            grad_value_blk = jnp.einsum(
                "bhrk,brhc->bkhc",
                probs.astype(jnp.bfloat16),
                grad_attn,
                preferred_element_type=jnp.float32,
            )
            keys_acc = lax.dynamic_update_slice_in_dim(
                state[3],
                lax.dynamic_slice_in_dim(state[3], offset, back_sub_len, 1) + grad_key_blk,
                offset,
                1,
            )
            values_acc = lax.dynamic_update_slice_in_dim(
                state[4],
                lax.dynamic_slice_in_dim(state[4], offset, back_sub_len, 1) + grad_value_blk,
                offset,
                1,
            )
            return (grad_query, state[1] + add_rows, state[2] + add_cols, keys_acc, values_acc)

        folded = lax.fori_loop(0, back_piece_len // back_sub_len, back_advance, back_init)
        grad_keys, grad_values = (
            lax.psum_scatter(
                folded[3].astype(jnp.bfloat16), "ctx", scatter_dimension=1, tiled=True
            ).astype(jnp.float32),
            lax.psum_scatter(
                folded[4].astype(jnp.bfloat16), "ctx", scatter_dimension=1, tiled=True
            ).astype(jnp.float32),
        )
        grad_query = jnp.transpose(folded[0] * score_scale, (0, 2, 1, 3))
        grad_rel_rows = jnp.transpose(folded[1], (0, 2, 1, 3)).reshape(
            images, band_grid, grid_side, local_heads, grid_side
        )
        grad_rel_cols = jnp.transpose(folded[2], (0, 2, 1, 3)).reshape(
            images, band_grid, grid_side, local_heads, grid_side
        )
        query_grid = queries.astype(jnp.float32).reshape(
            images, band_grid, grid_side, local_heads, head_dim
        )
        rel_query = jnp.einsum(
            "byxhk,ykc->byxhc", grad_rel_rows, band_table, precision=highest
        ) + jnp.einsum("byxhk,xkc->byxhc", grad_rel_cols, cols_table, precision=highest)
        grad_query = grad_query + rel_query.reshape(images, band_len, local_heads, head_dim)
        band_rows_grad = jnp.einsum(
            "byxhk,byxhc->ykc", grad_rel_rows, query_grid, precision=highest
        )
        cols_grad = jnp.einsum("byxhk,byxhc->xkc", grad_rel_cols, query_grid, precision=highest)
        grad_rows_tab = grad_rows_tab + jnp.einsum(
            "ykt,ykc->tc", band_hot, band_rows_grad, precision=highest
        )
        grad_cols_tab = grad_cols_tab + jnp.einsum(
            "xkt,xkc->tc", cols_hot, cols_grad, precision=highest
        )
        grad_mixed = (
            jnp.stack((grad_query, grad_keys, grad_values), axis=2)
            .astype(jnp.bfloat16)
            .reshape(tokens, qkv_width)
        )
        grad_qkv = grad_qkv + lax.dot_general(
            first_act, grad_mixed, over_rows, preferred_element_type=jnp.float32
        )
        grad_first = lax.dot_general(
            grad_mixed, flat_qkv, over_cols, preferred_element_type=jnp.float32
        ).reshape(images, band_len, model_width)
        gain_one = gain_one + jnp.sum(grad_first * normed1, axis=(0, 1))
        shift_one = shift_one + jnp.sum(grad_first, axis=(0, 1))
        input_grads.append(
            grad_middle
            + lax.psum_scatter(
                norm_back(grad_first, normed1, inv_std1, norm1_gain).astype(jnp.bfloat16),
                "tp",
                scatter_dimension=2,
                tiled=True,
            ).astype(jnp.float32)
        )
    owned_grads = (
        lax.psum_scatter(
            grad_qkv.reshape(model_width, 3, local_heads * head_dim).astype(jnp.bfloat16),
            ("fsdp", "ctx"),
            scatter_dimension=0,
            tiled=True,
        ).astype(jnp.float32),
        lax.psum_scatter(
            grad_proj.astype(jnp.bfloat16), ("fsdp", "ctx"), scatter_dimension=1, tiled=True
        ).astype(jnp.float32),
        lax.psum_scatter(
            grad_up.astype(jnp.bfloat16), ("fsdp", "ctx"), scatter_dimension=0, tiled=True
        ).astype(jnp.float32),
        lax.psum_scatter(
            grad_down.astype(jnp.bfloat16), ("fsdp", "ctx"), scatter_dimension=1, tiled=True
        ).astype(jnp.float32),
    )
    small_sums = lax.psum(
        (gain_one, shift_one, grad_rows_tab, grad_cols_tab, gain_two, shift_two),
        ("fsdp", "ctx", "tp"),
    )
    return (
        jnp.concatenate(outputs, axis=0),
        jnp.concatenate(input_grads, axis=0),
        small_sums[0],
        small_sums[1],
        owned_grads[0],
        small_sums[2],
        small_sums[3],
        owned_grads[1],
        small_sums[4],
        small_sums[5],
        owned_grads[2],
        owned_grads[3],
    )


f32 = jnp.float32
bf16 = jnp.bfloat16
LOG2E = 1.4426950408889634
NN = (((1,), (0,)), ((), ()))
NT = (((1,), (1,)), ((), ()))
TN = (((0,), (0,)), ((), ()))
VMEM_BYTES = 56 << 20


def mm(lhs, rhs, dims=NN):
    return lax.dot_general(lhs, rhs, dims, preferred_element_type=f32)


def pxor(value, axis, bit):
    size = lax.axis_size(axis)
    return lax.ppermute(value, axis, [(i, i ^ bit) for i in range(size)])


def gather_tp(share):
    from_x = pxor(share, "tp", 2)
    from_core = pxor(share, "tp", 1)
    return [share, from_core, from_x, pxor(from_x, "tp", 1)]


def swap_ctx(pieces):
    return [pieces[0]] + [pxor(pieces[s], "ctx", s) for s in range(1, len(pieces))]


def erf(x):
    x = jnp.clip(x, -3.7439211627767994, 3.7439211627767994)
    s = x * x
    top = jnp.full_like(s, 2.2905065861350646e-4)
    for coef in (3.4082910107109506e-3, 5.0955695062380861e-2, 0.18520832239976145, 1.128379143519084):
        top = top * s + coef
    low = jnp.full_like(s, -1.1791602954361697e-7)
    for coef in (
        2.3547966471313185e-5,
        1.0179625278914885e-3,
        1.4070470171167667e-2,
        1.1098505178285362e-1,
        4.9746925110067538e-1,
        1.0,
    ):
        low = low * s + coef
    return x * top / low


def assemble(place, pieces, full):
    count = len(pieces)
    for mine in range(count):

        @pl.when(place == mine)
        def _(mine=mine):
            full[...] = jnp.concatenate(
                [pieces[a ^ mine][...].astype(full.dtype) for a in range(count)], axis=1
            )


def split_out(place, value, keep_ref, send_ref):
    share = value.shape[1] // 4
    parts = [value[:, a * share : (a + 1) * share] for a in range(4)]
    even = jnp.concatenate([parts[0], parts[2]], axis=1).astype(bf16)
    odd = jnp.concatenate([parts[1], parts[3]], axis=1).astype(bf16)
    is_even = lax.rem(place, 2) == 0

    @pl.when(is_even)
    def _():
        keep_ref[...] = even
        send_ref[...] = odd

    @pl.when(jnp.logical_not(is_even))
    def _():
        keep_ref[...] = odd
        send_ref[...] = even


def normed_of(values):
    center = values - jnp.mean(values, axis=-1, keepdims=True)
    inv_std = lax.rsqrt(jnp.mean(center * center, axis=-1, keepdims=True) + epsilon)
    return center * inv_std, inv_std


def sum8(value):
    return jnp.sum(value.reshape(value.shape[0] // 8, 8, value.shape[1]), axis=0)


def norm_back_block(upstream, normed, inv_std, gain):
    scaled = upstream * gain
    return (
        scaled
        - jnp.mean(scaled, axis=-1, keepdims=True)
        - normed * jnp.mean(scaled * normed, axis=-1, keepdims=True)
    ) * inv_std


def whole_spec(shape):
    return pl.BlockSpec(shape, lambda *_: (0,) * len(shape))


def rows_spec(block, width):
    return pl.BlockSpec((block, width), lambda i, *_: (i, 0))


def cols_spec(height, block):
    return pl.BlockSpec((height, block), lambda i, *_: (0, i))


def call(body, place, grid, in_specs, out_specs, out_shape, scratch, name, flops, args, aliases=None):
    return pl.pallas_call(
        body,
        grid_spec=pltpu.PrefetchScalarGridSpec(
            num_scalar_prefetch=1,
            grid=grid,
            in_specs=in_specs,
            out_specs=out_specs,
            scratch_shapes=scratch,
        ),
        out_shape=[jax.ShapeDtypeStruct(s, d) for s, d in out_shape],
        compiler_params=pltpu.CompilerParams(vmem_limit_bytes=VMEM_BYTES),
        cost_estimate=pl.CostEstimate(flops=int(flops), bytes_accessed=1 << 20, transcendentals=0),
        name=name,
    )(place, *args)


def qkv_kernel(place, *refs):
    pieces, (gain, shift, weight), (full, act), outs, mixed = (
        refs[:4],
        refs[4:7],
        refs[7:9],
        refs[9:13],
        refs[13],
    )
    assemble(place[0], pieces, full)
    normed, _ = normed_of(full[...].astype(f32))
    act[...] = (normed * gain[...] + shift[...]).astype(bf16)
    heads, rows, width = weight.shape
    product = mm(weight[...].reshape(heads * rows, width), act[...], NT)
    mixed[...] = product.astype(bf16).reshape(heads, rows, product.shape[1])
    for s in range(4):
        outs[s][...] = mixed[place[1] ^ s]


def qkv_call(place, pieces, gain, shift, weight):
    tokens, share = pieces[0].shape
    width = gain.shape[1]
    heads, rows, _ = weight.shape
    block = 256
    return call(
        qkv_kernel,
        place,
        (tokens // block,),
        [rows_spec(block, share)] * 4
        + [whole_spec(gain.shape), whole_spec(gain.shape), whole_spec(weight.shape)],
        [rows_spec(block, width)] * 2 + [cols_spec(rows, block)] * 4,
        [((tokens, width), bf16)] * 2 + [((rows, tokens), bf16)] * 4,
        [pltpu.VMEM((heads, rows, block), bf16)],
        "qkv",
        2 * tokens * width * heads * rows,
        (*pieces, gain, shift, weight),
    )


def proj_kernel(place, *refs):
    pieces, weight, keep, send, joined = refs[:4], refs[4], refs[5], refs[6], refs[7]
    for s in range(4):
        joined[place[1] ^ s] = pieces[s][...]
    heads, rows, width = weight.shape
    product = mm(
        joined[...].reshape(heads * rows, joined.shape[2]),
        weight[...].reshape(heads * rows, width),
        TN,
    )
    split_out(place[0], product, keep, send)


def proj_call(place, pieces, weight):
    rows, tokens = pieces[0].shape
    heads, _, width = weight.shape
    block = 512
    return call(
        proj_kernel,
        place,
        (tokens // block,),
        [cols_spec(rows, block)] * 4 + [whole_spec(weight.shape)],
        [rows_spec(block, width // 2)] * 2,
        [((tokens, width // 2), bf16)] * 2,
        [pltpu.VMEM((heads, rows, block), bf16)],
        "proj",
        2 * tokens * width * heads * rows,
        (*pieces, weight),
    )


def mlp_kernel(place, *refs):
    mids, cots = refs[:4], refs[4:8]
    gain, shift, w_up, w_down = refs[8:12]
    act2, cot, hidden, grad_pre, keep_f, send_f, keep_b, send_b, sums = refs[12:21]
    full = refs[21]
    assemble(place[0], mids, full)
    assemble(place[0], cots, cot)
    normed, inv_std = normed_of(full[...])
    act2[...] = (normed * gain[...] + shift[...]).astype(bf16)
    pre = mm(act2[...], w_up[...])
    cdf = 0.5 * (1.0 + erf(pre * 0.7071067811865476))
    hidden[...] = (pre * cdf).astype(bf16)
    slope = cdf + pre * (jnp.exp(-0.5 * pre * pre) * 0.3989422804014327)
    split_out(place[0], mm(hidden[...], w_down[...]), keep_f, send_f)
    grad_pre[...] = (mm(cot[...], w_down[...], NT) * slope).astype(bf16)
    upstream = mm(grad_pre[...], w_up[...], NT)

    @pl.when(pl.program_id(0) == 0)
    def _():
        sums[...] = jnp.zeros_like(sums)

    sums[0:8] += sum8(upstream * normed)
    sums[8:16] += sum8(upstream)
    split_out(place[0], norm_back_block(upstream, normed, inv_std, gain[...]), keep_b, send_b)


def mlp_call(place, mids, cots, gain, shift, w_up, w_down):
    tokens, share = mids[0].shape
    width, hid = w_up.shape
    block = 256
    half = width // 2
    return call(
        mlp_kernel,
        place,
        (tokens // block,),
        [rows_spec(block, share)] * 8
        + [whole_spec(gain.shape)] * 2
        + [whole_spec(w_up.shape), whole_spec(w_down.shape)],
        [rows_spec(block, width)] * 2
        + [rows_spec(block, hid)] * 2
        + [rows_spec(block, half)] * 4
        + [whole_spec((16, width))],
        [((tokens, width), bf16)] * 2
        + [((tokens, hid), bf16)] * 2
        + [((tokens, half), bf16)] * 4
        + [((16, width), f32)],
        [pltpu.VMEM((block, width), f32)],
        "mlp",
        8 * tokens * width * hid,
        (*mids, *cots, gain, shift, w_up, w_down),
    )


def gattn_kernel(place, *refs):
    pieces, weight, full, outs, mixed = refs[:4], refs[4], refs[5], refs[6:10], refs[10]
    assemble(place[0], pieces, full)
    heads, rows, width = weight.shape
    product = mm(weight[...].reshape(heads * rows, width), full[...], NT)
    mixed[...] = product.astype(bf16).reshape(heads, rows, product.shape[1])
    for s in range(4):
        outs[s][...] = mixed[place[1] ^ s]


def gattn_call(place, pieces, weight):
    tokens, share = pieces[0].shape
    heads, rows, width = weight.shape
    block = 256
    return call(
        gattn_kernel,
        place,
        (tokens // block,),
        [rows_spec(block, share)] * 4 + [whole_spec(weight.shape)],
        [rows_spec(block, width)] + [cols_spec(rows, block)] * 4,
        [((tokens, width), bf16)] + [((rows, tokens), bf16)] * 4,
        [pltpu.VMEM((heads, rows, block), bf16)],
        "gattn",
        2 * tokens * width * heads * rows,
        (*pieces, weight),
    )


def gin_kernel(place, *refs):
    pieces, full, gain, weight = refs[:4], refs[4], refs[5], refs[6]
    keep, send, sums, joined = refs[7:11]
    for s in range(4):
        joined[place[1] ^ s] = pieces[s][...]
    heads, rows, width = weight.shape
    upstream = mm(
        joined[...].reshape(heads * rows, joined.shape[2]),
        weight[...].reshape(heads * rows, width),
        TN,
    )
    normed, inv_std = normed_of(full[...].astype(f32))

    @pl.when(pl.program_id(0) == 0)
    def _():
        sums[...] = jnp.zeros_like(sums)

    sums[0:8] += sum8(upstream * normed)
    sums[8:16] += sum8(upstream)
    split_out(place[0], norm_back_block(upstream, normed, inv_std, gain[...]), keep, send)


def gin_call(place, pieces, full, gain, weight):
    rows, tokens = pieces[0].shape
    heads, _, width = weight.shape
    block = 256
    half = width // 2
    return call(
        gin_kernel,
        place,
        (tokens // block,),
        [cols_spec(rows, block)] * 4
        + [rows_spec(block, width), whole_spec(gain.shape), whole_spec(weight.shape)],
        [rows_spec(block, half)] * 2 + [whole_spec((16, width))],
        [((tokens, half), bf16)] * 2 + [((16, width), f32)],
        [pltpu.VMEM((heads, rows, block), bf16)],
        "gin",
        2 * tokens * width * heads * rows,
        (*pieces, full, gain, weight),
    )


def wgrad_kernel(images, place, *refs):
    joined = refs[-1]
    out = refs[-2]
    for m in range(images):
        for s in range(4):
            joined[m, place[1] ^ s] = refs[4 * m + s][...]
    heads, rows, tokens = joined.shape[1:]
    width = out.shape[0]
    step = 256

    def advance(n, carry):
        cols = pl.ds(pl.multiple_of(n * step, step), step)
        total = jnp.zeros((heads * rows, step), f32)
        for m in range(images):
            total += mm(joined[m].reshape(heads * rows, tokens), refs[4 * images + m][:, cols])
        out[cols, :] = jnp.transpose(total).astype(bf16)
        return carry

    lax.fori_loop(0, width // step, advance, 0)


def wgrad_call(place, pieces, rights, name):
    images = len(pieces)
    rows, tokens = pieces[0][0].shape
    width = rights[0].shape[1]
    (out,) = call(
        functools.partial(wgrad_kernel, images),
        place,
        (1,),
        [whole_spec((rows, tokens))] * (4 * images) + [whole_spec((tokens, width))] * images,
        [whole_spec((width, 4 * rows))],
        [((width, 4 * rows), bf16)],
        [pltpu.VMEM((images, 4, rows, tokens), bf16)],
        name,
        2 * images * tokens * width * 4 * rows,
        (*[p for group in pieces for p in group], *rights),
    )
    return out


def band_start(place, chunk, size, band):
    return (place[1] ^ lax.div(chunk * size, band)) * band + lax.rem(chunk * size, band)


def fwd_kernel(dims, place, *refs):
    hd, side, scale = dims
    pieces, table = refs[:4], refs[4]
    outs, kvq, exact, lse, qa = refs[5:9], refs[9], refs[10], refs[11], refs[12]
    ka, va, low = refs[13:16]
    band = pieces[0].shape[1]
    seq = kvq.shape[1]
    step = 512
    bq, bk = band, 1024
    for s in range(4):
        kvq[:, s * band : (s + 1) * band] = pieces[s][...]
    lane = lax.broadcasted_iota(jnp.int32, (step, 128), 1)
    row = lax.broadcasted_iota(jnp.int32, (step, 128), 0)
    lane_side = lax.broadcasted_iota(jnp.int32, (side, 128), 1)
    row16 = lax.broadcasted_iota(jnp.int32, (16, step), 0)
    pad = jnp.zeros((128 - hd, step), bf16)

    def prepare(c, carry):
        at = pl.ds(pl.multiple_of(c * step, step), step)
        start = band_start(place, c, step, band)
        keys = jnp.transpose(jnp.concatenate([kvq[0:hd, at], pad], axis=0).astype(f32))
        ka[at, 0:128] = keys.astype(bf16)
        pos = row + start
        want = jnp.where(lane < side, lax.div(pos, side), lax.rem(pos, side) + side)
        ka[at, 128:256] = jnp.where(want == lane, 1.0, 0.0).astype(bf16)
        va[0:hd, at] = kvq[hd : 2 * hd, at]
        va[hd : hd + 16, at] = jnp.where(row16 == 0, 1.0, 0.0).astype(bf16)
        queries = jnp.concatenate([kvq[2 * hd : 3 * hd, at], pad], axis=0)
        qa[0:128, at] = (queries.astype(f32) * (scale * LOG2E)).astype(bf16)
        terms = lax.dot_general(queries, table[...], (((0,), (1,)), ((), ())), preferred_element_type=f32)
        parts = []
        for r in range(step // side):
            y = lax.div(start, side) + r
            by_row = terms[r * side : (r + 1) * side, 0:128]
            by_col = terms[r * side : (r + 1) * side, 128:256]
            by_row = pltpu.roll(by_row, lax.rem(side + 1 + y, 128), 1)
            by_col = pltpu.roll(by_col, 1, 1, stride=1, stride_axis=0)
            parts.append(jnp.where(lane_side < side, by_row, by_col))
        rel = jnp.concatenate(parts, axis=0) * LOG2E
        qa[128:256, at] = jnp.transpose(rel).astype(bf16)
        return carry

    lax.fori_loop(0, seq // step, prepare, 0)

    def queries_loop(i, carry):
        at = pl.ds(pl.multiple_of(i * bq, bq), bq)
        q_block = qa[:, at]

        def keys_loop(j, state):
            peak, total = state
            keys = pl.ds(pl.multiple_of(j * bk, bk), bk)
            logits = mm(ka[keys, :], q_block)
            new_peak = jnp.maximum(peak, jnp.max(logits, axis=0, keepdims=True))
            weights = jnp.exp2(logits - new_peak).astype(bf16)
            total = total * jnp.exp2(peak - new_peak) + mm(va[:, keys], weights)
            return new_peak, total

        peak, total = lax.fori_loop(
            0,
            seq // bk,
            keys_loop,
            (jnp.full((1, bq), lowest, f32), jnp.zeros((hd + 16, bq), f32)),
        )
        denom = total[hd : hd + 1]
        value = total[0:hd] / denom
        exact[:, at] = value
        low[:, at] = value.astype(bf16)
        lse[:, at] = jnp.broadcast_to(peak + jnp.log2(denom), (8, bq))
        return carry

    lax.fori_loop(0, seq // bq, queries_loop, 0)
    for s in range(4):
        outs[s][...] = low[:, s * band : (s + 1) * band]


def fwd_call(place, pieces, table, hd, side):
    rows, band = pieces[0].shape
    seq = 4 * band
    return call(
        functools.partial(fwd_kernel, (hd, side, hd ** (-0.5))),
        place,
        (1,),
        [whole_spec((rows, band))] * 4 + [whole_spec(table.shape)],
        [whole_spec((hd, band))] * 4
        + [whole_spec((rows, seq)), whole_spec((hd, seq)), whole_spec((8, seq)), whole_spec((256, seq))],
        [((hd, band), bf16)] * 4
        + [((rows, seq), bf16), ((hd, seq), f32), ((8, seq), f32), ((256, seq), bf16)],
        [
            pltpu.VMEM((seq, 256), bf16),
            pltpu.VMEM((hd + 16, seq), bf16),
            pltpu.VMEM((hd, seq), bf16),
        ],
        "attn_fwd",
        40e9,
        (*pieces, table),
    )


def split3(value):
    high = value.astype(bf16).astype(f32)
    rest = value - high
    mid = rest.astype(bf16).astype(f32)
    return high, mid, rest - mid


def bwd_kernel(dims, place, *refs):
    hd, side, scale = dims
    grads, kvq, qa_in, exact, lse, table = refs[:4], refs[4], refs[5], refs[6], refs[7], refs[8]
    outs, dtab = refs[9:13], refs[13]
    ka, kt, va, qa, da, qn, dn, dk, dv, res = refs[14:24]
    band = grads[0].shape[1]
    seq = kvq.shape[1]
    step = 512
    bq, bk = band, 1024
    for s in range(4):
        da[0:hd, s * band : (s + 1) * band] = grads[s][...]
    lane = lax.broadcasted_iota(jnp.int32, (step, 128), 1)
    row = lax.broadcasted_iota(jnp.int32, (step, 128), 0)
    lane_side = lax.broadcasted_iota(jnp.int32, (side, 128), 1)
    extra = lax.broadcasted_iota(jnp.int32, (128 - hd, step), 0)
    pad = jnp.zeros((128 - hd, step), bf16)
    ones = (lane >= hd) & (lane < hd + 3)

    def turned(value):
        return jnp.transpose(jnp.concatenate([value, pad], axis=0).astype(f32))

    def special(value):
        high, mid, rest = split3(value)
        picked = jnp.where(extra == 0, high, jnp.where(extra == 1, mid, jnp.where(extra == 2, rest, 0.0)))
        return picked.astype(bf16)

    def prepare(c, carry):
        at = pl.ds(pl.multiple_of(c * step, step), step)
        start = band_start(place, c, step, band)
        k_part = kvq[0:hd, at]
        q_part = kvq[2 * hd : 3 * hd, at]
        kt[0:128, at] = jnp.concatenate([k_part, pad], axis=0)
        ka[at, 0:128] = jnp.where(ones, 1.0, turned(k_part)).astype(bf16)
        pos = row + start
        want = jnp.where(lane < side, lax.div(pos, side), lax.rem(pos, side) + side)
        ka[at, 128:256] = jnp.where(want == lane, 1.0, 0.0).astype(bf16)
        want = jnp.where(lane < side, lax.div(pos, side), 2 * side - 1 - lax.rem(pos, side))
        kt[128:256, at] = jnp.transpose(jnp.where(want == lane, 1.0, 0.0)).astype(bf16)
        va[at, :] = jnp.where(ones, 1.0, turned(kvq[hd : 2 * hd, at])).astype(bf16)
        dk[at, :] = jnp.zeros((step, 128), f32)
        dv[at, :] = jnp.zeros((step, 128), f32)
        d_part = da[0:hd, at]
        qn[at, :] = turned(q_part).astype(bf16)
        dn[at, :] = turned(d_part).astype(bf16)
        delta = jnp.sum(d_part.astype(f32) * exact[:, at], axis=0, keepdims=True)
        qa[0:hd, at] = qa_in[0:hd, at]
        qa[hd:128, at] = special(-lse[0:1, at])
        qa[128:256, at] = qa_in[128:256, at]
        da[hd:128, at] = special(-delta)
        return carry

    lax.fori_loop(0, seq // step, prepare, 0)
    dtab[...] = jnp.zeros_like(dtab)

    def queries_loop(i, carry):
        at = pl.ds(pl.multiple_of(i * bq, bq), bq)
        qa_i, da_i, qn_i, dn_i = qa[:, at], da[:, at], qn[at, :], dn[at, :]

        def keys_loop(j, total):
            keys = pl.ds(pl.multiple_of(j * bk, bk), bk)
            probs = jnp.exp2(mm(ka[keys, :], qa_i))
            grad_logits = (probs * mm(va[keys, :], da_i)).astype(bf16)
            dv[keys, :] += mm(probs.astype(bf16), dn_i)
            dk[keys, :] += mm(grad_logits, qn_i)
            return total + mm(kt[:, keys], grad_logits)

        total = lax.fori_loop(0, seq // bk, keys_loop, jnp.zeros((256, bq), f32))
        rel = jnp.transpose(total[128:256])
        start = band_start(place, i, bq, band)
        parts = []
        for r in range(bq // side):
            y = lax.div(start, side) + r
            block = rel[r * side : (r + 1) * side]
            by_row = jnp.where(lane_side < side, block, 0.0)
            by_col = jnp.where(lane_side < side, 0.0, block)
            by_row = pltpu.roll(by_row, lax.rem(side + 127 - y, 128), 1)
            by_col = pltpu.roll(by_col, side + 1, 1, stride=1, stride_axis=0)
            parts.append(jnp.concatenate([by_row, by_col], axis=1))
        moved = jnp.concatenate(parts, axis=0).astype(bf16)
        dq = total[0:128] * scale + lax.dot_general(
            table[...], moved, (((0,), (1,)), ((), ())), preferred_element_type=f32
        )
        res[2 * hd : 3 * hd, at] = dq[0:hd].astype(bf16)
        dtab[...] += mm(moved, qn_i, TN)
        return carry

    lax.fori_loop(0, seq // bq, queries_loop, 0)

    def finish(c, carry):
        at = pl.ds(pl.multiple_of(c * step, step), step)
        res[0:hd, at] = jnp.transpose(dk[at, :] * scale)[0:hd].astype(bf16)
        res[hd : 2 * hd, at] = jnp.transpose(dv[at, :])[0:hd].astype(bf16)
        return carry

    lax.fori_loop(0, seq // step, finish, 0)
    for s in range(4):
        outs[s][...] = res[:, s * band : (s + 1) * band]


def bwd_call(place, grads, kvq, qa, exact, lse, table, hd, side):
    rows, seq = kvq.shape
    band = seq // 4
    return call(
        functools.partial(bwd_kernel, (hd, side, hd ** (-0.5))),
        place,
        (1,),
        [whole_spec((hd, band))] * 4
        + [whole_spec(a.shape) for a in (kvq, qa, exact, lse, table)],
        [whole_spec((rows, band))] * 4 + [whole_spec((256, 128))],
        [((rows, band), bf16)] * 4 + [((256, 128), f32)],
        [
            pltpu.VMEM((seq, 256), bf16),
            pltpu.VMEM((256, seq), bf16),
            pltpu.VMEM((seq, 128), bf16),
            pltpu.VMEM((256, seq), bf16),
            pltpu.VMEM((128, seq), bf16),
            pltpu.VMEM((seq, 128), bf16),
            pltpu.VMEM((seq, 128), bf16),
            pltpu.VMEM((seq, 128), f32),
            pltpu.VMEM((seq, 128), f32),
            pltpu.VMEM((rows, seq), bf16),
        ],
        "attn_bwd",
        72e9,
        (*grads, kvq, qa, exact, lse, table),
    )


def offset_rows(index, table):
    side = index.shape[0]
    picks = jnp.concatenate([index[::-1, 0], index[0, 1:]])
    hot = (picks[:, None] == jnp.arange(table.shape[0], dtype=jnp.int32)[None, :]).astype(f32)
    rows = jnp.dot(hot, table.astype(f32), precision=highest)
    return hot, jnp.pad(rows, ((0, 1), (0, 128 - table.shape[1]))).astype(bf16)


def fast_device(
    block_input,
    cotangent,
    norm1_gain,
    norm1_shift,
    w_qkv,
    table_rows,
    table_cols,
    w_proj,
    norm2_gain,
    norm2_shift,
    w_fc1,
    w_fc2,
    index_rows,
    index_cols,
):
    images, band_len, share = block_input.shape
    side = index_rows.shape[0]
    hd = table_rows.shape[1]
    width = norm1_gain.shape[0]
    heads = w_proj.shape[0] // hd
    t = lax.axis_index("tp")
    z = lax.axis_index("ctx")
    on_x = lax.div(t, 2) == 0
    place = jnp.stack([t, z]).astype(jnp.int32)
    gain1, shift1 = norm1_gain[None, :], norm1_shift[None, :]
    gain2, shift2 = norm2_gain[None, :], norm2_shift[None, :]

    packed = w_qkv.reshape(w_qkv.shape[0], 3, heads, hd)
    packed = jnp.concatenate([packed[:, 1:], packed[:, :1]], axis=1)
    packed = jnp.transpose(packed, (2, 1, 3, 0)).reshape(heads * 3 * hd, w_qkv.shape[0])
    full_qkv = lax.all_gather(packed, "fsdp", axis=1, tiled=True).reshape(heads, 3 * hd, width)
    full_proj = lax.all_gather(w_proj, "fsdp", axis=1, tiled=True).reshape(heads, hd, width)
    full_up = lax.all_gather(w_fc1, "fsdp", axis=0, tiled=True)
    full_down = lax.all_gather(w_fc2, "fsdp", axis=1, tiled=True)

    hot_rows, shifted_rows = offset_rows(index_rows, table_rows)
    hot_cols, shifted_cols = offset_rows(index_cols, table_cols)
    table = jnp.concatenate([shifted_rows, shifted_cols], axis=0)
    back_table = jnp.concatenate(
        [shifted_rows, jnp.zeros((1, 128), bf16), shifted_cols[:127][::-1]], axis=0
    )

    def reduce_tp(keep, send):
        got = keep.astype(f32) + pxor(send, "tp", 1).astype(f32)
        mine = jnp.where(on_x, got[:, :share], got[:, share:])
        other = jnp.where(on_x, got[:, share:], got[:, :share]).astype(bf16)
        return mine + pxor(other, "tp", 2).astype(f32)

    outputs, input_grads = [], []
    sums1, sums2, tabs = [], [], []
    w_qkv_parts, w_proj_parts, up_parts, down_parts = [], [], [], []
    for m in range(images):
        input_part = block_input[m]
        grad_part = cotangent[m]
        full_in, act1, *mixed = qkv_call(place, gather_tp(input_part), gain1, shift1, full_qkv)
        *attn, kvq, exact, lse, qa = fwd_call(place, swap_ctx(mixed), table, hd, side)
        attn = swap_ctx(attn)
        middle = input_part.astype(f32) + reduce_tp(*proj_call(place, attn, full_proj))
        mids = gather_tp(middle.astype(bf16))
        cots = gather_tp(grad_part)
        act2, cot, hidden, grad_pre, keep_f, send_f, keep_b, send_b, sums = mlp_call(
            place, mids, cots, gain2, shift2, full_up, full_down
        )
        outputs.append((middle + reduce_tp(keep_f, send_f)).astype(bf16))
        sums2.append(sums)
        grad_middle = grad_part.astype(f32) + reduce_tp(keep_b, send_b)
        branch, *grads = gattn_call(place, gather_tp(grad_middle.astype(bf16)), full_proj)
        *mixed_grads, dtab = bwd_call(
            place, swap_ctx(grads), kvq, qa, exact, lse, back_table, hd, side
        )
        tabs.append(dtab)
        mixed_grads = swap_ctx(mixed_grads)
        keep, send, sums = gin_call(place, mixed_grads, full_in, gain1, full_qkv)
        sums1.append(sums)
        input_grads.append(grad_middle + reduce_tp(keep, send))
        w_qkv_parts.append((mixed_grads, act1))
        w_proj_parts.append((attn, branch))
        up_parts.append(mm(act2, grad_pre, TN))
        down_parts.append(mm(cot, hidden, TN))

    def scatter(value):
        return lax.psum_scatter(value, ("fsdp", "ctx"), scatter_dimension=0, tiled=True).astype(f32)

    grad_up = scatter(sum(up_parts).astype(bf16))
    grad_down = scatter(sum(down_parts).astype(bf16)).T
    grad_proj = scatter(
        wgrad_call(place, [p for p, _ in w_proj_parts], [r for _, r in w_proj_parts], "wproj")
    ).T
    grad_qkv = scatter(
        wgrad_call(place, [p for p, _ in w_qkv_parts], [r for _, r in w_qkv_parts], "wqkv")
    ).reshape(-1, heads, 3, hd)
    grad_qkv = jnp.concatenate([grad_qkv[:, :, 2:], grad_qkv[:, :, :2]], axis=2)
    grad_qkv = jnp.transpose(grad_qkv, (0, 2, 1, 3)).reshape(-1, 3, heads * hd)

    def pair(parts):
        return jnp.sum(sum(parts).reshape(2, 8, width), axis=1)

    small = jnp.concatenate(
        [jnp.concatenate([pair(sums1), pair(sums2)], axis=0).reshape(-1, 128), sum(tabs)], axis=0
    )
    for axis in ("tp", "fsdp", "ctx"):
        bit = 1
        while bit < lax.axis_size(axis):
            small = small + pxor(small, axis, bit)
            bit *= 2
    norms = small[: 4 * width // 128].reshape(4, width)
    tabs = small[4 * width // 128 :]
    rows_grad = jnp.dot(hot_rows.T, tabs[:127, :hd], precision=highest)
    cols_grad = jnp.dot(hot_cols.T, tabs[129:256, :hd][::-1], precision=highest)
    return (
        jnp.stack(outputs),
        jnp.stack(input_grads),
        norms[0],
        norms[1],
        grad_qkv,
        rows_grad,
        cols_grad,
        grad_proj,
        norms[2],
        norms[3],
        grad_up,
        grad_down,
    )


def per_device(*args):
    block_input, w_proj, table_rows, index_rows = args[0], args[7], args[5], args[12]
    heads = w_proj.shape[0] // table_rows.shape[1]
    fits = (
        lax.axis_size("tp") == 4
        and lax.axis_size("ctx") == 4
        and heads == 4
        and index_rows.shape[0] == 64
        and table_rows.shape[1] == 80
        and block_input.shape[1] % 512 == 0
    )
    return fast_device(*args) if fits else plain_device(*args)


def solution(mesh):
    in_specs = (
        P("fsdp", "ctx", "tp"),
        P("fsdp", "ctx", "tp"),
        P(),
        P(),
        P("fsdp", None, "tp"),
        P(),
        P(),
        P("tp", "fsdp"),
        P(),
        P(),
        P("fsdp", "tp"),
        P("tp", "fsdp"),
        P(),
        P(),
    )
    out_specs = (
        P("fsdp", "ctx", "tp"),
        P("fsdp", "ctx", "tp"),
        P(),
        P(),
        P(("fsdp", "ctx"), None, "tp"),
        P(),
        P(),
        P("tp", ("fsdp", "ctx")),
        P(),
        P(),
        P(("fsdp", "ctx"), "tp"),
        P("tp", ("fsdp", "ctx")),
    )
    return jax.shard_map(
        per_device, mesh=mesh, in_specs=in_specs, out_specs=out_specs, check_vma=False
    )
```

```python
import functools
import math

import jax
import jax.numpy as jnp
from jax import lax
from jax.experimental import pallas as pl
from jax.experimental.pallas import tpu as pltpu
from jax.sharding import PartitionSpec as P

MICRO = 2


epsilon = 1e-06
highest = lax.Precision.HIGHEST
block_rows = 512
lowest = -1e30


def layer_norm(values, gain_vec, shift_vec):
    center = values - jnp.mean(values, axis=-1, keepdims=True)
    inv_std = lax.rsqrt(jnp.mean(center * center, axis=-1, keepdims=True) + epsilon)
    normed = center * inv_std
    return (normed * gain_vec + shift_vec, normed, inv_std)


def norm_back(upstream, normed, inv_std, gain_vec):
    scaled = upstream * gain_vec
    inner = (
        scaled
        - jnp.mean(scaled, axis=-1, keepdims=True)
        - normed * jnp.mean(scaled * normed, axis=-1, keepdims=True)
    )
    return inner * inv_std


def gelu_pair(values):
    normal_cdf = 0.5 * (1.0 + lax.erf(values * 0.7071067811865476))
    normal_pdf = jnp.exp(-0.5 * values * values) * 0.3989422804014327
    return (values * normal_cdf, normal_cdf + values * normal_pdf)


def rel_terms(queries, band_table, cols_table, grid_side):
    shape_in = queries.shape
    shaped = queries.astype(jnp.float32).reshape(
        shape_in[0], shape_in[1] // grid_side, grid_side, shape_in[2], shape_in[3]
    )
    rows_term = jnp.einsum("byxhc,ykc->byxhk", shaped, band_table, precision=highest)
    cols_term = jnp.einsum("byxhc,xkc->byxhk", shaped, cols_table, precision=highest)
    return (
        rows_term.reshape(shape_in[:3] + (grid_side,)),
        cols_term.reshape(shape_in[:3] + (grid_side,)),
    )


def key_bias(rows_term, cols_term, first_key, key_count, grid_side):
    picked = lax.dynamic_slice_in_dim(rows_term, first_key // grid_side, key_count // grid_side, 3)
    joined = picked[..., :, None] + cols_term[..., None, :]
    return joined.reshape(picked.shape[:3] + (key_count,))


def bias_back(grad_logits, first_key, key_count, grid_side):
    split = grad_logits.reshape(grad_logits.shape[:3] + (key_count // grid_side, grid_side))
    empty = jnp.zeros(grad_logits.shape[:3] + (grid_side,), jnp.float32)
    rows_part = lax.dynamic_update_slice_in_dim(
        empty, jnp.sum(split, axis=4), first_key // grid_side, 3
    )
    return (rows_part, jnp.sum(split, axis=3))


def scores_of(queries, key_blk, rows_term, cols_term, first_key, score_scale, grid_side):
    raw_dots = jnp.einsum("brhc,bkhc->bhrk", queries, key_blk, preferred_element_type=jnp.float32)
    return raw_dots * score_scale + key_bias(
        rows_term, cols_term, first_key, key_blk.shape[1], grid_side
    )


def plain_device(
    block_input,
    cotangent,
    norm1_gain,
    norm1_shift,
    w_qkv,
    table_rows,
    table_cols,
    w_proj,
    norm2_gain,
    norm2_shift,
    w_fc1,
    w_fc2,
    index_rows,
    index_cols,
):
    grid_side = index_rows.shape[0]
    table_len = table_rows.shape[0]
    head_dim = table_rows.shape[1]
    model_width = norm1_gain.shape[0]
    band_len = block_input.shape[1]
    band_grid = band_len // grid_side
    local_heads = w_proj.shape[0] // head_dim
    hidden_local = w_fc1.shape[1]
    per_micro = block_input.shape[0] // MICRO
    score_scale = head_dim ** (-0.5)
    ctx_place = lax.axis_index("ctx")
    whole_seq = band_len * lax.axis_size("ctx")
    levels = jnp.arange(table_len, dtype=jnp.int32)
    hot_rows = (index_rows.reshape(-1)[:, None] == levels[None, :]).astype(jnp.float32)
    hot_cols = (index_cols.reshape(-1)[:, None] == levels[None, :]).astype(jnp.float32)
    rows_table = jnp.dot(hot_rows, table_rows.astype(jnp.float32), precision=highest).reshape(
        grid_side, grid_side, head_dim
    )
    cols_table = jnp.dot(hot_cols, table_cols.astype(jnp.float32), precision=highest).reshape(
        grid_side, grid_side, head_dim
    )
    band_table = lax.dynamic_slice_in_dim(rows_table, ctx_place * band_grid, band_grid, 0)
    band_hot = lax.dynamic_slice_in_dim(
        hot_rows.reshape(grid_side, grid_side, table_len), ctx_place * band_grid, band_grid, 0
    )
    cols_hot = hot_cols.reshape(grid_side, grid_side, table_len)
    over_rows = (((0,), (0,)), ((), ()))
    over_cols = (((1,), (1,)), ((), ()))
    qkv_width = 3 * local_heads * head_dim
    grad_qkv = jnp.zeros((model_width, qkv_width), jnp.float32)
    grad_proj = jnp.zeros((local_heads * head_dim, model_width), jnp.float32)
    grad_up = jnp.zeros((model_width, hidden_local), jnp.float32)
    grad_down = jnp.zeros((hidden_local, model_width), jnp.float32)
    gain_one = jnp.zeros((model_width,), jnp.float32)
    shift_one = jnp.zeros((model_width,), jnp.float32)
    gain_two = jnp.zeros((model_width,), jnp.float32)
    shift_two = jnp.zeros((model_width,), jnp.float32)
    grad_rows_tab = jnp.zeros((table_len, head_dim), jnp.float32)
    grad_cols_tab = jnp.zeros((table_len, head_dim), jnp.float32)
    outputs = []
    input_grads = []
    for micro_step in range(MICRO):
        input_part = block_input[micro_step * per_micro : (micro_step + 1) * per_micro]
        grad_part = cotangent[micro_step * per_micro : (micro_step + 1) * per_micro]
        images = input_part.shape[0]
        tokens = images * band_len
        full_qkv, full_proj, full_up, full_down = (
            lax.all_gather(w_qkv, "fsdp", axis=0, tiled=True),
            lax.all_gather(w_proj, "fsdp", axis=1, tiled=True),
            lax.all_gather(w_fc1, "fsdp", axis=0, tiled=True),
            lax.all_gather(w_fc2, "fsdp", axis=1, tiled=True),
        )
        flat_qkv = full_qkv.reshape(model_width, qkv_width)
        input_full, grad_out_full = (
            lax.all_gather(input_part, "tp", axis=2, tiled=True),
            lax.all_gather(grad_part, "tp", axis=2, tiled=True),
        )
        normed_in, normed1, inv_std1 = layer_norm(
            input_full.astype(jnp.float32), norm1_gain, norm1_shift
        )
        first_act = normed_in.astype(jnp.bfloat16).reshape(tokens, model_width)
        mixed_qkv = jnp.dot(first_act, flat_qkv, preferred_element_type=jnp.float32).astype(
            jnp.bfloat16
        )
        mixed_qkv = mixed_qkv.reshape(images, band_len, 3, local_heads, head_dim)
        queries = mixed_qkv[:, :, 0]
        key_part = mixed_qkv[:, :, 1]
        value_part = mixed_qkv[:, :, 2]
        rows_term, cols_term = rel_terms(queries, band_table, cols_table, grid_side)
        rows_swap = jnp.transpose(rows_term, (0, 2, 1, 3))
        cols_swap = jnp.transpose(cols_term, (0, 2, 1, 3))
        fold_init = (
            jnp.full((images, local_heads, band_len), lowest, jnp.float32),
            jnp.zeros((images, local_heads, band_len), jnp.float32),
            jnp.zeros((images, local_heads, band_len, head_dim), jnp.float32),
        )
        key_piece = lax.all_gather(key_part, "ctx", axis=1, tiled=True)
        value_piece = lax.all_gather(value_part, "ctx", axis=1, tiled=True)
        piece_len = key_piece.shape[1]
        sub_len = math.gcd(piece_len, block_rows)

        def forward_advance(block_idx, state):
            running, denom_sum, acc_out = state
            offset = block_idx * sub_len
            key_blk = lax.dynamic_slice_in_dim(key_piece, offset, sub_len, 1)
            value_blk = lax.dynamic_slice_in_dim(value_piece, offset, sub_len, 1)
            logits = scores_of(
                queries, key_blk, rows_swap, cols_swap, offset, score_scale, grid_side
            )
            new_peak = jnp.maximum(running, jnp.max(logits, axis=-1))
            rescale = jnp.exp(running - new_peak)
            weights = jnp.exp(logits - new_peak[..., None])
            denom_sum = denom_sum * rescale + jnp.sum(weights, axis=-1)
            acc_out = acc_out * rescale[..., None] + jnp.einsum(
                "bhrk,bkhc->bhrc",
                weights.astype(jnp.bfloat16),
                value_blk,
                preferred_element_type=jnp.float32,
            )
            return (new_peak, denom_sum, acc_out)

        peak_all, denom_all, acc_all = lax.fori_loop(
            0, piece_len // sub_len, forward_advance, fold_init
        )
        attn_exact = jnp.transpose(acc_all / denom_all[..., None], (0, 2, 1, 3))
        log_total = peak_all + jnp.log(denom_all)
        attn_low = attn_exact.astype(jnp.bfloat16).reshape(tokens, local_heads * head_dim)
        attn_branch = jnp.dot(attn_low, full_proj, preferred_element_type=jnp.float32).reshape(
            images, band_len, model_width
        )
        attn_share = lax.psum_scatter(
            attn_branch.astype(jnp.bfloat16), "tp", scatter_dimension=2, tiled=True
        ).astype(jnp.float32)
        middle_share = input_part.astype(jnp.float32) + attn_share
        middle_full = lax.all_gather(
            middle_share.astype(jnp.bfloat16), "tp", axis=2, tiled=True
        ).astype(middle_share.dtype)
        normed_mid, normed2, inv_std2 = layer_norm(middle_full, norm2_gain, norm2_shift)
        second_act = normed_mid.astype(jnp.bfloat16).reshape(tokens, model_width)
        pre_act = jnp.dot(second_act, full_up, preferred_element_type=jnp.float32)
        gelu_out, gelu_slope = gelu_pair(pre_act)
        hidden_low = gelu_out.astype(jnp.bfloat16)
        mlp_branch = jnp.dot(hidden_low, full_down, preferred_element_type=jnp.float32).reshape(
            images, band_len, model_width
        )
        mlp_share = lax.psum_scatter(
            mlp_branch.astype(jnp.bfloat16), "tp", scatter_dimension=2, tiled=True
        ).astype(jnp.float32)
        outputs.append((middle_share + mlp_share).astype(jnp.bfloat16))
        grad_out_flat = grad_out_full.reshape(tokens, model_width)
        grad_down = grad_down + lax.dot_general(
            hidden_low, grad_out_flat, over_rows, preferred_element_type=jnp.float32
        )
        grad_hidden = lax.dot_general(
            grad_out_flat, full_down, over_cols, preferred_element_type=jnp.float32
        )
        grad_pre = (grad_hidden * gelu_slope).astype(jnp.bfloat16)
        grad_up = grad_up + lax.dot_general(
            second_act, grad_pre, over_rows, preferred_element_type=jnp.float32
        )
        grad_second = lax.dot_general(
            grad_pre, full_up, over_cols, preferred_element_type=jnp.float32
        ).reshape(images, band_len, model_width)
        gain_two = gain_two + jnp.sum(grad_second * normed2, axis=(0, 1))
        shift_two = shift_two + jnp.sum(grad_second, axis=(0, 1))
        grad_middle = grad_part.astype(jnp.float32) + lax.psum_scatter(
            norm_back(grad_second, normed2, inv_std2, norm2_gain).astype(jnp.bfloat16),
            "tp",
            scatter_dimension=2,
            tiled=True,
        ).astype(jnp.float32)
        grad_branch = lax.all_gather(
            grad_middle.astype(jnp.bfloat16), "tp", axis=2, tiled=True
        ).reshape(tokens, model_width)
        grad_proj = grad_proj + lax.dot_general(
            attn_low, grad_branch, over_rows, preferred_element_type=jnp.float32
        )
        grad_attn = lax.dot_general(
            grad_branch, full_proj, over_cols, preferred_element_type=jnp.float32
        ).astype(jnp.bfloat16)
        grad_attn = grad_attn.reshape(images, band_len, local_heads, head_dim)
        delta_rows = jnp.sum(grad_attn.astype(jnp.float32) * attn_exact, axis=-1)
        delta_swap = jnp.transpose(delta_rows, (0, 2, 1))
        query_zero = jnp.zeros((images, local_heads, band_len, head_dim), jnp.float32)
        rel_zero = jnp.zeros((images, local_heads, band_len, grid_side), jnp.float32)
        whole_zero = jnp.zeros((images, whole_seq, local_heads, head_dim), jnp.float32)
        back_init = (query_zero, rel_zero, rel_zero, whole_zero, whole_zero)
        back_key_piece = lax.all_gather(key_part, "ctx", axis=1, tiled=True)
        back_value_piece = lax.all_gather(value_part, "ctx", axis=1, tiled=True)
        back_piece_len = back_key_piece.shape[1]
        back_sub_len = math.gcd(back_piece_len, block_rows)

        def back_advance(block_idx, state):
            offset = block_idx * back_sub_len
            key_blk = lax.dynamic_slice_in_dim(back_key_piece, offset, back_sub_len, 1)
            value_blk = lax.dynamic_slice_in_dim(back_value_piece, offset, back_sub_len, 1)
            logits = scores_of(
                queries, key_blk, rows_swap, cols_swap, offset, score_scale, grid_side
            )
            probs = jnp.exp(logits - log_total[..., None])
            grad_probs = jnp.einsum(
                "brhc,bkhc->bhrk", grad_attn, value_blk, preferred_element_type=jnp.float32
            )
            grad_logits = (probs * (grad_probs - delta_swap[..., None])).astype(jnp.bfloat16)
            grad_query = state[0] + jnp.einsum(
                "bhrk,bkhc->bhrc", grad_logits, key_blk, preferred_element_type=jnp.float32
            )
            add_rows, add_cols = bias_back(
                grad_logits.astype(jnp.float32), offset, back_sub_len, grid_side
            )
            grad_key_blk = (
                jnp.einsum(
                    "bhrk,brhc->bkhc", grad_logits, queries, preferred_element_type=jnp.float32
                )
                * score_scale
            )
            grad_value_blk = jnp.einsum(
                "bhrk,brhc->bkhc",
                probs.astype(jnp.bfloat16),
                grad_attn,
                preferred_element_type=jnp.float32,
            )
            keys_acc = lax.dynamic_update_slice_in_dim(
                state[3],
                lax.dynamic_slice_in_dim(state[3], offset, back_sub_len, 1) + grad_key_blk,
                offset,
                1,
            )
            values_acc = lax.dynamic_update_slice_in_dim(
                state[4],
                lax.dynamic_slice_in_dim(state[4], offset, back_sub_len, 1) + grad_value_blk,
                offset,
                1,
            )
            return (grad_query, state[1] + add_rows, state[2] + add_cols, keys_acc, values_acc)

        folded = lax.fori_loop(0, back_piece_len // back_sub_len, back_advance, back_init)
        grad_keys, grad_values = (
            lax.psum_scatter(
                folded[3].astype(jnp.bfloat16), "ctx", scatter_dimension=1, tiled=True
            ).astype(jnp.float32),
            lax.psum_scatter(
                folded[4].astype(jnp.bfloat16), "ctx", scatter_dimension=1, tiled=True
            ).astype(jnp.float32),
        )
        grad_query = jnp.transpose(folded[0] * score_scale, (0, 2, 1, 3))
        grad_rel_rows = jnp.transpose(folded[1], (0, 2, 1, 3)).reshape(
            images, band_grid, grid_side, local_heads, grid_side
        )
        grad_rel_cols = jnp.transpose(folded[2], (0, 2, 1, 3)).reshape(
            images, band_grid, grid_side, local_heads, grid_side
        )
        query_grid = queries.astype(jnp.float32).reshape(
            images, band_grid, grid_side, local_heads, head_dim
        )
        rel_query = jnp.einsum(
            "byxhk,ykc->byxhc", grad_rel_rows, band_table, precision=highest
        ) + jnp.einsum("byxhk,xkc->byxhc", grad_rel_cols, cols_table, precision=highest)
        grad_query = grad_query + rel_query.reshape(images, band_len, local_heads, head_dim)
        band_rows_grad = jnp.einsum(
            "byxhk,byxhc->ykc", grad_rel_rows, query_grid, precision=highest
        )
        cols_grad = jnp.einsum("byxhk,byxhc->xkc", grad_rel_cols, query_grid, precision=highest)
        grad_rows_tab = grad_rows_tab + jnp.einsum(
            "ykt,ykc->tc", band_hot, band_rows_grad, precision=highest
        )
        grad_cols_tab = grad_cols_tab + jnp.einsum(
            "xkt,xkc->tc", cols_hot, cols_grad, precision=highest
        )
        grad_mixed = (
            jnp.stack((grad_query, grad_keys, grad_values), axis=2)
            .astype(jnp.bfloat16)
            .reshape(tokens, qkv_width)
        )
        grad_qkv = grad_qkv + lax.dot_general(
            first_act, grad_mixed, over_rows, preferred_element_type=jnp.float32
        )
        grad_first = lax.dot_general(
            grad_mixed, flat_qkv, over_cols, preferred_element_type=jnp.float32
        ).reshape(images, band_len, model_width)
        gain_one = gain_one + jnp.sum(grad_first * normed1, axis=(0, 1))
        shift_one = shift_one + jnp.sum(grad_first, axis=(0, 1))
        input_grads.append(
            grad_middle
            + lax.psum_scatter(
                norm_back(grad_first, normed1, inv_std1, norm1_gain).astype(jnp.bfloat16),
                "tp",
                scatter_dimension=2,
                tiled=True,
            ).astype(jnp.float32)
        )
    owned_grads = (
        lax.psum_scatter(
            grad_qkv.reshape(model_width, 3, local_heads * head_dim).astype(jnp.bfloat16),
            ("fsdp", "ctx"),
            scatter_dimension=0,
            tiled=True,
        ).astype(jnp.float32),
        lax.psum_scatter(
            grad_proj.astype(jnp.bfloat16), ("fsdp", "ctx"), scatter_dimension=1, tiled=True
        ).astype(jnp.float32),
        lax.psum_scatter(
            grad_up.astype(jnp.bfloat16), ("fsdp", "ctx"), scatter_dimension=0, tiled=True
        ).astype(jnp.float32),
        lax.psum_scatter(
            grad_down.astype(jnp.bfloat16), ("fsdp", "ctx"), scatter_dimension=1, tiled=True
        ).astype(jnp.float32),
    )
    small_sums = lax.psum(
        (gain_one, shift_one, grad_rows_tab, grad_cols_tab, gain_two, shift_two),
        ("fsdp", "ctx", "tp"),
    )
    return (
        jnp.concatenate(outputs, axis=0),
        jnp.concatenate(input_grads, axis=0),
        small_sums[0],
        small_sums[1],
        owned_grads[0],
        small_sums[2],
        small_sums[3],
        owned_grads[1],
        small_sums[4],
        small_sums[5],
        owned_grads[2],
        owned_grads[3],
    )


f32 = jnp.float32
bf16 = jnp.bfloat16
LOG2E = 1.4426950408889634
NN = (((1,), (0,)), ((), ()))
NT = (((1,), (1,)), ((), ()))
TN = (((0,), (0,)), ((), ()))
VMEM_BYTES = 56 << 20


def mm(lhs, rhs, dims=NN):
    return lax.dot_general(lhs, rhs, dims, preferred_element_type=f32)


def pxor(value, axis, bit):
    size = lax.axis_size(axis)
    return lax.ppermute(value, axis, [(i, i ^ bit) for i in range(size)])


def after(values, done):
    return lax.optimization_barrier((values, done))[0]


def gather_tp(share):
    from_x = pxor(share, "tp", 2)
    from_core = pxor(share, "tp", 1)
    return [share, from_core, from_x, pxor(from_x, "tp", 1)]


def swap_ctx(pieces):
    return [pieces[0]] + [pxor(pieces[s], "ctx", s) for s in range(1, len(pieces))]


def erf(x):
    x = jnp.clip(x, -3.7439211627767994, 3.7439211627767994)
    s = x * x
    top = jnp.full_like(s, 2.2905065861350646e-4)
    for coef in (3.4082910107109506e-3, 5.0955695062380861e-2, 0.18520832239976145, 1.128379143519084):
        top = top * s + coef
    low = jnp.full_like(s, -1.1791602954361697e-7)
    for coef in (
        2.3547966471313185e-5,
        1.0179625278914885e-3,
        1.4070470171167667e-2,
        1.1098505178285362e-1,
        4.9746925110067538e-1,
        1.0,
    ):
        low = low * s + coef
    return x * top / low


ROWS = 64
ANY = pl.BlockSpec(memory_space=pl.ANY)
MESH = pl.DeviceIdType.MESH


def xor4(a, b):
    high = lax.rem(lax.div(a, 2) + lax.div(b, 2), 2)
    return 2 * high + lax.rem(lax.rem(a, 2) + lax.rem(b, 2), 2)


def spots():
    t, y = lax.axis_index("tp"), lax.axis_index("fsdp")
    return xor4(t, 2 * y), lax.axis_index("ctx")


def peer(axis, bit):
    return {axis: xor4(lax.axis_index(axis), bit)}


def greet(peers):
    barrier = pltpu.get_barrier_semaphore()
    for device in peers:
        pl.semaphore_signal(barrier, inc=1, device_id=device, device_id_type=MESH)
    pl.semaphore_wait(barrier, len(peers))


def remote(source, target, sems, slot, device):
    send, recv = sems
    return pltpu.make_async_remote_copy(
        src_ref=source,
        dst_ref=target,
        send_sem=send.at[slot],
        recv_sem=recv.at[slot],
        device_id=device,
        device_id_type=MESH,
    )


class Quiet:
    ins, out_shape, scratch, ident = (), (), (), None

    def steps(self, ins, outs, scratch):
        return {}


class SwapCtx:
    def __init__(self, pieces, ident, last):
        self.ins, self.ident, self.last = tuple(pieces[1:]), ident, last
        self.out_shape = [(p.shape, bf16) for p in self.ins]
        self.scratch = [pltpu.SemaphoreType.DMA((3,)), pltpu.SemaphoreType.DMA((3,))]

    def steps(self, ins, outs, scratch):
        def copies():
            return [remote(ins[s], outs[s], scratch, s, peer("ctx", s + 1)) for s in range(3)]

        def begin():
            greet([peer("ctx", s) for s in (1, 2, 3)])
            for copy in copies():
                copy.start()

        def end():
            for copy in copies():
                copy.wait()

        return {0: begin, self.last: end}


class SpreadHeads:
    def __init__(self, pieces, ident, points):
        self.ins, self.ident, self.points = tuple(pieces), ident, points
        self.out_shape = [((4, 4) + pieces[0].shape, bf16)]
        self.scratch = [
            pltpu.SemaphoreType.DMA((6,)),
            pltpu.SemaphoreType.DMA((6,)),
            pltpu.SemaphoreType.DMA,
        ]

    def steps(self, ins, outs, scratch):
        (out,) = outs
        sems, local_sem = scratch[:2], scratch[2]

        def first():
            return [
                remote(ins[s], out.at[0, s], sems, s - 1, peer("ctx", s)) for s in range(1, 4)
            ]

        def local():
            return pltpu.make_async_copy(ins[0], out.at[0, 0], local_sem)

        def second():
            return [
                remote(out.at[0], out.at[2], sems, 3, peer("tp", 2)),
                remote(out.at[0], out.at[1], sems, 4, peer("tp", 1)),
            ]

        def third():
            return remote(out.at[2], out.at[3], sems, 5, peer("tp", 1))

        def begin():
            greet([peer("ctx", s) for s in (1, 2, 3)] + [peer("tp", 1), peer("tp", 2)])
            local().start()
            for copy in first():
                copy.start()

        def forward():
            local().wait()
            for copy in first():
                copy.wait()
            for copy in second():
                copy.start()

        def final():
            second()[0].wait()
            third().start()

        def end():
            second()[1].wait()
            third().wait()

        return dict(zip(self.points, (begin, forward, final, end)))


class ReduceTp:
    def __init__(self, keep, send, cot, ident, points):
        self.ins, self.ident, self.points = (keep, send, cot), ident, points
        rows, tokens = keep.shape
        self.out_shape = [
            (keep.shape, bf16),
            (keep.shape, bf16),
            ((rows // 2, tokens), f32),
        ]
        self.scratch = [pltpu.VMEM(keep.shape, bf16)] * 5 + [
            pltpu.VMEM((rows // 2, tokens), f32),
            pltpu.SemaphoreType.DMA((3,)),
            pltpu.SemaphoreType.DMA((3,)),
            pltpu.SemaphoreType.DMA((5,)),
        ]

    def steps(self, ins, outs, scratch):
        keep, send, cot = ins
        own_out, other_out, exact_out = outs
        mine, from_core, from_x, grads, result, exact = scratch[:6]
        sems, local_sem = scratch[6:8], scratch[8]
        rows = mine.shape[0]
        half = rows // 2
        spot, _ = spots()
        core = lax.rem(spot, 2)

        def core_copy():
            return remote(send, from_core, sems, 0, peer("tp", 1))

        def x_copy():
            return remote(mine, from_x, sems, 1, peer("tp", 2))

        def back_copy():
            return remote(result, other_out, sems, 2, peer("tp", 1))

        def loads():
            copies = [pltpu.make_async_copy(keep, mine, local_sem.at[0])]
            for n in range(2):
                rows_at = pl.ds(pl.multiple_of((2 * n + core) * half, half), half)
                copies.append(
                    pltpu.make_async_copy(
                        cot.at[rows_at], grads.at[n * half : (n + 1) * half], local_sem.at[n + 1]
                    )
                )
            return copies

        def stores():
            return [
                pltpu.make_async_copy(result, own_out, local_sem.at[3]),
                pltpu.make_async_copy(exact, exact_out, local_sem.at[4]),
            ]

        def begin():
            greet([peer("tp", 1), peer("tp", 2)])
            core_copy().start()
            for copy in loads():
                copy.start()

        def add_core():
            for copy in loads():
                copy.wait()
            core_copy().wait()

            def add(n, carry):
                at = pl.ds(pl.multiple_of(n * 16, 16), 16)
                mine[at] = (mine[at].astype(f32) + from_core[at].astype(f32)).astype(bf16)
                return carry

            lax.fori_loop(0, rows // 16, add, 0)
            x_copy().start()

        def add_x():
            x_copy().wait()
            for part in range(2):

                def add(n, carry, part=part):
                    at = pl.ds(pl.multiple_of(part * half + n * 16, 16), 16)
                    total = mine[at].astype(f32) + from_x[at].astype(f32) + grads[at].astype(f32)
                    result[at] = total.astype(bf16)

                    @pl.when(lax.div(spot, 2) == part)
                    def _():
                        exact[pl.ds(pl.multiple_of(n * 16, 16), 16)] = total

                    return carry

                lax.fori_loop(0, half // 16, add, 0)
            back_copy().start()
            for copy in stores():
                copy.start()

        def end():
            for copy in stores():
                copy.wait()
            back_copy().wait()

        return dict(zip(self.points, (begin, add_core, add_x, end)))


def take(refs, count):
    return refs[:count], refs[count:]


def run_step(steps, index, last=None):
    for point, step in steps.items():
        if point != "end":
            pl.when(index == point)(step)
    if last is not None and "end" in steps:
        pl.when(last)(steps["end"])


def assemble(place, pieces, full):
    count = len(pieces)
    share = pieces[0].shape[-2]
    for mine in range(count):

        @pl.when(place == mine)
        def _(mine=mine):
            for a in range(count):
                piece = pieces[a ^ mine]
                value = piece[0] if len(piece.shape) == 3 else piece[...]
                full[a * share : (a + 1) * share, :] = value


def spread(parts, place, keep_ref, send_ref):
    core = lax.rem(place, 2)
    share = parts.shape[1]
    for n in range(2):
        keep_ref[n * share : (n + 1) * share] = parts[2 * n + core]
        send_ref[n * share : (n + 1) * share] = parts[2 * n + 1 - core]


def put_parts(parts, first, value):
    share = parts.shape[1]
    for n in range(value.shape[0] // share):
        parts[first + n] = value[n * share : (n + 1) * share].astype(bf16)


def over_rows_of(count, body, init, unroll=2):
    def advance(n, carry):
        return body(pl.ds(pl.multiple_of(n * ROWS, ROWS), ROWS), carry)

    return lax.fori_loop(0, count // ROWS, advance, init, unroll=unroll)


def fold8(value):
    return jnp.sum(value.reshape(value.shape[0] // 8, 8, value.shape[1]), axis=0)


def wide(value, lanes):
    return jnp.concatenate([value] * (lanes // 128), axis=1)


def moments(full):
    rows, lanes = full.shape
    zero = jnp.zeros((8, lanes), f32)
    total = over_rows_of(rows, lambda at, c: c + fold8(full[at].astype(f32)), zero)
    mean = jnp.sum(total, axis=0, keepdims=True) * (1.0 / rows)

    def square(at, c):
        center = full[at].astype(f32) - mean
        return c + fold8(center * center)

    total = over_rows_of(rows, square, zero)
    var = jnp.sum(total, axis=0, keepdims=True) * (1.0 / rows)
    return mean, lax.rsqrt(var + epsilon)


def normalize(full, act, gain, shift):
    mean, inv_std = moments(full)
    lanes = full.shape[1]

    def write(at, carry):
        normed = (full[at].astype(f32) - mean) * inv_std
        act[at] = (normed * wide(gain[at], lanes) + wide(shift[at], lanes)).astype(bf16)
        return carry

    over_rows_of(full.shape[0], write, 0)
    return mean, inv_std


def lane_sums(value):
    total = value[:, 0:128]
    for n in range(1, value.shape[1] // 128):
        total += value[:, n * 128 : (n + 1) * 128]
    return total


def norm_back_into(parts, upstream, full, mean, inv_std, gain, sums):
    width, lanes = upstream.shape
    share = parts.shape[1]
    scale = 1.0 / width

    @pl.when(pl.program_id(0) == 0)
    def _():
        sums[...] = jnp.zeros_like(sums)

    def gather(at, carry):
        plain, mixed = carry
        up = upstream[at]
        normed = (full[at].astype(f32) - mean) * inv_std
        both = up * normed
        g = gain[at]
        sums[0, at] += lane_sums(both)
        sums[1, at] += lane_sums(up)
        g = wide(g, lanes)
        return plain + fold8(up * g), mixed + fold8(both * g)

    zero = jnp.zeros((8, lanes), f32)
    plain, mixed = over_rows_of(width, gather, (zero, zero))
    plain = jnp.sum(plain, axis=0, keepdims=True) * scale
    mixed = jnp.sum(mixed, axis=0, keepdims=True) * scale
    for p in range(4):

        def write(n, carry, p=p):
            at = pl.ds(pl.multiple_of(p * share + n * ROWS, ROWS), ROWS)
            normed = (full[at].astype(f32) - mean) * inv_std
            result = (upstream[at] * wide(gain[at], lanes) - plain - normed * mixed) * inv_std
            parts[p, pl.ds(pl.multiple_of(n * ROWS, ROWS), ROWS)] = result.astype(bf16)
            return carry

        lax.fori_loop(0, share // ROWS, write, 0)


def whole_spec(shape):
    return pl.BlockSpec(shape, lambda *_: (0,) * len(shape))


def cols_spec(height, block):
    return pl.BlockSpec((height, block), lambda i, *_: (0, i))


def image_spec(image, height, block):
    return pl.BlockSpec((1, height, block), lambda i, *_: (image, 0, i))


def fixed_spec(shape):
    return pl.BlockSpec(shape, lambda *_: (0,) * len(shape), pipeline_mode=pl.Buffered(1))


def call(body, grid, in_specs, out_specs, out_shape, scratch, name, args, back=Quiet(), vmem=48):
    count = len(out_shape)

    def kernel(*refs):
        ins, refs = take(refs, len(args))
        back_ins, refs = take(refs, len(back.ins))
        outs, refs = take(refs, count)
        back_outs, refs = take(refs, len(back.out_shape))
        own, back_scratch = take(refs, len(scratch))
        body(back.steps(back_ins, back_outs, back_scratch), *ins, *outs, *own)

    shapes = list(out_shape) + list(back.out_shape)
    params = dict(vmem_limit_bytes=vmem << 20)
    if back.ident is not None:
        params.update(collective_id=back.ident, has_side_effects=True)
    out = pl.pallas_call(
        kernel,
        grid=grid,
        in_specs=list(in_specs) + [ANY] * len(back.ins),
        out_specs=list(out_specs) + [ANY] * len(back.out_shape),
        scratch_shapes=list(scratch) + list(back.scratch),
        out_shape=[jax.ShapeDtypeStruct(s, d) for s, d in shapes],
        compiler_params=pltpu.CompilerParams(**params),
        cost_estimate=pl.CostEstimate(flops=1 << 20, bytes_accessed=1 << 16, transcendentals=0),
        name=name,
    )(*args, *back.ins)
    return out if back.ident is None else (out[:count], out[count:])


def qkv_kernel(_, *refs):
    pieces, (gain, shift, own, other), (full, act), outs, mixed = (
        refs[:4],
        refs[4:8],
        refs[8:10],
        refs[10:14],
        refs[14],
    )
    spot, z = spots()
    assemble(spot, pieces, full)
    normalize(full, act, gain, shift)
    half = own.shape[1]
    product = mm(own[...], act[0:half]) + mm(other[...], act[half:])
    mixed[...] = product.astype(bf16).reshape(mixed.shape)
    rows = mixed.shape[1]
    for s in range(4):
        head = xor4(z, s)
        for k, part in enumerate((1, 2, 0)):
            outs[s][k * rows : (k + 1) * rows] = mixed[part * 4 + head]


def qkv_call(pieces, gain, shift, own, other, hd):
    share, tokens = pieces[0].shape
    width = gain.shape[0]
    total = own.shape[0]
    block = 256
    return call(
        qkv_kernel,
        (tokens // block,),
        [cols_spec(share, block)] * 4 + [fixed_spec(gain.shape)] * 2 + [fixed_spec(own.shape)] * 2,
        [cols_spec(width, block)] * 2 + [cols_spec(3 * hd, block)] * 4,
        [((width, tokens), bf16)] * 2 + [((3 * hd, tokens), bf16)] * 4,
        [pltpu.VMEM((total // hd, hd, block), bf16)],
        "qkv",
        (*pieces, gain, shift, own, other),
        vmem=24,
    )


def mlp_kernel(steps, heads, full, *refs):
    cots = refs[:4]
    gain, shift, proj, up, down = refs[4:9]
    act2, cot, hidden, grad_pre, keep_f, send_f, keep_b, send_b, sums, mid_own, joined = refs[9:20]
    mixed, mid, upstream, parts = refs[20:24]
    step_at = pl.program_id(0)
    run_step(steps, step_at)
    spot, z = spots()
    for r in range(4):
        for s in range(4):
            mixed[r, xor4(z, s)] = heads[r, s]
    joined[...] = mixed[0].reshape(joined.shape)
    assemble(spot, cots, cot)
    width, lanes = mid.shape
    mid[...] = mm(proj[...], mixed[...].reshape(width, lanes), TN)

    def residual(at, carry):
        mid[at] += full[at].astype(f32)
        return carry

    over_rows_of(width, residual, 0)
    share = mid_own.shape[0]
    mid_own[...] = mid[pl.ds(pl.multiple_of(spot * share, share), share)]
    mean, inv_std = normalize(mid, act2, gain, shift)
    step, rows = 256, 32
    for n in range(hidden.shape[0] // step):
        at = slice(n * step, (n + 1) * step)
        pre_all = mm(up[:, at], act2[...], TN)
        grad_all = mm(down[at], cot[...])
        for r in range(step // rows):
            part = slice(r * rows, (r + 1) * rows)
            to = slice(n * step + r * rows, n * step + (r + 1) * rows)
            pre = pre_all[part]
            cdf = 0.5 * (1.0 + erf(pre * 0.7071067811865476))
            hidden[to] = (pre * cdf).astype(bf16)
            slope = cdf + pre * (jnp.exp(-0.5 * pre * pre) * 0.3989422804014327)
            grad_pre[to] = (grad_all[part] * slope).astype(bf16)
    put_parts(parts, 0, mm(down[...], hidden[...], TN))
    spread(parts, spot, keep_f, send_f)
    upstream[...] = mm(up[...], grad_pre[...])
    norm_back_into(parts, upstream, mid, mean, inv_std, gain, sums)
    spread(parts, spot, keep_b, send_b)
    pl.when(step_at == pl.num_programs(0) - 1)(steps.get("end", lambda: None))


def mlp_call(image, heads, full, cots, gain, shift, proj, up, down, back):
    width, tokens = full.shape
    hid = up.shape[1]
    share = width // 4
    hd = heads.shape[2]
    block = 256
    half = width // 2
    return call(
        mlp_kernel,
        (tokens // block,),
        [
            pl.BlockSpec((4, 4, hd, block), lambda i: (0, 0, 0, i)),
            cols_spec(width, block),
        ]
        + [image_spec(image, share, block)] * 4
        + [fixed_spec(gain.shape)] * 2
        + [fixed_spec(proj.shape), fixed_spec(up.shape), fixed_spec(down.shape)],
        [cols_spec(width, block)] * 2
        + [cols_spec(hid, block)] * 2
        + [cols_spec(half, block)] * 4
        + [whole_spec((2, width, 128)), cols_spec(share, block), cols_spec(4 * hd, block)],
        [((width, tokens), bf16)] * 2
        + [((hid, tokens), bf16)] * 2
        + [((half, tokens), bf16)] * 4
        + [((2, width, 128), f32), ((share, tokens), f32), ((4 * hd, tokens), bf16)],
        [
            pltpu.VMEM((4, 4, hd, block), bf16),
            pltpu.VMEM((width, block), f32),
            pltpu.VMEM((width, block), f32),
            pltpu.VMEM((4, share, block), bf16),
        ],
        "mlp%d" % image,
        (heads, full, *cots, gain, shift, proj, up, down),
        back,
    )


def gattn_kernel(_, own, other, weight, full, *refs):
    outs, mixed = refs[:4], refs[4]
    spot, z = spots()
    core = lax.rem(spot, 2)
    half = own.shape[0] // 2
    for n in range(2):
        rows = slice(n * half, (n + 1) * half)
        full[pl.ds(pl.multiple_of((2 * n + core) * half, half), half)] = own[rows]
        full[pl.ds(pl.multiple_of((2 * n + 1 - core) * half, half), half)] = other[rows]
    mixed[...] = mm(weight[...], full[...]).astype(bf16).reshape(mixed.shape)
    for s in range(4):
        outs[s][...] = mixed[xor4(z, s)]


def gattn_call(own, other, weight, hd):
    half, tokens = own.shape
    total, width = weight.shape
    block = 256
    return call(
        gattn_kernel,
        (tokens // block,),
        [cols_spec(half, block)] * 2 + [fixed_spec(weight.shape)],
        [cols_spec(width, block)] + [cols_spec(hd, block)] * 4,
        [((width, tokens), bf16)] + [((hd, tokens), bf16)] * 4,
        [pltpu.VMEM((total // hd, hd, block), bf16)],
        "gattn",
        (own, other, weight),
        vmem=20,
    )


def gin_kernel(_, *refs):
    pieces, full, gain, own, other = refs[:4], refs[4], refs[5], refs[6], refs[7]
    keep, send, joined, sums, mixed, upstream, parts = refs[8:15]
    spot, z = spots()
    rows = mixed.shape[1]
    for s in range(4):
        head = xor4(z, s)
        for k, part in enumerate((1, 2, 0)):
            mixed[part * 4 + head] = pieces[s][k * rows : (k + 1) * rows]
    joined[...] = mixed[...].reshape(joined.shape)
    half = own.shape[1]
    upstream[0:half] = mm(own[...], joined[...], TN)
    upstream[half:] = mm(other[...], joined[...], TN)
    mean, inv_std = moments(full)
    norm_back_into(parts, upstream, full, mean, inv_std, gain, sums)
    spread(parts, spot, keep, send)


def gin_call(pieces, full, gain, own, other, hd):
    rows, tokens = pieces[0].shape
    width = gain.shape[0]
    total = own.shape[0]
    block = 256
    half = width // 2
    return call(
        gin_kernel,
        (tokens // block,),
        [cols_spec(rows, block)] * 4
        + [cols_spec(width, block), fixed_spec(gain.shape)]
        + [fixed_spec(own.shape)] * 2,
        [cols_spec(half, block)] * 2 + [cols_spec(total, block), whole_spec((2, width, 128))],
        [((half, tokens), bf16)] * 2 + [((total, tokens), bf16), ((2, width, 128), f32)],
        [
            pltpu.VMEM((total // hd, hd, block), bf16),
            pltpu.VMEM((width, block), f32),
            pltpu.VMEM((4, width // 4, block), bf16),
        ],
        "gin",
        (*pieces, full, gain, own, other),
        vmem=28,
    )


def band_start(place, chunk, size, band):
    return xor4(place, lax.div(chunk * size, band)) * band + lax.rem(chunk * size, band)


def fwd_kernel(dims, steps, *refs):
    hd, side, scale = dims
    _, place = spots()
    pieces, table = refs[:4], refs[4]
    outs, kvq, exact, lse, qa = refs[5:9], refs[9], refs[10], refs[11], refs[12]
    ka, va, low = refs[13:16]
    band = pieces[0].shape[1]
    seq = kvq.shape[1]
    step = 512
    bq, bk = band, 1024
    for s in range(4):
        kvq[:, s * band : (s + 1) * band] = pieces[s][...]
    lane = lax.broadcasted_iota(jnp.int32, (step, 128), 1)
    row = lax.broadcasted_iota(jnp.int32, (step, 128), 0)
    lane_side = lax.broadcasted_iota(jnp.int32, (side, 128), 1)
    row16 = lax.broadcasted_iota(jnp.int32, (16, step), 0)
    pad = jnp.zeros((128 - hd, step), bf16)

    def prepare(c, carry):
        at = pl.ds(pl.multiple_of(c * step, step), step)
        start = band_start(place, c, step, band)
        keys = jnp.transpose(jnp.concatenate([kvq[0:hd, at], pad], axis=0).astype(f32))
        ka[at, 0:128] = keys.astype(bf16)
        pos = row + start
        want = jnp.where(lane < side, lax.div(pos, side), lax.rem(pos, side) + side)
        ka[at, 128:256] = jnp.where(want == lane, 1.0, 0.0).astype(bf16)
        va[0:hd, at] = kvq[hd : 2 * hd, at]
        va[hd : hd + 16, at] = jnp.where(row16 == 0, 1.0, 0.0).astype(bf16)
        queries = jnp.concatenate([kvq[2 * hd : 3 * hd, at], pad], axis=0)
        qa[0:128, at] = (queries.astype(f32) * (scale * LOG2E)).astype(bf16)
        terms = lax.dot_general(queries, table[...], (((0,), (1,)), ((), ())), preferred_element_type=f32)
        parts = []
        for r in range(step // side):
            y = lax.div(start, side) + r
            by_row = terms[r * side : (r + 1) * side, 0:128]
            by_col = terms[r * side : (r + 1) * side, 128:256]
            by_row = pltpu.roll(by_row, lax.rem(side + 1 + y, 128), 1)
            by_col = pltpu.roll(by_col, 1, 1, stride=1, stride_axis=0)
            parts.append(jnp.where(lane_side < side, by_row, by_col))
        rel = jnp.concatenate(parts, axis=0) * LOG2E
        qa[128:256, at] = jnp.transpose(rel).astype(bf16)
        return carry

    lax.fori_loop(0, seq // step, prepare, 0)

    def queries_loop(i, carry):
        at = pl.ds(pl.multiple_of(i * bq, bq), bq)
        q_block = qa[:, at]

        def keys_loop(j, state):
            peak, total = state
            run_step(steps, i * (seq // bk) + j)
            keys = pl.ds(pl.multiple_of(j * bk, bk), bk)
            logits = mm(ka[keys, :], q_block)
            new_peak = jnp.maximum(peak, jnp.max(logits, axis=0, keepdims=True))
            weights = jnp.exp2(logits - new_peak).astype(bf16)
            total = total * jnp.exp2(peak - new_peak) + mm(va[:, keys], weights)
            return new_peak, total

        peak, total = lax.fori_loop(
            0,
            seq // bk,
            keys_loop,
            (jnp.full((1, bq), lowest, f32), jnp.zeros((hd + 16, bq), f32)),
        )
        denom = total[hd : hd + 1]
        value = total[0:hd] / denom
        exact[:, at] = value
        low[:, at] = value.astype(bf16)
        lse[:, at] = jnp.broadcast_to(peak + jnp.log2(denom), (8, bq))
        return carry

    lax.fori_loop(0, seq // bq, queries_loop, 0)
    for s in range(4):
        outs[s][...] = low[:, s * band : (s + 1) * band]
    steps.get("end", lambda: None)()


def fwd_call(pieces, table, hd, side, back, name):
    rows, band = pieces[0].shape
    seq = 4 * band
    return call(
        functools.partial(fwd_kernel, (hd, side, hd ** (-0.5))),
        (1,),
        [fixed_spec((rows, band))] * 4 + [fixed_spec(table.shape)],
        [fixed_spec((hd, band))] * 4
        + [fixed_spec((rows, seq)), fixed_spec((hd, seq)), fixed_spec((8, seq)), fixed_spec((256, seq))],
        [((hd, band), bf16)] * 4
        + [((rows, seq), bf16), ((hd, seq), f32), ((8, seq), f32), ((256, seq), bf16)],
        [
            pltpu.VMEM((seq, 256), bf16),
            pltpu.VMEM((hd + 16, seq), bf16),
            pltpu.VMEM((hd, seq), bf16),
        ],
        name,
        (*pieces, table),
        back,
        vmem=36,
    )


def split3(value):
    high = value.astype(bf16).astype(f32)
    rest = value - high
    mid = rest.astype(bf16).astype(f32)
    return high, mid, rest - mid


def bwd_kernel(dims, steps, *refs):
    hd, side, scale = dims
    _, place = spots()
    grads, kvq, qa_in, exact, lse, table = refs[:4], refs[4], refs[5], refs[6], refs[7], refs[8]
    outs, dtab = refs[9:13], refs[13]
    ka, kt, va, qa, da, qn, dn, dk, dv, res = refs[14:24]
    band = grads[0].shape[1]
    seq = kvq.shape[1]
    step = 512
    bq, bk = band, 1024
    for s in range(4):
        da[0:hd, s * band : (s + 1) * band] = grads[s][...]
    lane = lax.broadcasted_iota(jnp.int32, (step, 128), 1)
    row = lax.broadcasted_iota(jnp.int32, (step, 128), 0)
    lane_side = lax.broadcasted_iota(jnp.int32, (side, 128), 1)
    extra = lax.broadcasted_iota(jnp.int32, (128 - hd, step), 0)
    pad = jnp.zeros((128 - hd, step), bf16)
    ones = (lane >= hd) & (lane < hd + 3)

    def turned(value):
        return jnp.transpose(jnp.concatenate([value, pad], axis=0).astype(f32))

    def special(value):
        high, mid, rest = split3(value)
        picked = jnp.where(extra == 0, high, jnp.where(extra == 1, mid, jnp.where(extra == 2, rest, 0.0)))
        return picked.astype(bf16)

    def prepare(c, carry):
        at = pl.ds(pl.multiple_of(c * step, step), step)
        start = band_start(place, c, step, band)
        k_part = kvq[0:hd, at]
        q_part = kvq[2 * hd : 3 * hd, at]
        kt[0:128, at] = jnp.concatenate([k_part, pad], axis=0)
        ka[at, 0:128] = jnp.where(ones, 1.0, turned(k_part)).astype(bf16)
        pos = row + start
        want = jnp.where(lane < side, lax.div(pos, side), lax.rem(pos, side) + side)
        ka[at, 128:256] = jnp.where(want == lane, 1.0, 0.0).astype(bf16)
        want = jnp.where(lane < side, lax.div(pos, side), 2 * side - 1 - lax.rem(pos, side))
        kt[128:256, at] = jnp.transpose(jnp.where(want == lane, 1.0, 0.0)).astype(bf16)
        va[at, :] = jnp.where(ones, 1.0, turned(kvq[hd : 2 * hd, at])).astype(bf16)
        dk[at, :] = jnp.zeros((step, 128), f32)
        dv[at, :] = jnp.zeros((step, 128), f32)
        d_part = da[0:hd, at]
        qn[at, :] = turned(q_part).astype(bf16)
        dn[at, :] = turned(d_part).astype(bf16)
        delta = jnp.sum(d_part.astype(f32) * exact[:, at], axis=0, keepdims=True)
        qa[0:hd, at] = qa_in[0:hd, at]
        qa[hd:128, at] = special(-lse[0:1, at])
        qa[128:256, at] = qa_in[128:256, at]
        da[hd:128, at] = special(-delta)
        return carry

    lax.fori_loop(0, seq // step, prepare, 0)
    dtab[...] = jnp.zeros_like(dtab)

    def queries_loop(i, carry):
        at = pl.ds(pl.multiple_of(i * bq, bq), bq)
        qa_i, da_i, qn_i, dn_i = qa[:, at], da[:, at], qn[at, :], dn[at, :]

        def keys_loop(j, total):
            run_step(steps, i * (seq // bk) + j)
            keys = pl.ds(pl.multiple_of(j * bk, bk), bk)
            probs = jnp.exp2(mm(ka[keys, :], qa_i))
            grad_logits = (probs * mm(va[keys, :], da_i)).astype(bf16)
            dv[keys, :] += mm(probs.astype(bf16), dn_i)
            dk[keys, :] += mm(grad_logits, qn_i)
            return total + mm(kt[:, keys], grad_logits)

        total = lax.fori_loop(0, seq // bk, keys_loop, jnp.zeros((256, bq), f32))
        rel = jnp.transpose(total[128:256])
        start = band_start(place, i, bq, band)
        parts = []
        for r in range(bq // side):
            y = lax.div(start, side) + r
            block = rel[r * side : (r + 1) * side]
            by_row = jnp.where(lane_side < side, block, 0.0)
            by_col = jnp.where(lane_side < side, 0.0, block)
            by_row = pltpu.roll(by_row, lax.rem(side + 127 - y, 128), 1)
            by_col = pltpu.roll(by_col, side + 1, 1, stride=1, stride_axis=0)
            parts.append(jnp.concatenate([by_row, by_col], axis=1))
        moved = jnp.concatenate(parts, axis=0).astype(bf16)
        dq = total[0:128] * scale + lax.dot_general(
            table[...], moved, (((0,), (1,)), ((), ())), preferred_element_type=f32
        )
        res[2 * hd : 3 * hd, at] = dq[0:hd].astype(bf16)
        dtab[...] += mm(moved, qn_i, TN)
        return carry

    lax.fori_loop(0, seq // bq, queries_loop, 0)

    def finish(c, carry):
        at = pl.ds(pl.multiple_of(c * step, step), step)
        res[0:hd, at] = jnp.transpose(dk[at, :] * scale)[0:hd].astype(bf16)
        res[hd : 2 * hd, at] = jnp.transpose(dv[at, :])[0:hd].astype(bf16)
        return carry

    lax.fori_loop(0, seq // step, finish, 0)
    for s in range(4):
        outs[s][...] = res[:, s * band : (s + 1) * band]
    steps.get("end", lambda: None)()


def bwd_call(grads, kvq, qa, exact, lse, table, hd, side, back, name):
    rows, seq = kvq.shape
    band = seq // 4
    return call(
        functools.partial(bwd_kernel, (hd, side, hd ** (-0.5))),
        (1,),
        [fixed_spec((hd, band))] * 4
        + [fixed_spec(a.shape) for a in (kvq, qa, exact, lse, table)],
        [fixed_spec((rows, band))] * 4 + [fixed_spec((256, 128))],
        [((rows, band), bf16)] * 4 + [((256, 128), f32)],
        [
            pltpu.VMEM((seq, 256), bf16),
            pltpu.VMEM((256, seq), bf16),
            pltpu.VMEM((seq, 128), bf16),
            pltpu.VMEM((256, seq), bf16),
            pltpu.VMEM((128, seq), bf16),
            pltpu.VMEM((seq, 128), bf16),
            pltpu.VMEM((seq, 128), bf16),
            pltpu.VMEM((seq, 128), f32),
            pltpu.VMEM((seq, 128), f32),
            pltpu.VMEM((rows, seq), bf16),
        ],
        name,
        (*grads, kvq, qa, exact, lse, table),
        back,
        vmem=52,
    )


def offset_rows(index, table):
    side = index.shape[0]
    picks = jnp.concatenate([index[::-1, 0], index[0, 1:]])
    hot = (picks[:, None] == jnp.arange(table.shape[0], dtype=jnp.int32)[None, :]).astype(f32)
    rows = jnp.dot(hot, table.astype(f32), precision=highest)
    return hot, jnp.pad(rows, ((0, 1), (0, 128 - table.shape[1]))).astype(bf16)


def fast_device(
    block_input,
    cotangent,
    norm1_gain,
    norm1_shift,
    w_qkv,
    table_rows,
    table_cols,
    w_proj,
    norm2_gain,
    norm2_shift,
    w_fc1,
    w_fc2,
    index_rows,
    index_cols,
):
    images, band_len, share = block_input.shape
    hd = table_rows.shape[1]
    side = index_rows.shape[0]
    width = norm1_gain.shape[0]
    half = width // 2
    heads = w_proj.shape[0] // hd
    t = lax.axis_index("tp")
    z = lax.axis_index("ctx")
    y = lax.axis_index("fsdp")
    spot = t ^ (2 * y)
    first = lax.div(spot, 2) == 0

    def halves(vector):
        return jnp.where(y == 0, vector, jnp.roll(vector, half, axis=-1))

    def lanes(vector):
        return jnp.broadcast_to(halves(vector)[:, None], (width, 128))

    gain1, shift1 = lanes(norm1_gain), lanes(norm1_shift)
    gain2, shift2 = lanes(norm2_gain), lanes(norm2_shift)

    tokens_in = jnp.swapaxes(block_input, 1, 2)
    grads_in = jnp.swapaxes(cotangent, 1, 2)
    own_qkv = jnp.transpose(w_qkv, (1, 2, 0)).reshape(3 * heads * hd, half)
    other_qkv = pxor(own_qkv, "fsdp", 1)
    inputs = [gather_tp(tokens_in[0])]
    for m in range(1, images):
        inputs.append(gather_tp(after(tokens_in[m], inputs[m - 1][2])))
    proj_s, up_s, down_s = after((w_proj, w_fc1, w_fc2), other_qkv)
    own_proj = jnp.concatenate([w_proj, pxor(proj_s, "fsdp", 1)], axis=1)
    projs = gather_tp(after(own_proj, inputs[-1][2]))
    full_proj = jnp.concatenate(projs, axis=0)
    cots = gather_tp(after(grads_in, projs[2]))
    full_up = jnp.concatenate([w_fc1, pxor(up_s, "fsdp", 1)], axis=0)
    full_down = jnp.concatenate([w_fc2, pxor(down_s, "fsdp", 1)], axis=1)

    hot_rows, shifted_rows = offset_rows(index_rows, table_rows)
    hot_cols, shifted_cols = offset_rows(index_cols, table_cols)
    table = jnp.concatenate([shifted_rows, shifted_cols], axis=0)
    back_table = jnp.concatenate(
        [shifted_rows, jnp.zeros((1, 128), bf16), shifted_cols[:127][::-1]], axis=0
    )

    def reduce_tp(keep, send):
        got = keep.astype(f32) + pxor(send, "tp", 1).astype(f32)
        mine = jnp.where(first, got[:share], got[share:])
        other = jnp.where(first, got[share:], got[:share]).astype(bf16)
        return mine + pxor(other, "tp", 2).astype(f32)

    state = [{} for _ in range(images)]
    token = [None]

    def ordered(values):
        return values if token[0] is None else after(values, token[0])

    def do_qkv(m):
        st = state[m]
        pieces = ordered(tuple(inputs[m]))
        st["full"], st["act1"], *st["mixed"] = qkv_call(
            pieces, gain1, shift1, own_qkv, other_qkv, hd
        )
        token[0] = st["mixed"][0]

    def do_fwd(m, back):
        st = state[m]
        pieces = ordered(tuple(st["mixed"]))
        out, extra = fwd_call(pieces, table, hd, side, back, "attn_fwd%d" % m)
        *st["attn"], st["kvq"], st["exact"], st["lse"], st["qa"] = out
        token[0] = st["lse"]
        return extra

    def do_mlp(m, back):
        st = state[m]
        heads_all = ordered(st["heads"])
        out, extra = mlp_call(
            m, heads_all, st["full"], cots, gain2, shift2, full_proj, full_up, full_down, back
        )
        st["act2"], st["cot"], st["hidden"], st["grad_pre"] = out[:4]
        st["forward"], st["backward"] = out[4:6], out[6:8]
        st["sums2"], st["middle"], st["joined"] = out[8:]
        token[0] = out[8]
        return extra

    def do_output(m):
        st = state[m]
        keep, send = ordered(tuple(st["forward"]))
        st["output"] = (st["middle"] + reduce_tp(keep, send)).astype(bf16)

    def do_gattn(m):
        st = state[m]
        own, other = ordered(tuple(st["reduced"][:2]))
        st["branch"], *grads = gattn_call(own, other, own_proj, hd)
        token[0] = st["branch"]
        st["grads"] = swap_ctx(grads)

    def do_bwd(m, back):
        st = state[m]
        pieces = ordered(tuple(st["grads"]))
        out, extra = bwd_call(
            pieces,
            st["kvq"],
            st["qa"],
            st["exact"],
            st["lse"],
            back_table,
            hd,
            side,
            back,
            "attn_bwd%d" % m,
        )
        *st["grad_mixed"], st["dtab"] = out
        token[0] = st["dtab"]
        return extra

    def do_gin(m):
        st = state[m]
        pieces = ordered(tuple(st["grad_mixed"]))
        keep, send, st["grad_joined"], st["sums1"] = gin_call(
            pieces, st["full"], gain1, own_qkv, other_qkv, hd
        )
        token[0] = st["sums1"]
        st["input_grad"] = st["reduced"][2] + reduce_tp(keep, send)

    def do_wgrad(left, right):
        parts = [state[m][left] for m in range(images)], [state[m][right] for m in range(images)]
        lefts, rights = ordered((tuple(parts[0]), tuple(parts[1])))
        total = sum(mm(a, b, NT) for a, b in zip(lefts, rights)).astype(bf16)
        token[0] = total
        return total

    first_image, second_image = state
    do_qkv(0)
    first_image["mixed"] = swap_ctx(first_image["mixed"])
    do_qkv(1)
    second_image["mixed"] = second_image["mixed"][:1] + list(
        do_fwd(0, SwapCtx(second_image["mixed"], 0, "end"))
    )
    (first_image["heads"],) = do_fwd(1, SpreadHeads(first_image["attn"], 1, (0, 8, 15, "end")))
    (second_image["heads"],) = do_mlp(0, SpreadHeads(second_image["attn"], 2, (0, 2, 3, "end")))
    first_image["reduced"] = do_mlp(
        1, ReduceTp(*first_image["backward"], first_image["cot"], 3, (0, 1, 3, "end"))
    )
    do_gattn(0)
    up_total = do_wgrad("act2", "grad_pre")
    down_total = do_wgrad("cot", "hidden")
    second_image["reduced"] = do_bwd(
        0, ReduceTp(*second_image["backward"], second_image["cot"], 4, (0, 2, 10, "end"))
    )
    do_output(0)
    do_output(1)
    do_gattn(1)
    proj_total = do_wgrad("branch", "joined")
    first_image["grad_mixed"] = first_image["grad_mixed"][:1] + list(
        do_bwd(1, SwapCtx(first_image["grad_mixed"], 5, "end"))
    )
    second_image["grad_mixed"] = swap_ctx(second_image["grad_mixed"])
    do_gin(0)
    do_gin(1)
    qkv_total = do_wgrad("act1", "grad_joined")
    sums1 = [st["sums1"] for st in state]
    sums2 = [st["sums2"] for st in state]
    tabs = [st["dtab"] for st in state]
    outputs = [st["output"] for st in state]
    input_grads = [st["input_grad"] for st in state]

    def scatter(total):
        got = total[:half].astype(f32) + pxor(total[half:], "fsdp", 1).astype(f32)
        low = got.astype(bf16)
        rows = half // 4

        def chunk(value, s):
            return lax.dynamic_slice_in_dim(value, (z ^ s) * rows, rows, 0)

        mine = chunk(got, 0)
        for s in range(1, 4):
            mine = mine + pxor(chunk(low, s), "ctx", s).astype(f32)
        return mine

    grad_up = scatter(up_total)
    grad_down = scatter(down_total).T
    grad_proj = scatter(proj_total).T
    grad_qkv = scatter(qkv_total).reshape(half // 4, 3, heads * hd)

    def pair(parts):
        return halves(jnp.sum(sum(parts), axis=2))

    small = jnp.concatenate(
        [jnp.concatenate([pair(sums1), pair(sums2)], axis=0).reshape(-1, 128), sum(tabs)], axis=0
    )
    for axis in ("tp", "fsdp", "ctx"):
        bit = 1
        while bit < lax.axis_size(axis):
            small = small + pxor(small, axis, bit)
            bit *= 2
    norms = small[: 4 * width // 128].reshape(4, width)
    tabs = small[4 * width // 128 :]
    rows_grad = jnp.dot(hot_rows.T, tabs[:127, :hd], precision=highest)
    cols_grad = jnp.dot(hot_cols.T, tabs[129:256, :hd][::-1], precision=highest)
    return (
        jnp.swapaxes(jnp.stack(outputs), 1, 2),
        jnp.swapaxes(jnp.stack(input_grads), 1, 2),
        norms[0],
        norms[1],
        grad_qkv,
        rows_grad,
        cols_grad,
        grad_proj,
        norms[2],
        norms[3],
        grad_up,
        grad_down,
    )


def per_device(*args):
    block_input, w_proj, table_rows, index_rows = args[0], args[7], args[5], args[12]
    heads = w_proj.shape[0] // table_rows.shape[1]
    fits = (
        lax.axis_size("tp") == 4
        and lax.axis_size("ctx") == 4
        and lax.axis_size("fsdp") == 2
        and heads == 4
        and index_rows.shape[0] == 64
        and table_rows.shape[1] == 80
        and block_input.shape[1] % 512 == 0
        and block_input.shape[0] == 2
    )
    return fast_device(*args) if fits else plain_device(*args)


def solution(mesh):
    in_specs = (
        P("fsdp", "ctx", "tp"),
        P("fsdp", "ctx", "tp"),
        P(),
        P(),
        P("fsdp", None, "tp"),
        P(),
        P(),
        P("tp", "fsdp"),
        P(),
        P(),
        P("fsdp", "tp"),
        P("tp", "fsdp"),
        P(),
        P(),
    )
    out_specs = (
        P("fsdp", "ctx", "tp"),
        P("fsdp", "ctx", "tp"),
        P(),
        P(),
        P(("fsdp", "ctx"), None, "tp"),
        P(),
        P(),
        P("tp", ("fsdp", "ctx")),
        P(),
        P(),
        P(("fsdp", "ctx"), "tp"),
        P("tp", ("fsdp", "ctx")),
    )
    return jax.shard_map(
        per_device, mesh=mesh, in_specs=in_specs, out_specs=out_specs, check_vma=False
    )
```

```python
import functools
import math

import jax
import jax.numpy as jnp
from jax import lax
from jax.experimental import pallas as pl
from jax.experimental.pallas import tpu as pltpu
from jax.sharding import PartitionSpec as P

MICRO = 2


epsilon = 1e-06
highest = lax.Precision.HIGHEST
block_rows = 512
lowest = -1e30


def layer_norm(values, gain_vec, shift_vec):
    center = values - jnp.mean(values, axis=-1, keepdims=True)
    inv_std = lax.rsqrt(jnp.mean(center * center, axis=-1, keepdims=True) + epsilon)
    normed = center * inv_std
    return (normed * gain_vec + shift_vec, normed, inv_std)


def norm_back(upstream, normed, inv_std, gain_vec):
    scaled = upstream * gain_vec
    inner = (
        scaled
        - jnp.mean(scaled, axis=-1, keepdims=True)
        - normed * jnp.mean(scaled * normed, axis=-1, keepdims=True)
    )
    return inner * inv_std


def gelu_pair(values):
    normal_cdf = 0.5 * (1.0 + lax.erf(values * 0.7071067811865476))
    normal_pdf = jnp.exp(-0.5 * values * values) * 0.3989422804014327
    return (values * normal_cdf, normal_cdf + values * normal_pdf)


def rel_terms(queries, band_table, cols_table, grid_side):
    shape_in = queries.shape
    shaped = queries.astype(jnp.float32).reshape(
        shape_in[0], shape_in[1] // grid_side, grid_side, shape_in[2], shape_in[3]
    )
    rows_term = jnp.einsum("byxhc,ykc->byxhk", shaped, band_table, precision=highest)
    cols_term = jnp.einsum("byxhc,xkc->byxhk", shaped, cols_table, precision=highest)
    return (
        rows_term.reshape(shape_in[:3] + (grid_side,)),
        cols_term.reshape(shape_in[:3] + (grid_side,)),
    )


def key_bias(rows_term, cols_term, first_key, key_count, grid_side):
    picked = lax.dynamic_slice_in_dim(rows_term, first_key // grid_side, key_count // grid_side, 3)
    joined = picked[..., :, None] + cols_term[..., None, :]
    return joined.reshape(picked.shape[:3] + (key_count,))


def bias_back(grad_logits, first_key, key_count, grid_side):
    split = grad_logits.reshape(grad_logits.shape[:3] + (key_count // grid_side, grid_side))
    empty = jnp.zeros(grad_logits.shape[:3] + (grid_side,), jnp.float32)
    rows_part = lax.dynamic_update_slice_in_dim(
        empty, jnp.sum(split, axis=4), first_key // grid_side, 3
    )
    return (rows_part, jnp.sum(split, axis=3))


def scores_of(queries, key_blk, rows_term, cols_term, first_key, score_scale, grid_side):
    raw_dots = jnp.einsum("brhc,bkhc->bhrk", queries, key_blk, preferred_element_type=jnp.float32)
    return raw_dots * score_scale + key_bias(
        rows_term, cols_term, first_key, key_blk.shape[1], grid_side
    )


def plain_device(
    block_input,
    cotangent,
    norm1_gain,
    norm1_shift,
    w_qkv,
    table_rows,
    table_cols,
    w_proj,
    norm2_gain,
    norm2_shift,
    w_fc1,
    w_fc2,
    index_rows,
    index_cols,
):
    grid_side = index_rows.shape[0]
    table_len = table_rows.shape[0]
    head_dim = table_rows.shape[1]
    model_width = norm1_gain.shape[0]
    band_len = block_input.shape[1]
    band_grid = band_len // grid_side
    local_heads = w_proj.shape[0] // head_dim
    hidden_local = w_fc1.shape[1]
    per_micro = block_input.shape[0] // MICRO
    score_scale = head_dim ** (-0.5)
    ctx_place = lax.axis_index("ctx")
    whole_seq = band_len * lax.axis_size("ctx")
    levels = jnp.arange(table_len, dtype=jnp.int32)
    hot_rows = (index_rows.reshape(-1)[:, None] == levels[None, :]).astype(jnp.float32)
    hot_cols = (index_cols.reshape(-1)[:, None] == levels[None, :]).astype(jnp.float32)
    rows_table = jnp.dot(hot_rows, table_rows.astype(jnp.float32), precision=highest).reshape(
        grid_side, grid_side, head_dim
    )
    cols_table = jnp.dot(hot_cols, table_cols.astype(jnp.float32), precision=highest).reshape(
        grid_side, grid_side, head_dim
    )
    band_table = lax.dynamic_slice_in_dim(rows_table, ctx_place * band_grid, band_grid, 0)
    band_hot = lax.dynamic_slice_in_dim(
        hot_rows.reshape(grid_side, grid_side, table_len), ctx_place * band_grid, band_grid, 0
    )
    cols_hot = hot_cols.reshape(grid_side, grid_side, table_len)
    over_rows = (((0,), (0,)), ((), ()))
    over_cols = (((1,), (1,)), ((), ()))
    qkv_width = 3 * local_heads * head_dim
    grad_qkv = jnp.zeros((model_width, qkv_width), jnp.float32)
    grad_proj = jnp.zeros((local_heads * head_dim, model_width), jnp.float32)
    grad_up = jnp.zeros((model_width, hidden_local), jnp.float32)
    grad_down = jnp.zeros((hidden_local, model_width), jnp.float32)
    gain_one = jnp.zeros((model_width,), jnp.float32)
    shift_one = jnp.zeros((model_width,), jnp.float32)
    gain_two = jnp.zeros((model_width,), jnp.float32)
    shift_two = jnp.zeros((model_width,), jnp.float32)
    grad_rows_tab = jnp.zeros((table_len, head_dim), jnp.float32)
    grad_cols_tab = jnp.zeros((table_len, head_dim), jnp.float32)
    outputs = []
    input_grads = []
    for micro_step in range(MICRO):
        input_part = block_input[micro_step * per_micro : (micro_step + 1) * per_micro]
        grad_part = cotangent[micro_step * per_micro : (micro_step + 1) * per_micro]
        images = input_part.shape[0]
        tokens = images * band_len
        full_qkv, full_proj, full_up, full_down = (
            lax.all_gather(w_qkv, "fsdp", axis=0, tiled=True),
            lax.all_gather(w_proj, "fsdp", axis=1, tiled=True),
            lax.all_gather(w_fc1, "fsdp", axis=0, tiled=True),
            lax.all_gather(w_fc2, "fsdp", axis=1, tiled=True),
        )
        flat_qkv = full_qkv.reshape(model_width, qkv_width)
        input_full, grad_out_full = (
            lax.all_gather(input_part, "tp", axis=2, tiled=True),
            lax.all_gather(grad_part, "tp", axis=2, tiled=True),
        )
        normed_in, normed1, inv_std1 = layer_norm(
            input_full.astype(jnp.float32), norm1_gain, norm1_shift
        )
        first_act = normed_in.astype(jnp.bfloat16).reshape(tokens, model_width)
        mixed_qkv = jnp.dot(first_act, flat_qkv, preferred_element_type=jnp.float32).astype(
            jnp.bfloat16
        )
        mixed_qkv = mixed_qkv.reshape(images, band_len, 3, local_heads, head_dim)
        queries = mixed_qkv[:, :, 0]
        key_part = mixed_qkv[:, :, 1]
        value_part = mixed_qkv[:, :, 2]
        rows_term, cols_term = rel_terms(queries, band_table, cols_table, grid_side)
        rows_swap = jnp.transpose(rows_term, (0, 2, 1, 3))
        cols_swap = jnp.transpose(cols_term, (0, 2, 1, 3))
        fold_init = (
            jnp.full((images, local_heads, band_len), lowest, jnp.float32),
            jnp.zeros((images, local_heads, band_len), jnp.float32),
            jnp.zeros((images, local_heads, band_len, head_dim), jnp.float32),
        )
        key_piece = lax.all_gather(key_part, "ctx", axis=1, tiled=True)
        value_piece = lax.all_gather(value_part, "ctx", axis=1, tiled=True)
        piece_len = key_piece.shape[1]
        sub_len = math.gcd(piece_len, block_rows)

        def forward_advance(block_idx, state):
            running, denom_sum, acc_out = state
            offset = block_idx * sub_len
            key_blk = lax.dynamic_slice_in_dim(key_piece, offset, sub_len, 1)
            value_blk = lax.dynamic_slice_in_dim(value_piece, offset, sub_len, 1)
            logits = scores_of(
                queries, key_blk, rows_swap, cols_swap, offset, score_scale, grid_side
            )
            new_peak = jnp.maximum(running, jnp.max(logits, axis=-1))
            rescale = jnp.exp(running - new_peak)
            weights = jnp.exp(logits - new_peak[..., None])
            denom_sum = denom_sum * rescale + jnp.sum(weights, axis=-1)
            acc_out = acc_out * rescale[..., None] + jnp.einsum(
                "bhrk,bkhc->bhrc",
                weights.astype(jnp.bfloat16),
                value_blk,
                preferred_element_type=jnp.float32,
            )
            return (new_peak, denom_sum, acc_out)

        peak_all, denom_all, acc_all = lax.fori_loop(
            0, piece_len // sub_len, forward_advance, fold_init
        )
        attn_exact = jnp.transpose(acc_all / denom_all[..., None], (0, 2, 1, 3))
        log_total = peak_all + jnp.log(denom_all)
        attn_low = attn_exact.astype(jnp.bfloat16).reshape(tokens, local_heads * head_dim)
        attn_branch = jnp.dot(attn_low, full_proj, preferred_element_type=jnp.float32).reshape(
            images, band_len, model_width
        )
        attn_share = lax.psum_scatter(
            attn_branch.astype(jnp.bfloat16), "tp", scatter_dimension=2, tiled=True
        ).astype(jnp.float32)
        middle_share = input_part.astype(jnp.float32) + attn_share
        middle_full = lax.all_gather(
            middle_share.astype(jnp.bfloat16), "tp", axis=2, tiled=True
        ).astype(middle_share.dtype)
        normed_mid, normed2, inv_std2 = layer_norm(middle_full, norm2_gain, norm2_shift)
        second_act = normed_mid.astype(jnp.bfloat16).reshape(tokens, model_width)
        pre_act = jnp.dot(second_act, full_up, preferred_element_type=jnp.float32)
        gelu_out, gelu_slope = gelu_pair(pre_act)
        hidden_low = gelu_out.astype(jnp.bfloat16)
        mlp_branch = jnp.dot(hidden_low, full_down, preferred_element_type=jnp.float32).reshape(
            images, band_len, model_width
        )
        mlp_share = lax.psum_scatter(
            mlp_branch.astype(jnp.bfloat16), "tp", scatter_dimension=2, tiled=True
        ).astype(jnp.float32)
        outputs.append((middle_share + mlp_share).astype(jnp.bfloat16))
        grad_out_flat = grad_out_full.reshape(tokens, model_width)
        grad_down = grad_down + lax.dot_general(
            hidden_low, grad_out_flat, over_rows, preferred_element_type=jnp.float32
        )
        grad_hidden = lax.dot_general(
            grad_out_flat, full_down, over_cols, preferred_element_type=jnp.float32
        )
        grad_pre = (grad_hidden * gelu_slope).astype(jnp.bfloat16)
        grad_up = grad_up + lax.dot_general(
            second_act, grad_pre, over_rows, preferred_element_type=jnp.float32
        )
        grad_second = lax.dot_general(
            grad_pre, full_up, over_cols, preferred_element_type=jnp.float32
        ).reshape(images, band_len, model_width)
        gain_two = gain_two + jnp.sum(grad_second * normed2, axis=(0, 1))
        shift_two = shift_two + jnp.sum(grad_second, axis=(0, 1))
        grad_middle = grad_part.astype(jnp.float32) + lax.psum_scatter(
            norm_back(grad_second, normed2, inv_std2, norm2_gain).astype(jnp.bfloat16),
            "tp",
            scatter_dimension=2,
            tiled=True,
        ).astype(jnp.float32)
        grad_branch = lax.all_gather(
            grad_middle.astype(jnp.bfloat16), "tp", axis=2, tiled=True
        ).reshape(tokens, model_width)
        grad_proj = grad_proj + lax.dot_general(
            attn_low, grad_branch, over_rows, preferred_element_type=jnp.float32
        )
        grad_attn = lax.dot_general(
            grad_branch, full_proj, over_cols, preferred_element_type=jnp.float32
        ).astype(jnp.bfloat16)
        grad_attn = grad_attn.reshape(images, band_len, local_heads, head_dim)
        delta_rows = jnp.sum(grad_attn.astype(jnp.float32) * attn_exact, axis=-1)
        delta_swap = jnp.transpose(delta_rows, (0, 2, 1))
        query_zero = jnp.zeros((images, local_heads, band_len, head_dim), jnp.float32)
        rel_zero = jnp.zeros((images, local_heads, band_len, grid_side), jnp.float32)
        whole_zero = jnp.zeros((images, whole_seq, local_heads, head_dim), jnp.float32)
        back_init = (query_zero, rel_zero, rel_zero, whole_zero, whole_zero)
        back_key_piece = lax.all_gather(key_part, "ctx", axis=1, tiled=True)
        back_value_piece = lax.all_gather(value_part, "ctx", axis=1, tiled=True)
        back_piece_len = back_key_piece.shape[1]
        back_sub_len = math.gcd(back_piece_len, block_rows)

        def back_advance(block_idx, state):
            offset = block_idx * back_sub_len
            key_blk = lax.dynamic_slice_in_dim(back_key_piece, offset, back_sub_len, 1)
            value_blk = lax.dynamic_slice_in_dim(back_value_piece, offset, back_sub_len, 1)
            logits = scores_of(
                queries, key_blk, rows_swap, cols_swap, offset, score_scale, grid_side
            )
            probs = jnp.exp(logits - log_total[..., None])
            grad_probs = jnp.einsum(
                "brhc,bkhc->bhrk", grad_attn, value_blk, preferred_element_type=jnp.float32
            )
            grad_logits = (probs * (grad_probs - delta_swap[..., None])).astype(jnp.bfloat16)
            grad_query = state[0] + jnp.einsum(
                "bhrk,bkhc->bhrc", grad_logits, key_blk, preferred_element_type=jnp.float32
            )
            add_rows, add_cols = bias_back(
                grad_logits.astype(jnp.float32), offset, back_sub_len, grid_side
            )
            grad_key_blk = (
                jnp.einsum(
                    "bhrk,brhc->bkhc", grad_logits, queries, preferred_element_type=jnp.float32
                )
                * score_scale
            )
            grad_value_blk = jnp.einsum(
                "bhrk,brhc->bkhc",
                probs.astype(jnp.bfloat16),
                grad_attn,
                preferred_element_type=jnp.float32,
            )
            keys_acc = lax.dynamic_update_slice_in_dim(
                state[3],
                lax.dynamic_slice_in_dim(state[3], offset, back_sub_len, 1) + grad_key_blk,
                offset,
                1,
            )
            values_acc = lax.dynamic_update_slice_in_dim(
                state[4],
                lax.dynamic_slice_in_dim(state[4], offset, back_sub_len, 1) + grad_value_blk,
                offset,
                1,
            )
            return (grad_query, state[1] + add_rows, state[2] + add_cols, keys_acc, values_acc)

        folded = lax.fori_loop(0, back_piece_len // back_sub_len, back_advance, back_init)
        grad_keys, grad_values = (
            lax.psum_scatter(
                folded[3].astype(jnp.bfloat16), "ctx", scatter_dimension=1, tiled=True
            ).astype(jnp.float32),
            lax.psum_scatter(
                folded[4].astype(jnp.bfloat16), "ctx", scatter_dimension=1, tiled=True
            ).astype(jnp.float32),
        )
        grad_query = jnp.transpose(folded[0] * score_scale, (0, 2, 1, 3))
        grad_rel_rows = jnp.transpose(folded[1], (0, 2, 1, 3)).reshape(
            images, band_grid, grid_side, local_heads, grid_side
        )
        grad_rel_cols = jnp.transpose(folded[2], (0, 2, 1, 3)).reshape(
            images, band_grid, grid_side, local_heads, grid_side
        )
        query_grid = queries.astype(jnp.float32).reshape(
            images, band_grid, grid_side, local_heads, head_dim
        )
        rel_query = jnp.einsum(
            "byxhk,ykc->byxhc", grad_rel_rows, band_table, precision=highest
        ) + jnp.einsum("byxhk,xkc->byxhc", grad_rel_cols, cols_table, precision=highest)
        grad_query = grad_query + rel_query.reshape(images, band_len, local_heads, head_dim)
        band_rows_grad = jnp.einsum(
            "byxhk,byxhc->ykc", grad_rel_rows, query_grid, precision=highest
        )
        cols_grad = jnp.einsum("byxhk,byxhc->xkc", grad_rel_cols, query_grid, precision=highest)
        grad_rows_tab = grad_rows_tab + jnp.einsum(
            "ykt,ykc->tc", band_hot, band_rows_grad, precision=highest
        )
        grad_cols_tab = grad_cols_tab + jnp.einsum(
            "xkt,xkc->tc", cols_hot, cols_grad, precision=highest
        )
        grad_mixed = (
            jnp.stack((grad_query, grad_keys, grad_values), axis=2)
            .astype(jnp.bfloat16)
            .reshape(tokens, qkv_width)
        )
        grad_qkv = grad_qkv + lax.dot_general(
            first_act, grad_mixed, over_rows, preferred_element_type=jnp.float32
        )
        grad_first = lax.dot_general(
            grad_mixed, flat_qkv, over_cols, preferred_element_type=jnp.float32
        ).reshape(images, band_len, model_width)
        gain_one = gain_one + jnp.sum(grad_first * normed1, axis=(0, 1))
        shift_one = shift_one + jnp.sum(grad_first, axis=(0, 1))
        input_grads.append(
            grad_middle
            + lax.psum_scatter(
                norm_back(grad_first, normed1, inv_std1, norm1_gain).astype(jnp.bfloat16),
                "tp",
                scatter_dimension=2,
                tiled=True,
            ).astype(jnp.float32)
        )
    owned_grads = (
        lax.psum_scatter(
            grad_qkv.reshape(model_width, 3, local_heads * head_dim).astype(jnp.bfloat16),
            ("fsdp", "ctx"),
            scatter_dimension=0,
            tiled=True,
        ).astype(jnp.float32),
        lax.psum_scatter(
            grad_proj.astype(jnp.bfloat16), ("fsdp", "ctx"), scatter_dimension=1, tiled=True
        ).astype(jnp.float32),
        lax.psum_scatter(
            grad_up.astype(jnp.bfloat16), ("fsdp", "ctx"), scatter_dimension=0, tiled=True
        ).astype(jnp.float32),
        lax.psum_scatter(
            grad_down.astype(jnp.bfloat16), ("fsdp", "ctx"), scatter_dimension=1, tiled=True
        ).astype(jnp.float32),
    )
    small_sums = lax.psum(
        (gain_one, shift_one, grad_rows_tab, grad_cols_tab, gain_two, shift_two),
        ("fsdp", "ctx", "tp"),
    )
    return (
        jnp.concatenate(outputs, axis=0),
        jnp.concatenate(input_grads, axis=0),
        small_sums[0],
        small_sums[1],
        owned_grads[0],
        small_sums[2],
        small_sums[3],
        owned_grads[1],
        small_sums[4],
        small_sums[5],
        owned_grads[2],
        owned_grads[3],
    )


f32 = jnp.float32
bf16 = jnp.bfloat16
LOG2E = 1.4426950408889634
NN = (((1,), (0,)), ((), ()))
NT = (((1,), (1,)), ((), ()))
TN = (((0,), (0,)), ((), ()))
VMEM_BYTES = 56 << 20


def mm(lhs, rhs, dims=NN):
    return lax.dot_general(lhs, rhs, dims, preferred_element_type=f32)


def pxor(value, axis, bit):
    size = lax.axis_size(axis)
    return lax.ppermute(value, axis, [(i, i ^ bit) for i in range(size)])


def after(values, done):
    return lax.optimization_barrier((values, done))[0]


def gather_tp(share):
    from_x = pxor(share, "tp", 2)
    from_core = pxor(share, "tp", 1)
    return [share, from_core, from_x, pxor(from_x, "tp", 1)]


def swap_ctx(pieces):
    return [pieces[0]] + [pxor(pieces[s], "ctx", s) for s in range(1, len(pieces))]


def gelu_parts(x):
    size = jnp.abs(x)
    t = 1.0 / (1.0 + 0.23164190 * size)
    poly = jnp.full_like(t, 0.5307027145)
    for coef in (-0.726576013, 0.7107068705, -0.142248368, 0.127414796):
        poly = poly * t + coef
    bell = jnp.exp2((-0.5 * LOG2E) * (x * x))
    tail = poly * t * bell
    cdf = jnp.where(x >= 0.0, 1.0 - tail, tail)
    return cdf, bell * 0.3989422804014327


ROWS = 64
ANY = pl.BlockSpec(memory_space=pl.ANY)
MESH = pl.DeviceIdType.MESH


def xor4(a, b):
    high = lax.rem(lax.div(a, 2) + lax.div(b, 2), 2)
    return 2 * high + lax.rem(lax.rem(a, 2) + lax.rem(b, 2), 2)


def spots():
    t, y = lax.axis_index("tp"), lax.axis_index("fsdp")
    return xor4(t, 2 * y), lax.axis_index("ctx")


def peer(axis, bit):
    return {axis: xor4(lax.axis_index(axis), bit)}


def greet(peers):
    barrier = pltpu.get_barrier_semaphore()
    for device in peers:
        pl.semaphore_signal(barrier, inc=1, device_id=device, device_id_type=MESH)
    pl.semaphore_wait(barrier, len(peers))


def remote(source, target, sems, slot, device):
    send, recv = sems
    return pltpu.make_async_remote_copy(
        src_ref=source,
        dst_ref=target,
        send_sem=send.at[slot],
        recv_sem=recv.at[slot],
        device_id=device,
        device_id_type=MESH,
    )


def dma(count=1):
    return pltpu.SemaphoreType.DMA((count,))


def start_all(copies):
    for copy in copies:
        copy.start()


def wait_all(copies):
    for copy in copies:
        copy.wait()


def add_rows(rows, body, step=32):
    def advance(n, carry):
        body(pl.ds(pl.multiple_of(n * step, step), step))
        return carry

    lax.fori_loop(0, rows // step, advance, 0, unroll=2 if rows % (2 * step) == 0 else 1)


CTX_PEERS = (("ctx", 1), ("ctx", 2), ("ctx", 3))
TP_PEERS = (("tp", 1), ("tp", 2))
Y_PEERS = (("fsdp", 1),)


class Quiet:
    ins, out_shape, scratch, peers = (), (), (), ()
    ident = None

    def steps(self, ins, outs, scratch):
        return {}


class Together:
    def __init__(self, ident, *backs):
        self.backs, self.ident = backs, ident
        self.ins = sum((tuple(b.ins) for b in backs), ())
        self.out_shape = sum((list(b.out_shape) for b in backs), [])
        self.scratch = sum((list(b.scratch) for b in backs), [])
        self.peers = tuple(dict.fromkeys(sum((tuple(b.peers) for b in backs), ())))

    def split(self, outs):
        groups = []
        for b in self.backs:
            group, outs = take(outs, len(b.out_shape))
            groups.append(group)
        return groups

    def steps(self, ins, outs, scratch):
        table = {0: [lambda: greet([peer(*p) for p in self.peers])]}
        for b in self.backs:
            mine_in, ins = take(ins, len(b.ins))
            mine_out, outs = take(outs, len(b.out_shape))
            mine_scratch, scratch = take(scratch, len(b.scratch))
            for point, step in b.steps(mine_in, mine_out, mine_scratch):
                table.setdefault(point, []).append(step)

        def chain(fns):
            def run():
                for fn in fns:
                    fn()

            return run

        return {point: chain(fns) for point, fns in table.items()}


class SwapCtx:
    peers = CTX_PEERS

    def __init__(self, pieces, begin=0, end="end"):
        self.ins, self.points = tuple(pieces[1:]), (begin, end)
        self.out_shape = [(p.shape, bf16) for p in self.ins]
        self.scratch = [dma(3), dma(3)]

    def steps(self, ins, outs, scratch):
        def copies():
            return [remote(ins[s], outs[s], scratch, s, peer("ctx", s + 1)) for s in (2, 1, 0)]

        return zip(self.points, (lambda: start_all(copies()), lambda: wait_all(copies())))


class JoinY:
    peers = Y_PEERS

    def __init__(self, own, axis, begin=0, end="end"):
        self.ins, self.axis, self.points = (own,), axis, (begin, end)
        shape = list(own.shape)
        shape[axis] *= 2
        self.out_shape = [(tuple(shape), bf16)]
        self.scratch = [dma(1), dma(1), dma(1)]

    def steps(self, ins, outs, scratch):
        (own,), (full,) = ins, outs
        half = own.shape[self.axis]
        low, high = pl.ds(0, half), pl.ds(half, half)

        def at(part):
            return full.at[part] if self.axis == 0 else full.at[:, part]

        def copies():
            return [
                remote(own, at(high), scratch[:2], 0, peer("fsdp", 1)),
                pltpu.make_async_copy(own, at(low), scratch[2].at[0]),
            ]

        return zip(self.points, (lambda: start_all(copies()), lambda: wait_all(copies())))


class GatherTp:
    peers = TP_PEERS

    def __init__(self, own, points):
        self.ins, self.points = (own,), points
        self.out_shape = [((4,) + own.shape, bf16)]
        self.scratch = [dma(3), dma(3), dma(1)]

    def steps(self, ins, outs, scratch):
        (own,), (full,) = ins, outs
        sems, local_sem = scratch[:2], scratch[2]

        def local():
            return pltpu.make_async_copy(own, full.at[0], local_sem.at[0])

        def to_x():
            return remote(own, full.at[2], sems, 0, peer("tp", 2))

        def to_core():
            return remote(own, full.at[1], sems, 1, peer("tp", 1))

        def onward():
            return remote(full.at[2], full.at[3], sems, 2, peer("tp", 1))

        def forward():
            to_x().wait()
            onward().start()

        return zip(
            self.points,
            (
                lambda: start_all([to_x(), to_core(), local()]),
                forward,
                lambda: wait_all([to_core(), onward(), local()]),
            ),
        )


class SpreadHeads:
    peers = CTX_PEERS + TP_PEERS

    def __init__(self, pieces, points):
        self.ins, self.points = tuple(pieces), points
        self.out_shape = [((4, 4) + pieces[0].shape, bf16)]
        self.scratch = [dma(6), dma(6), dma(1)]

    def steps(self, ins, outs, scratch):
        (out,) = outs
        sems, local_sem = scratch[:2], scratch[2]

        def arrivals():
            copies = [remote(ins[s], out.at[0, s], sems, s - 1, peer("ctx", s)) for s in range(1, 4)]
            return copies + [pltpu.make_async_copy(ins[0], out.at[0, 0], local_sem.at[0])]

        def to_x():
            return remote(out.at[0], out.at[2], sems, 3, peer("tp", 2))

        def to_core():
            return remote(out.at[0], out.at[1], sems, 4, peer("tp", 1))

        def onward():
            return remote(out.at[2], out.at[3], sems, 5, peer("tp", 1))

        def forward():
            wait_all(arrivals())
            start_all([to_x(), to_core()])

        def final():
            to_x().wait()
            onward().start()

        return zip(
            self.points,
            (
                lambda: start_all(arrivals()),
                forward,
                final,
                lambda: wait_all([to_core(), onward()]),
            ),
        )


class ReduceTp:
    peers = TP_PEERS

    def __init__(self, keep, send, cot, points, weight=None):
        self.ins, self.points = (keep, send, cot), points
        rows, tokens = keep.shape
        self.heads = weight is not None
        self.out_shape = [((2 * rows, tokens), bf16), ((rows // 2, tokens), f32)]
        self.scratch = [pltpu.VMEM(keep.shape, bf16)] * 4 + [
            pltpu.VMEM((2 * rows, tokens), bf16),
            pltpu.VMEM((rows // 2, tokens), f32),
            dma(8),
            dma(8),
            dma(7),
        ]
        if self.heads:
            self.ins += (weight,)
            hd = weight.shape[0] // 4
            self.out_shape += [((hd, tokens), bf16)] * 4
            self.scratch += [pltpu.VMEM(weight.shape, bf16), pltpu.VMEM((4, hd, tokens), bf16)]
            self.peers = TP_PEERS + CTX_PEERS

    def steps(self, ins, outs, scratch):
        keep, send, cot = ins[:3]
        full_out, exact_out = outs[:2]
        mine, from_core, from_x, grads, full, exact = scratch[:6]
        sems, local_sem = scratch[6:8], scratch[8]
        rows = mine.shape[0]
        half = rows // 2
        spot, z = spots()
        core = lax.rem(spot, 2)

        def rows_of(n, which):
            return pl.ds(pl.multiple_of((2 * n + which) * half, half), half)

        def core_copy():
            return remote(send, from_core, sems, 0, peer("tp", 1))

        def x_copy():
            return remote(mine, from_x, sems, 1, peer("tp", 2))

        def back_copies():
            return [
                remote(full.at[rows_of(n, core)], full.at[rows_of(n, core)], sems, 2 * n + 2, peer("tp", 1))
                for n in range(2)
            ]

        def loads():
            copies = [pltpu.make_async_copy(keep, mine, local_sem.at[0])]
            for n in range(2):
                copies.append(
                    pltpu.make_async_copy(
                        cot.at[rows_of(n, core)],
                        grads.at[n * half : (n + 1) * half],
                        local_sem.at[n + 1],
                    )
                )
            if self.heads:
                copies.append(pltpu.make_async_copy(ins[3], scratch[9], local_sem.at[5]))
            return copies

        def store_exact():
            return pltpu.make_async_copy(exact, exact_out, local_sem.at[4])

        def store_full():
            return pltpu.make_async_copy(full, full_out, local_sem.at[3])

        def begin():
            core_copy().start()
            start_all(loads())

        def add_core():
            wait_all(loads())
            core_copy().wait()

            def add(at):
                mine[at] = (mine[at].astype(f32) + from_core[at].astype(f32)).astype(bf16)

            add_rows(rows, add)
            x_copy().start()

        def add_x():
            x_copy().wait()
            step = 32
            for part in range(2):

                def add(n, carry, part=part):
                    at = pl.ds(pl.multiple_of(part * half + n * step, step), step)
                    total = mine[at].astype(f32) + from_x[at].astype(f32) + grads[at].astype(f32)
                    to = (2 * part + core) * half + n * step
                    full[pl.ds(pl.multiple_of(to, step), step)] = total.astype(bf16)

                    @pl.when(lax.div(spot, 2) == part)
                    def _():
                        exact[pl.ds(pl.multiple_of(n * step, step), step)] = total

                    return carry

                lax.fori_loop(0, half // step, add, 0)
            start_all(back_copies())
            store_exact().start()

        def swaps():
            parts = scratch[10]
            return [
                remote(parts.at[xor4(z, s)], outs[2 + s], sems, 4 + s, peer("ctx", s))
                for s in (1, 2, 3)
            ]

        def local_head():
            return pltpu.make_async_copy(scratch[10].at[z], outs[2], local_sem.at[6])

        def spread_heads():
            wait_all(back_copies())
            store_full().start()
            if self.heads:
                weight, parts = scratch[9], scratch[10]
                tokens = full.shape[1]
                step = 256
                for n in range(tokens // step):
                    at = slice(n * step, (n + 1) * step)
                    product = mm(weight[...], full[:, at]).astype(bf16)
                    parts[:, :, at] = product.reshape(parts.shape[0], parts.shape[1], step)
                start_all(swaps() + [local_head()])

        def end():
            wait_all([store_exact(), store_full()])
            if self.heads:
                wait_all(swaps() + [local_head()])

        return zip(self.points, (begin, add_core, add_x, spread_heads, end))


class ReduceShare:
    peers = TP_PEERS

    def __init__(self, keep, send, points):
        self.ins, self.points = (keep, send), points
        rows, tokens = keep.shape
        self.out_shape = [((rows // 2, tokens), f32)]
        self.scratch = [pltpu.VMEM(keep.shape, bf16)] * 2 + [
            pltpu.VMEM((rows // 2, tokens), bf16),
            pltpu.VMEM((rows // 2, tokens), f32),
            dma(2),
            dma(2),
            dma(2),
        ]

    def steps(self, ins, outs, scratch):
        keep, send = ins
        mine, from_core, from_x, exact = scratch[:4]
        sems, local_sem = scratch[4:6], scratch[6]
        half = exact.shape[0]
        spot, _ = spots()
        first = lax.div(spot, 2) * half
        second = half - first

        def core_copy():
            return remote(send, from_core, sems, 0, peer("tp", 1))

        def x_copy():
            source = mine.at[pl.ds(pl.multiple_of(second, half), half)]
            return remote(source, from_x, sems, 1, peer("tp", 2))

        def load():
            return pltpu.make_async_copy(keep, mine, local_sem.at[0])

        def store():
            return pltpu.make_async_copy(exact, outs[0], local_sem.at[1])

        def add_core():
            load().wait()
            core_copy().wait()

            def add(at):
                mine[at] = (mine[at].astype(f32) + from_core[at].astype(f32)).astype(bf16)

            add_rows(2 * half, add)
            x_copy().start()

        def add_x():
            x_copy().wait()

            def add(n, carry):
                at = pl.ds(pl.multiple_of(n * 16, 16), 16)
                own = pl.ds(pl.multiple_of(first + n * 16, 16), 16)
                exact[at] = mine[own].astype(f32) + from_x[at].astype(f32)
                return carry

            lax.fori_loop(0, half // 16, add, 0)
            store().start()

        return zip(
            self.points,
            (
                lambda: start_all([core_copy(), load()]),
                add_core,
                add_x,
                lambda: store().wait(),
            ),
        )


class GradsY:
    peers = Y_PEERS

    def __init__(self, total, points):
        self.ins, self.points = (total,), points
        half = (total.shape[0] // 2, total.shape[1])
        self.out_shape = [(half, bf16)]
        self.scratch = [pltpu.VMEM(half, bf16)] * 2 + [dma(1), dma(1), dma(2)]

    def steps(self, ins, outs, scratch):
        (total,) = ins
        mine, got = scratch[:2]
        sems, local_sem = scratch[2:4], scratch[4]
        half = mine.shape[0]

        def across():
            return remote(total.at[half:], got, sems, 0, peer("fsdp", 1))

        def load():
            return pltpu.make_async_copy(total.at[:half], mine, local_sem.at[0])

        def store():
            return pltpu.make_async_copy(mine, outs[0], local_sem.at[1])

        def add_y():
            load().wait()
            across().wait()

            def add(at):
                mine[at] = (mine[at].astype(f32) + got[at].astype(f32)).astype(bf16)

            add_rows(half, add)
            store().start()

        return zip(
            self.points,
            (lambda: start_all([across(), load()]), add_y, lambda: store().wait()),
        )


class GradsZ:
    peers = (("ctx", 1), ("ctx", 2))

    def __init__(self, low, points):
        self.ins, self.points = (low,), points
        rows, cols = low.shape[0] // 4, low.shape[1]
        self.out_shape = [((rows, cols), f32)]
        self.scratch = [
            pltpu.VMEM((5, rows, cols), bf16),
            pltpu.VMEM((rows, cols), f32),
            dma(3),
            dma(3),
            dma(3),
        ]

    def steps(self, ins, outs, scratch):
        (low,) = ins
        buf, exact = scratch[:2]
        sems, local_sem = scratch[2:4], scratch[4]
        rows = exact.shape[0]
        _, z = spots()

        def chunk(s):
            return low.at[pl.ds(pl.multiple_of(xor4(z, s) * rows, 16), rows)]

        def near():
            return [
                remote(chunk(s), buf.at[2 + n], sems, n, peer("ctx", 1)) for n, s in enumerate((1, 3))
            ]

        def far():
            return remote(buf.at[1], buf.at[4], sems, 2, peer("ctx", 2))

        def loads():
            return [
                pltpu.make_async_copy(chunk(s), buf.at[n], local_sem.at[n])
                for n, s in enumerate((0, 2))
            ]

        def store():
            return pltpu.make_async_copy(exact, outs[0], local_sem.at[2])

        def add_near():
            wait_all(loads() + near())

            def add(at):
                buf[1, at] = (buf[1, at].astype(f32) + buf[3, at].astype(f32)).astype(bf16)

            add_rows(rows, add)
            far().start()

        def add_far():
            far().wait()

            def add(at):
                exact[at] = (buf[0, at].astype(f32) + buf[2, at].astype(f32)) + buf[4, at].astype(f32)

            add_rows(rows, add)
            store().start()

        return zip(
            self.points,
            (lambda: start_all(near() + loads()), add_near, add_far, lambda: store().wait()),
        )


class GradsZThenY:
    peers = (("ctx", 1), ("ctx", 2)) + Y_PEERS

    def __init__(self, total, points):
        self.ins, self.points = (total,), points
        rows, cols = total.shape[0] // 8, total.shape[1]
        self.out_shape = [((rows, cols), f32)]
        self.scratch = [
            pltpu.VMEM((2, 5, rows, cols), bf16),
            pltpu.VMEM((rows, cols), bf16),
            pltpu.VMEM((rows, cols), f32),
            dma(7),
            dma(7),
            dma(5),
        ]

    def steps(self, ins, outs, scratch):
        (total,) = ins
        buf, from_y, exact = scratch[:3]
        sems, local_sem = scratch[3:5], scratch[5]
        rows = exact.shape[0]
        _, z = spots()

        def chunk(n, s):
            return total.at[pl.ds(pl.multiple_of((4 * n + xor4(z, s)) * rows, 16), rows)]

        def near(n):
            return [
                remote(chunk(n, s), buf.at[n, 2 + k], sems, 2 * n + k, peer("ctx", 1))
                for k, s in enumerate((1, 3))
            ]

        def far(n):
            return remote(buf.at[n, 1], buf.at[n, 4], sems, 4 + n, peer("ctx", 2))

        def to_y():
            return remote(buf.at[1, 0], from_y, sems, 6, peer("fsdp", 1))

        def loads():
            return [
                pltpu.make_async_copy(chunk(n, s), buf.at[n, k], local_sem.at[2 * n + k])
                for n in range(2)
                for k, s in enumerate((0, 2))
            ]

        def store():
            return pltpu.make_async_copy(exact, outs[0], local_sem.at[4])

        def begin():
            start_all(near(1) + loads())

        def add_near(n):
            wait_all(near(n))

            def add(at):
                buf[n, 1, at] = (buf[n, 1, at].astype(f32) + buf[n, 3, at].astype(f32)).astype(bf16)

            add_rows(rows, add)
            far(n).start()

        def summed(n, at):
            return (buf[n, 0, at].astype(f32) + buf[n, 2, at].astype(f32)) + buf[n, 4, at].astype(f32)

        def second():
            wait_all(loads())
            add_near(1)
            start_all(near(0))

        def third():
            add_near(0)
            far(1).wait()

            def add(at):
                buf[1, 0, at] = summed(1, at).astype(bf16)

            add_rows(rows, add)
            to_y().start()

        def end():
            to_y().wait()
            far(0).wait()

            def add(at):
                exact[at] = summed(0, at) + from_y[at].astype(f32)

            add_rows(rows, add)
            store().start()
            store().wait()

        return zip(self.points, (begin, second, third, end))


def take(refs, count):
    return refs[:count], refs[count:]


def run_step(steps, index, last=None):
    for point, step in steps.items():
        if point != "end":
            pl.when(index == point)(step)
    if last is not None and "end" in steps:
        pl.when(last)(steps["end"])


def assemble(place, pieces, full):
    count = len(pieces)
    share = pieces[0].shape[-2]
    for mine in range(count):

        @pl.when(place == mine)
        def _(mine=mine):
            for a in range(count):
                piece = pieces[a ^ mine]
                value = piece[0] if len(piece.shape) == 3 else piece[...]
                full[a * share : (a + 1) * share, :] = value


def spread(parts, place, keep_ref, send_ref):
    core = lax.rem(place, 2)
    share = parts.shape[1]
    for n in range(2):
        keep_ref[n * share : (n + 1) * share] = parts[2 * n + core]
        send_ref[n * share : (n + 1) * share] = parts[2 * n + 1 - core]


def over_rows_of(count, body, init, unroll=2):
    def advance(n, carry):
        return body(pl.ds(pl.multiple_of(n * ROWS, ROWS), ROWS), carry)

    return lax.fori_loop(0, count // ROWS, advance, init, unroll=unroll)


def fold8(value):
    return jnp.sum(value.reshape(value.shape[0] // 8, 8, value.shape[1]), axis=0)


def wide(value, lanes):
    return jnp.concatenate([value] * (lanes // 128), axis=1)


def moments(full):
    rows, lanes = full.shape
    zero = jnp.zeros((8, lanes), f32)
    total = over_rows_of(rows, lambda at, c: c + fold8(full[at].astype(f32)), zero)
    mean = jnp.sum(total, axis=0, keepdims=True) * (1.0 / rows)

    def square(at, c):
        center = full[at].astype(f32) - mean
        return c + fold8(center * center)

    total = over_rows_of(rows, square, zero)
    var = jnp.sum(total, axis=0, keepdims=True) * (1.0 / rows)
    return mean, lax.rsqrt(var + epsilon)


def normalize(full, act, gain, shift):
    mean, inv_std = moments(full)
    lanes = full.shape[1]

    def write(at, carry):
        normed = (full[at].astype(f32) - mean) * inv_std
        act[at] = (normed * wide(gain[at], lanes) + wide(shift[at], lanes)).astype(bf16)
        return carry

    over_rows_of(full.shape[0], write, 0)
    return mean, inv_std


def lane_sums(value):
    total = value[:, 0:128]
    for n in range(1, value.shape[1] // 128):
        total += value[:, n * 128 : (n + 1) * 128]
    return total


CHUNK = 256
SUB = 32


def subs(first):
    for r in range(CHUNK // SUB):
        yield slice(r * SUB, (r + 1) * SUB), slice(first + r * SUB, first + (r + 1) * SUB)


def gather_chunk(state, up_all, first, full, mean, inv_std, gain, sums, upstream):
    plain, mixed = state
    lanes = up_all.shape[1]
    for part, to in subs(first):
        up = up_all[part]
        upstream[to] = up
        both = up * ((full[to].astype(f32) - mean) * inv_std)
        g = wide(gain[to], lanes)
        sums[0, to] += lane_sums(both)
        sums[1, to] += lane_sums(up)
        plain += fold8(up * g)
        mixed += fold8(both * g)
    return plain, mixed


def finish_stats(state, width):
    plain, mixed = state
    scale = 1.0 / width
    return (
        jnp.sum(plain, axis=0, keepdims=True) * scale,
        jnp.sum(mixed, axis=0, keepdims=True) * scale,
    )


def write_chunk(parts, first, upstream, full, mean, inv_std, gain, stats):
    plain, mixed = stats
    share = parts.shape[1]
    lanes = upstream.shape[1]
    for _, to in subs(first):
        normed = (full[to].astype(f32) - mean) * inv_std
        result = (upstream[to] * wide(gain[to], lanes) - plain - normed * mixed) * inv_std
        at = to.start % share
        parts[to.start // share, at : at + SUB] = result.astype(bf16)


def normalize_chunk(full, act, first, mean, inv_std, gain, shift):
    lanes = full.shape[1]
    for _, to in subs(first):
        normed = (full[to].astype(f32) - mean) * inv_std
        act[to] = (normed * wide(gain[to], lanes) + wide(shift[to], lanes)).astype(bf16)


def spread_rows(value, parts, first):
    share = parts.shape[1]
    for part, to in subs(first):
        at = to.start % share
        parts[to.start // share, at : at + SUB] = value[part].astype(bf16)


def whole_spec(shape):
    return pl.BlockSpec(shape, lambda *_: (0,) * len(shape))


def cols_spec(height, block):
    return pl.BlockSpec((height, block), lambda i, *_: (0, i))


def image_spec(image, height, block):
    return pl.BlockSpec((1, height, block), lambda i, *_: (image, 0, i))


def fixed_spec(shape):
    return pl.BlockSpec(shape, lambda *_: (0,) * len(shape), pipeline_mode=pl.Buffered(1))


def call(body, grid, in_specs, out_specs, out_shape, scratch, name, args, back=Quiet(), vmem=48):
    count = len(out_shape)

    def kernel(*refs):
        ins, refs = take(refs, len(args))
        back_ins, refs = take(refs, len(back.ins))
        outs, refs = take(refs, count)
        back_outs, refs = take(refs, len(back.out_shape))
        own, back_scratch = take(refs, len(scratch))
        body(back.steps(back_ins, back_outs, back_scratch), *ins, *outs, *own)

    shapes = list(out_shape) + list(back.out_shape)
    params = dict(vmem_limit_bytes=vmem << 20)
    if back.ident is not None:
        params.update(collective_id=back.ident, has_side_effects=True)
    out = pl.pallas_call(
        kernel,
        grid=grid,
        in_specs=list(in_specs) + [ANY] * len(back.ins),
        out_specs=list(out_specs) + [ANY] * len(back.out_shape),
        scratch_shapes=list(scratch) + list(back.scratch),
        out_shape=[jax.ShapeDtypeStruct(s, d) for s, d in shapes],
        compiler_params=pltpu.CompilerParams(**params),
        cost_estimate=pl.CostEstimate(flops=1 << 20, bytes_accessed=1 << 16, transcendentals=0),
        name=name,
    )(*args, *back.ins)
    return out if back.ident is None else (out[:count], back.split(out[count:]))


def qkv_kernel(steps, *refs):
    run_step(steps, pl.program_id(0))
    pieces, (gain, shift, own, other), (full, act), outs, mixed = (
        refs[:4],
        refs[4:8],
        refs[8:10],
        refs[10:14],
        refs[14],
    )
    spot, z = spots()
    assemble(spot, pieces, full)
    normalize(full, act, gain, shift)
    half = own.shape[1]
    product = mm(own[...], act[0:half]) + mm(other[...], act[half:])
    mixed[...] = product.astype(bf16).reshape(mixed.shape)
    rows = mixed.shape[1]
    for s in range(4):
        head = xor4(z, s)
        for k, part in enumerate((1, 2, 0)):
            outs[s][k * rows : (k + 1) * rows] = mixed[part * 4 + head]
    pl.when(pl.program_id(0) == pl.num_programs(0) - 1)(steps.get("end", lambda: None))


def qkv_call(pieces, gain, shift, own, other, hd, back, name):
    share, tokens = pieces[0].shape
    width = gain.shape[0]
    total = own.shape[0]
    block = 256
    return call(
        qkv_kernel,
        (tokens // block,),
        [cols_spec(share, block)] * 4 + [fixed_spec(gain.shape)] * 2 + [fixed_spec(own.shape)] * 2,
        [cols_spec(width, block)] * 2 + [cols_spec(3 * hd, block)] * 4,
        [((width, tokens), bf16)] * 2 + [((3 * hd, tokens), bf16)] * 4,
        [pltpu.VMEM((total // hd, hd, block), bf16)],
        name,
        (*pieces, gain, shift, own, other),
        back,
        vmem=24,
    )


def mlp_kernel(steps, heads, full, cots, *refs):
    gain, shift, proj, up, down = refs[:5]
    act2, cot, hidden, grad_pre, keep_f, send_f, keep_b, send_b, sums, mid_own, joined = refs[5:16]
    mixed, mid, upstream, parts, parts_f = refs[16:21]
    step_at = pl.program_id(0)
    run_step(steps, step_at)
    spot, z = spots()
    for r in range(4):
        for s in range(4):
            mixed[r, xor4(z, s)] = heads[r, s]
    joined[...] = mixed[0].reshape(joined.shape)
    assemble(spot, [cots.at[r, 0] for r in range(4)], cot)
    width, lanes = mid.shape
    hid = hidden.shape[0]
    attn = mixed[...].reshape(width, lanes)
    zero = jnp.zeros((8, lanes), f32)

    @pl.when(step_at == 0)
    def _():
        sums[...] = jnp.zeros_like(sums)

    total = zero
    for first in range(0, width, CHUNK):
        product = mm(proj[:, first : first + CHUNK], attn, TN)
        for part, to in subs(first):
            value = product[part] + full[to].astype(f32)
            mid[to] = value
            total += fold8(value)
    mean = jnp.sum(total, axis=0, keepdims=True) * (1.0 / width)
    share = mid_own.shape[0]
    mid_own[...] = mid[pl.ds(pl.multiple_of(spot * share, share), share)]
    total = zero
    for first in range(0, width, SUB):
        center = mid[first : first + SUB] - mean
        total += fold8(center * center)
    inv_std = lax.rsqrt(jnp.sum(total, axis=0, keepdims=True) * (1.0 / width) + epsilon)
    for first in range(0, width, CHUNK):
        upstream[first : first + CHUNK] = mm(down[first : first + CHUNK], cot[...])
        normalize_chunk(mid, act2, first, mean, inv_std, gain, shift)
    for first in range(0, hid, CHUNK):
        pre_all = mm(up[:, first : first + CHUNK], act2[...], TN)
        for part, to in subs(first):
            pre = pre_all[part]
            cdf, density = gelu_parts(pre)
            hidden[to] = (pre * cdf).astype(bf16)
            grad_pre[to] = (upstream[to] * (cdf + pre * density)).astype(bf16)
    state = (zero, zero)
    for first in range(0, width, CHUNK):
        up_all = mm(up[first : first + CHUNK], grad_pre[...])
        state = gather_chunk(state, up_all, first, mid, mean, inv_std, gain, sums, upstream)
    stats = finish_stats(state, width)
    for first in range(0, width, CHUNK):
        spread_rows(mm(down[:, first : first + CHUNK], hidden[...], TN), parts_f, first)
        write_chunk(parts, first, upstream, mid, mean, inv_std, gain, stats)
    spread(parts_f, spot, keep_f, send_f)
    spread(parts, spot, keep_b, send_b)
    pl.when(step_at == pl.num_programs(0) - 1)(steps.get("end", lambda: None))


def mlp_call(image, heads, full, cots, gain, shift, proj, up, down, back):
    width, tokens = full.shape
    hid = up.shape[1]
    share = width // 4
    hd = heads.shape[2]
    block = 256
    half = width // 2
    return call(
        mlp_kernel,
        (tokens // block,),
        [
            pl.BlockSpec((4, 4, hd, block), lambda i: (0, 0, 0, i)),
            cols_spec(width, block),
        ]
        + [pl.BlockSpec((4, 1, share, block), lambda i: (0, image, 0, i))]
        + [fixed_spec(gain.shape)] * 2
        + [fixed_spec(proj.shape), fixed_spec(up.shape), fixed_spec(down.shape)],
        [cols_spec(width, block)] * 2
        + [cols_spec(hid, block)] * 2
        + [cols_spec(half, block)] * 4
        + [whole_spec((2, width, 128)), cols_spec(share, block), cols_spec(4 * hd, block)],
        [((width, tokens), bf16)] * 2
        + [((hid, tokens), bf16)] * 2
        + [((half, tokens), bf16)] * 4
        + [((2, width, 128), f32), ((share, tokens), f32), ((4 * hd, tokens), bf16)],
        [
            pltpu.VMEM((4, 4, hd, block), bf16),
            pltpu.VMEM((width, block), f32),
            pltpu.VMEM((width, block), f32),
            pltpu.VMEM((4, share, block), bf16),
            pltpu.VMEM((4, share, block), bf16),
        ],
        "mlp%d" % image,
        (heads, full, cots, gain, shift, proj, up, down),
        back,
    )


def gattn_kernel(_, full, weight, *refs):
    outs, mixed = refs[:4], refs[4]
    _, z = spots()
    mixed[...] = mm(weight[...], full[...]).astype(bf16).reshape(mixed.shape)
    for s in range(4):
        outs[s][...] = mixed[xor4(z, s)]


def gattn_call(full, weight, hd):
    width, tokens = full.shape
    total = weight.shape[0]
    block = 256
    return call(
        gattn_kernel,
        (tokens // block,),
        [cols_spec(width, block), fixed_spec(weight.shape)],
        [cols_spec(hd, block)] * 4,
        [((hd, tokens), bf16)] * 4,
        [pltpu.VMEM((total // hd, hd, block), bf16)],
        "gattn",
        (full, weight),
        vmem=20,
    )


def gin_block(joined, full, gain, own, other, sums, upstream, parts):
    half = own.shape[1]
    width, lanes = full.shape
    mean, inv_std = moments(full)
    zero = jnp.zeros((8, lanes), f32)
    state = (zero, zero)
    step = 128
    for first in range(0, width, CHUNK):
        ups = []
        for n in range(first, first + CHUNK, step):
            weight = own if n < half else other
            ups.append(mm(weight[:, n % half : n % half + step], joined, TN))
        up_all = jnp.concatenate(ups, axis=0)
        state = gather_chunk(state, up_all, first, full, mean, inv_std, gain, sums, upstream)
    stats = finish_stats(state, width)
    for first in range(0, width, CHUNK):
        write_chunk(parts, first, upstream, full, mean, inv_std, gain, stats)


def tail_kernel(_, *refs):
    pieces, (full_0, act_0, gain, own, other, small_in), refs = refs[:4], refs[4:10], refs[10:]
    sends, (full_any, act_any, proj_any), refs = refs[:4], refs[4:7], refs[7:]
    (out_0, out_1, out_w, out_small, out_p), refs = refs[:5], refs[5:]
    (mixed, got, full_1, act_1, total, low, upstream, parts, block, sums), refs = refs[:10], refs[10:]
    (keep, send, from_core, from_x, exact, from_y, from_z, exact_w, small, hops), refs = (
        refs[:10],
        refs[10:],
    )
    (mine_p, got_p, from_p, exact_p), refs = refs[:4], refs[4:]
    send_sem, recv_sem, local_sem = refs
    sems = (send_sem, recv_sem)
    spot, z = spots()
    core = lax.rem(spot, 2)
    tokens = mixed.shape[2]
    rows = mixed.shape[1]
    width = full_0.shape[0]
    half = width // 2
    share = half // 2
    lanes = block.shape[1]
    chunk = half // 4

    greet([peer(*p) for p in CTX_PEERS + TP_PEERS + Y_PEERS])

    def swaps():
        return [remote(sends[s], got.at[s], sems, s - 1, peer("ctx", s)) for s in (3, 2, 1)]

    def loads():
        return [
            pltpu.make_async_copy(sends[0], got.at[0], local_sem.at[0]),
            pltpu.make_async_copy(full_any, full_1, local_sem.at[1]),
            pltpu.make_async_copy(act_any, act_1, local_sem.at[2]),
        ]

    def proj_y():
        return remote(proj_any.at[half:], got_p, sems, 19, peer("fsdp", 1))

    def proj_load():
        return pltpu.make_async_copy(proj_any.at[:half], mine_p, local_sem.at[7])

    def proj_z(s):
        source = mine_p.at[pl.ds(pl.multiple_of(xor4(z, s) * chunk, 16), chunk)]
        return remote(source, from_p.at[s], sems, 19 + s, peer("ctx", s))

    start_all(swaps() + loads() + [proj_y(), proj_load()])
    sums[...] = jnp.zeros_like(sums)

    def join(source):
        for s in range(4):
            head = xor4(z, s)
            for k, part in enumerate((1, 2, 0)):
                mixed[part * 4 + head] = source(s)[k * rows : (k + 1) * rows]

    def all_blocks(full, image):
        def advance(b, carry):
            at = pl.ds(pl.multiple_of(b * lanes, lanes), lanes)
            block[...] = full[:, at]
            joined = mixed[:, :, at].reshape(mixed.shape[0] * rows, lanes)
            gin_block(joined, block, gain, own, other, sums, upstream, parts)
            for n in range(2):
                to = slice(n * share, (n + 1) * share)
                keep[image, to, at] = parts[2 * n + core]
                send[image, to, at] = parts[2 * n + 1 - core]
            return carry

        lax.fori_loop(0, tokens // lanes, advance, 0)

    def core_copy(image):
        return remote(send.at[image], from_core.at[image], sems, 3 + image, peer("tp", 1))

    first = lax.div(spot, 2) * share
    second = share - first

    def x_copy(image):
        source = keep.at[image, pl.ds(pl.multiple_of(second, share), share)]
        return remote(source, from_x.at[image], sems, 5 + image, peer("tp", 2))

    def add_core(image):
        core_copy(image).wait()

        def add(at):
            keep[image, at] = (
                keep[image, at].astype(f32) + from_core[image, at].astype(f32)
            ).astype(bf16)

        add_rows(half, add)
        x_copy(image).start()

    def add_x(image):
        x_copy(image).wait()

        def add(n, carry):
            at = pl.ds(pl.multiple_of(n * 16, 16), 16)
            mine = pl.ds(pl.multiple_of(first + n * 16, 16), 16)
            exact[image, at] = keep[image, mine].astype(f32) + from_x[image, at].astype(f32)
            return carry

        lax.fori_loop(0, share // 16, add, 0)

    def out_copy(image, out):
        return pltpu.make_async_copy(exact.at[image], out, local_sem.at[3 + image])

    def y_copy(s):
        place = pl.multiple_of(half + xor4(z, s) * chunk, 16)
        return remote(low.at[pl.ds(place, chunk)], from_y.at[s], sems, 7 + s, peer("fsdp", 1))

    def z_copy(s):
        return remote(from_y.at[s], from_z.at[s], sems, 10 + s, peer("ctx", s))

    def product(act, at):
        return mm(act[at], mixed[...].reshape(mixed.shape[0] * rows, tokens), NT)

    step = 128

    def weight_first(n, carry):
        at = pl.ds(pl.multiple_of(n * step, step), step)
        total[at] = product(act_0, at)
        return carry

    def weight_second(n, carry):
        at = pl.ds(pl.multiple_of(n * step, step), step)
        low[at] = (total[at] + product(act_1, at)).astype(bf16)
        return carry

    join(lambda s: pieces[s])
    all_blocks(full_0, 0)
    core_copy(0).start()
    lax.fori_loop(0, width // step, weight_first, 0)
    add_core(0)
    wait_all([proj_load(), proj_y()])

    def add_p(at):
        mine_p[at] = (mine_p[at].astype(f32) + got_p[at].astype(f32)).astype(bf16)

    add_rows(half, add_p)
    wait_all(swaps() + loads())
    start_all([proj_z(s) for s in (3, 2, 1)])
    join(lambda s: got.at[s])
    lax.fori_loop(half // step, width // step, weight_second, 0)
    start_all([y_copy(s) for s in (3, 2, 1, 0)])
    lax.fori_loop(0, half // step, weight_second, 0)
    add_x(0)
    out_copy(0, out_0).start()
    all_blocks(full_1, 1)
    core_copy(1).start()
    small[0:288] = small_in[...]
    y = lax.axis_index("fsdp")
    for n in range(2):
        line = jnp.sum(jnp.transpose(sums[n]), axis=0, keepdims=True)
        line = jnp.where(y == 0, line, jnp.concatenate([line[:, half:], line[:, :half]], axis=1))
        for k in range(width // 128):
            small[288 + n * 16 + k : 289 + n * 16 + k] = line[:, k * 128 : (k + 1) * 128]
    def hop(k, axis, bit):
        return remote(small, hops.at[k], sems, 14 + k, peer(axis, bit))

    for k, (axis, bit) in enumerate(TP_PEERS + CTX_PEERS[:2]):
        hop(k, axis, bit).start()
        hop(k, axis, bit).wait()
        small[...] += hops[k]
        if k == 1:
            add_core(1)
    hop(4, *Y_PEERS[0]).start()
    for s in (3, 2, 1):
        y_copy(s).wait()

        def add(at, s=s):
            mine = low[pl.ds(pl.multiple_of(xor4(z, s) * chunk + at.start, 16), at.size)]
            from_y[s, at] = (from_y[s, at].astype(f32) + mine.astype(f32)).astype(bf16)

        add_rows(chunk, add)
        z_copy(s).start()
    hop(4, *Y_PEERS[0]).wait()
    small[...] += hops[4]
    wait_all([proj_z(s) for s in (3, 2, 1)])

    def last_p(at):
        mine = mine_p[pl.ds(pl.multiple_of(z * chunk + at.start, 16), at.size)].astype(f32)
        exact_p[at] = (mine + from_p[1, at].astype(f32)) + (
            from_p[2, at].astype(f32) + from_p[3, at].astype(f32)
        )

    add_rows(chunk, last_p)
    add_x(1)
    out_copy(1, out_1).start()
    y_copy(0).wait()
    wait_all([z_copy(s) for s in (3, 2, 1)])

    def add_last(at):
        mine = low[pl.ds(pl.multiple_of(z * chunk + at.start, 16), at.size)].astype(f32)
        exact_w[at] = ((mine + from_y[0, at].astype(f32)) + from_z[1, at].astype(f32)) + (
            from_z[2, at].astype(f32) + from_z[3, at].astype(f32)
        )

    add_rows(chunk, add_last)
    lasts = [
        pltpu.make_async_copy(exact_w, out_w, local_sem.at[5]),
        pltpu.make_async_copy(small, out_small, local_sem.at[6]),
        pltpu.make_async_copy(exact_p, out_p, local_sem.at[8]),
    ]
    start_all(lasts)
    wait_all(lasts + [out_copy(0, out_0), out_copy(1, out_1)])


def tail_call(pieces, full_0, act_0, gain, own, other, small, sends, full_1, act_1, proj, hd, ident):
    part_rows, tokens = pieces[0].shape
    width = gain.shape[0]
    total = own.shape[0]
    half = width // 2
    share = half // 2
    block = 256
    ins = (*pieces, full_0, act_0, gain, own, other, small)
    anys = (*sends, full_1, act_1, proj)
    cols = proj.shape[1]
    scratch = [
        pltpu.VMEM((total // hd, hd, tokens), bf16),
        pltpu.VMEM((4, part_rows, tokens), bf16),
        pltpu.VMEM((width, tokens), bf16),
        pltpu.VMEM((width, tokens), bf16),
        pltpu.VMEM((width, total), f32),
        pltpu.VMEM((width, total), bf16),
        pltpu.VMEM((width, block), f32),
        pltpu.VMEM((4, share, block), bf16),
        pltpu.VMEM((width, block), bf16),
        pltpu.VMEM((2, width, 128), f32),
        pltpu.VMEM((2, half, tokens), bf16),
        pltpu.VMEM((2, half, tokens), bf16),
        pltpu.VMEM((2, half, tokens), bf16),
        pltpu.VMEM((2, share, tokens), bf16),
        pltpu.VMEM((2, share, tokens), f32),
        pltpu.VMEM((4, half // 4, total), bf16),
        pltpu.VMEM((4, half // 4, total), bf16),
        pltpu.VMEM((half // 4, total), f32),
        pltpu.VMEM((320, 128), f32),
        pltpu.VMEM((5, 320, 128), f32),
        pltpu.VMEM((half, cols), bf16),
        pltpu.VMEM((half, cols), bf16),
        pltpu.VMEM((4, half // 4, cols), bf16),
        pltpu.VMEM((half // 4, cols), f32),
        dma(23),
        dma(23),
        dma(9),
    ]
    return pl.pallas_call(
        functools.partial(tail_kernel, None),
        in_specs=[pl.BlockSpec(memory_space=pltpu.VMEM)] * len(ins) + [ANY] * len(anys),
        out_specs=[ANY] * 5,
        scratch_shapes=scratch,
        out_shape=[
            jax.ShapeDtypeStruct((share, tokens), f32),
            jax.ShapeDtypeStruct((share, tokens), f32),
            jax.ShapeDtypeStruct((half // 4, total), f32),
            jax.ShapeDtypeStruct((320, 128), f32),
            jax.ShapeDtypeStruct((half // 4, cols), f32),
        ],
        compiler_params=pltpu.CompilerParams(
            vmem_limit_bytes=60 << 20, collective_id=ident, has_side_effects=True
        ),
        cost_estimate=pl.CostEstimate(flops=1 << 20, bytes_accessed=1 << 16, transcendentals=0),
        name="tail",
    )(*ins, *anys)


def band_start(place, chunk, size, band):
    return xor4(place, lax.div(chunk * size, band)) * band + lax.rem(chunk * size, band)


def fwd_kernel(dims, steps, *refs):
    hd, side, scale = dims
    _, place = spots()
    pieces, table = refs[:4], refs[4]
    outs, kvq, exact, lse, qa = refs[5:9], refs[9], refs[10], refs[11], refs[12]
    ka, va, low = refs[13:16]
    band = pieces[0].shape[1]
    seq = kvq.shape[1]
    step = 512
    bq, bk = band, 1024
    for s in range(4):
        kvq[:, s * band : (s + 1) * band] = pieces[s][...]
    lane = lax.broadcasted_iota(jnp.int32, (step, 128), 1)
    row = lax.broadcasted_iota(jnp.int32, (step, 128), 0)
    lane_side = lax.broadcasted_iota(jnp.int32, (side, 128), 1)
    row16 = lax.broadcasted_iota(jnp.int32, (16, step), 0)
    pad = jnp.zeros((128 - hd, step), bf16)

    def prepare(c, carry):
        at = pl.ds(pl.multiple_of(c * step, step), step)
        start = band_start(place, c, step, band)
        keys = jnp.transpose(jnp.concatenate([kvq[0:hd, at], pad], axis=0).astype(f32))
        ka[at, 0:128] = keys.astype(bf16)
        pos = row + start
        want = jnp.where(lane < side, lax.div(pos, side), lax.rem(pos, side) + side)
        ka[at, 128:256] = jnp.where(want == lane, 1.0, 0.0).astype(bf16)
        va[0:hd, at] = kvq[hd : 2 * hd, at]
        va[hd : hd + 16, at] = jnp.where(row16 == 0, 1.0, 0.0).astype(bf16)
        queries = jnp.concatenate([kvq[2 * hd : 3 * hd, at], pad], axis=0)
        qa[0:128, at] = (queries.astype(f32) * (scale * LOG2E)).astype(bf16)
        terms = lax.dot_general(queries, table[...], (((0,), (1,)), ((), ())), preferred_element_type=f32)
        parts = []
        for r in range(step // side):
            y = lax.div(start, side) + r
            by_row = terms[r * side : (r + 1) * side, 0:128]
            by_col = terms[r * side : (r + 1) * side, 128:256]
            by_row = pltpu.roll(by_row, lax.rem(side + 1 + y, 128), 1)
            by_col = pltpu.roll(by_col, 1, 1, stride=1, stride_axis=0)
            parts.append(jnp.where(lane_side < side, by_row, by_col))
        rel = jnp.concatenate(parts, axis=0) * LOG2E
        qa[128:256, at] = jnp.transpose(rel).astype(bf16)
        return carry

    lax.fori_loop(0, seq // step, prepare, 0)

    def queries_loop(i, carry):
        at = pl.ds(pl.multiple_of(i * bq, bq), bq)
        q_block = qa[:, at]

        def keys_loop(j, state):
            peak, total = state
            run_step(steps, i * (seq // bk) + j)
            keys = pl.ds(pl.multiple_of(j * bk, bk), bk)
            logits = mm(ka[keys, :], q_block)
            new_peak = jnp.maximum(peak, jnp.max(logits, axis=0, keepdims=True))
            weights = jnp.exp2(logits - new_peak).astype(bf16)
            total = total * jnp.exp2(peak - new_peak) + mm(va[:, keys], weights)
            return new_peak, total

        peak, total = lax.fori_loop(
            0,
            seq // bk,
            keys_loop,
            (jnp.full((1, bq), lowest, f32), jnp.zeros((hd + 16, bq), f32)),
        )
        denom = total[hd : hd + 1]
        value = total[0:hd] / denom
        exact[:, at] = value
        low[:, at] = value.astype(bf16)
        lse[:, at] = jnp.broadcast_to(peak + jnp.log2(denom), (8, bq))
        return carry

    lax.fori_loop(0, seq // bq, queries_loop, 0)
    for s in range(4):
        outs[s][...] = low[:, s * band : (s + 1) * band]
    steps.get("end", lambda: None)()


def fwd_call(pieces, table, hd, side, back, name):
    rows, band = pieces[0].shape
    seq = 4 * band
    return call(
        functools.partial(fwd_kernel, (hd, side, hd ** (-0.5))),
        (1,),
        [fixed_spec((rows, band))] * 4 + [fixed_spec(table.shape)],
        [fixed_spec((hd, band))] * 4
        + [fixed_spec((rows, seq)), fixed_spec((hd, seq)), fixed_spec((8, seq)), fixed_spec((256, seq))],
        [((hd, band), bf16)] * 4
        + [((rows, seq), bf16), ((hd, seq), f32), ((8, seq), f32), ((256, seq), bf16)],
        [
            pltpu.VMEM((seq, 256), bf16),
            pltpu.VMEM((hd + 16, seq), bf16),
            pltpu.VMEM((hd, seq), bf16),
        ],
        name,
        (*pieces, table),
        back,
        vmem=36,
    )


def split3(value):
    high = value.astype(bf16).astype(f32)
    rest = value - high
    mid = rest.astype(bf16).astype(f32)
    return high, mid, rest - mid


def bwd_kernel(dims, steps, *refs):
    hd, side, scale = dims
    _, place = spots()
    grads, kvq, qa_in, exact, lse, table = refs[:4], refs[4], refs[5], refs[6], refs[7], refs[8]
    outs, dtab = refs[9:13], refs[13]
    ka, kt, va, qa, da, qn, dn, dk, dv, res = refs[14:24]
    band = grads[0].shape[1]
    seq = kvq.shape[1]
    step = 512
    bq, bk = band, 1024
    for s in range(4):
        da[0:hd, s * band : (s + 1) * band] = grads[s][...]
    lane = lax.broadcasted_iota(jnp.int32, (step, 128), 1)
    row = lax.broadcasted_iota(jnp.int32, (step, 128), 0)
    lane_side = lax.broadcasted_iota(jnp.int32, (side, 128), 1)
    extra = lax.broadcasted_iota(jnp.int32, (128 - hd, step), 0)
    pad = jnp.zeros((128 - hd, step), bf16)
    ones = (lane >= hd) & (lane < hd + 3)

    def turned(value):
        return jnp.transpose(jnp.concatenate([value, pad], axis=0).astype(f32))

    def special(value):
        high, mid, rest = split3(value)
        picked = jnp.where(extra == 0, high, jnp.where(extra == 1, mid, jnp.where(extra == 2, rest, 0.0)))
        return picked.astype(bf16)

    def prepare(c, carry):
        at = pl.ds(pl.multiple_of(c * step, step), step)
        start = band_start(place, c, step, band)
        k_part = kvq[0:hd, at]
        q_part = kvq[2 * hd : 3 * hd, at]
        kt[0:128, at] = jnp.concatenate([k_part, pad], axis=0)
        ka[at, 0:128] = jnp.where(ones, 1.0, turned(k_part)).astype(bf16)
        pos = row + start
        want = jnp.where(lane < side, lax.div(pos, side), lax.rem(pos, side) + side)
        ka[at, 128:256] = jnp.where(want == lane, 1.0, 0.0).astype(bf16)
        want = jnp.where(lane < side, lax.div(pos, side), 2 * side - 1 - lax.rem(pos, side))
        kt[128:256, at] = jnp.transpose(jnp.where(want == lane, 1.0, 0.0)).astype(bf16)
        va[at, :] = jnp.where(ones, 1.0, turned(kvq[hd : 2 * hd, at])).astype(bf16)
        dk[at, :] = jnp.zeros((step, 128), f32)
        dv[at, :] = jnp.zeros((step, 128), f32)
        d_part = da[0:hd, at]
        qn[at, :] = turned(q_part).astype(bf16)
        dn[at, :] = turned(d_part).astype(bf16)
        delta = jnp.sum(d_part.astype(f32) * exact[:, at], axis=0, keepdims=True)
        qa[0:hd, at] = qa_in[0:hd, at]
        qa[hd:128, at] = special(-lse[0:1, at])
        qa[128:256, at] = qa_in[128:256, at]
        da[hd:128, at] = special(-delta)
        return carry

    lax.fori_loop(0, seq // step, prepare, 0)
    dtab[...] = jnp.zeros_like(dtab)

    def queries_loop(i, carry):
        at = pl.ds(pl.multiple_of(i * bq, bq), bq)
        qa_i, da_i, qn_i, dn_i = qa[:, at], da[:, at], qn[at, :], dn[at, :]

        def keys_loop(j, total):
            run_step(steps, i * (seq // bk) + j)
            keys = pl.ds(pl.multiple_of(j * bk, bk), bk)
            probs = jnp.exp2(mm(ka[keys, :], qa_i))
            grad_logits = (probs * mm(va[keys, :], da_i)).astype(bf16)
            dv[keys, :] += mm(probs.astype(bf16), dn_i)
            dk[keys, :] += mm(grad_logits, qn_i)
            return total + mm(kt[:, keys], grad_logits)

        total = lax.fori_loop(0, seq // bk, keys_loop, jnp.zeros((256, bq), f32))
        rel = jnp.transpose(total[128:256])
        start = band_start(place, i, bq, band)
        parts = []
        for r in range(bq // side):
            y = lax.div(start, side) + r
            block = rel[r * side : (r + 1) * side]
            by_row = jnp.where(lane_side < side, block, 0.0)
            by_col = jnp.where(lane_side < side, 0.0, block)
            by_row = pltpu.roll(by_row, lax.rem(side + 127 - y, 128), 1)
            by_col = pltpu.roll(by_col, side + 1, 1, stride=1, stride_axis=0)
            parts.append(jnp.concatenate([by_row, by_col], axis=1))
        moved = jnp.concatenate(parts, axis=0).astype(bf16)
        dq = total[0:128] * scale + lax.dot_general(
            table[...], moved, (((0,), (1,)), ((), ())), preferred_element_type=f32
        )
        res[2 * hd : 3 * hd, at] = dq[0:hd].astype(bf16)
        dtab[...] += mm(moved, qn_i, TN)
        return carry

    lax.fori_loop(0, seq // bq, queries_loop, 0)

    def finish(c, carry):
        at = pl.ds(pl.multiple_of(c * step, step), step)
        res[0:hd, at] = jnp.transpose(dk[at, :] * scale)[0:hd].astype(bf16)
        res[hd : 2 * hd, at] = jnp.transpose(dv[at, :])[0:hd].astype(bf16)
        return carry

    lax.fori_loop(0, seq // step, finish, 0)
    for s in range(4):
        outs[s][...] = res[:, s * band : (s + 1) * band]
    steps.get("end", lambda: None)()


def bwd_call(grads, kvq, qa, exact, lse, table, hd, side, back, name):
    rows, seq = kvq.shape
    band = seq // 4
    return call(
        functools.partial(bwd_kernel, (hd, side, hd ** (-0.5))),
        (1,),
        [fixed_spec((hd, band))] * 4
        + [fixed_spec(a.shape) for a in (kvq, qa, exact, lse, table)],
        [fixed_spec((rows, band))] * 4 + [fixed_spec((256, 128))],
        [((rows, band), bf16)] * 4 + [((256, 128), f32)],
        [
            pltpu.VMEM((seq, 256), bf16),
            pltpu.VMEM((256, seq), bf16),
            pltpu.VMEM((seq, 128), bf16),
            pltpu.VMEM((256, seq), bf16),
            pltpu.VMEM((128, seq), bf16),
            pltpu.VMEM((seq, 128), bf16),
            pltpu.VMEM((seq, 128), bf16),
            pltpu.VMEM((seq, 128), f32),
            pltpu.VMEM((seq, 128), f32),
            pltpu.VMEM((rows, seq), bf16),
        ],
        name,
        (*grads, kvq, qa, exact, lse, table),
        back,
        vmem=60,
    )


def offset_rows(index, table):
    side = index.shape[0]
    picks = jnp.concatenate([index[::-1, 0], index[0, 1:]])
    hot = (picks[:, None] == jnp.arange(table.shape[0], dtype=jnp.int32)[None, :]).astype(f32)
    rows = jnp.dot(hot, table.astype(f32), precision=highest)
    return hot, jnp.pad(rows, ((0, 1), (0, 128 - table.shape[1]))).astype(bf16)


def fast_device(
    block_input,
    cotangent,
    norm1_gain,
    norm1_shift,
    w_qkv,
    table_rows,
    table_cols,
    w_proj,
    norm2_gain,
    norm2_shift,
    w_fc1,
    w_fc2,
    index_rows,
    index_cols,
):
    images, band_len, share = block_input.shape
    hd = table_rows.shape[1]
    side = index_rows.shape[0]
    width = norm1_gain.shape[0]
    half = width // 2
    heads = w_proj.shape[0] // hd
    t = lax.axis_index("tp")
    z = lax.axis_index("ctx")
    y = lax.axis_index("fsdp")
    spot = t ^ (2 * y)
    first = lax.div(spot, 2) == 0

    def halves(vector):
        return jnp.where(y == 0, vector, jnp.roll(vector, half, axis=-1))

    def lanes(vector):
        return jnp.broadcast_to(halves(vector)[:, None], (width, 128))

    gain1, shift1 = lanes(norm1_gain), lanes(norm1_shift)
    gain2, shift2 = lanes(norm2_gain), lanes(norm2_shift)

    tokens_in = jnp.swapaxes(block_input, 1, 2)
    grads_in = jnp.swapaxes(cotangent, 1, 2)
    own_qkv = jnp.transpose(w_qkv, (1, 2, 0)).reshape(3 * heads * hd, half)
    other_qkv = pxor(own_qkv, "fsdp", 1)
    inputs = [gather_tp(tokens_in[0])]
    for m in range(1, images):
        inputs.append(gather_tp(after(tokens_in[m], inputs[m - 1][2])))
    hot_rows, shifted_rows = offset_rows(index_rows, table_rows)
    hot_cols, shifted_cols = offset_rows(index_cols, table_cols)
    table = jnp.concatenate([shifted_rows, shifted_cols], axis=0)
    back_table = jnp.concatenate(
        [shifted_rows, jnp.zeros((1, 128), bf16), shifted_cols[:127][::-1]], axis=0
    )

    def reduce_tp(keep, send):
        got = keep.astype(f32) + pxor(send, "tp", 1).astype(f32)
        mine = jnp.where(first, got[:share], got[share:])
        other = jnp.where(first, got[share:], got[:share]).astype(bf16)
        return mine + pxor(other, "tp", 2).astype(f32)

    state = [{} for _ in range(images)]
    token = [None]

    def ordered(values):
        return values if token[0] is None else after(values, token[0])

    def do_qkv(m, back):
        st = state[m]
        pieces = ordered(tuple(inputs[m]))
        out = qkv_call(pieces, gain1, shift1, own_qkv, other_qkv, hd, back, "qkv%d" % m)
        out, extra = out if back.ident is not None else (out, ())
        st["full"], st["act1"], *st["mixed"] = out
        token[0] = st["mixed"][0]
        return extra

    def do_fwd(m, back):
        st = state[m]
        pieces = ordered(tuple(st["mixed"]))
        out, extra = fwd_call(pieces, table, hd, side, back, "attn_fwd%d" % m)
        *st["attn"], st["kvq"], st["exact"], st["lse"], st["qa"] = out
        token[0] = st["lse"]
        return extra

    def do_mlp(m, back):
        st = state[m]
        heads_all = ordered(st["heads"])
        out, extra = mlp_call(
            m, heads_all, st["full"], cots, gain2, shift2, full_proj, full_up, full_down, back
        )
        st["act2"], st["cot"], st["hidden"], st["grad_pre"] = out[:4]
        st["forward"], st["backward"] = out[4:6], out[6:8]
        st["sums2"], st["middle"], st["joined"] = out[8:]
        token[0] = out[8]
        return extra

    def do_gattn(m):
        st = state[m]
        branch = ordered(st["branch"])
        grads = gattn_call(branch, own_proj, hd)
        token[0] = grads[0]
        st["grads"] = swap_ctx(grads)

    def do_bwd(m, back):
        st = state[m]
        pieces = ordered(tuple(st["grads"]))
        out, extra = bwd_call(
            pieces,
            st["kvq"],
            st["qa"],
            st["exact"],
            st["lse"],
            back_table,
            hd,
            side,
            back,
            "attn_bwd%d" % m,
        )
        *st["grad_mixed"], st["dtab"] = out
        token[0] = st["dtab"]
        return extra

    def do_wgrad(left, right):
        parts = [state[m][left] for m in range(images)], [state[m][right] for m in range(images)]
        lefts, rights = ordered((tuple(parts[0]), tuple(parts[1])))
        total = sum(mm(a, b, NT) for a, b in zip(lefts, rights)).astype(bf16)
        token[0] = total
        return total

    first_image, second_image = state
    do_qkv(0, Quiet())
    got, (own_proj,), (full_up,) = do_qkv(
        1, Together(0, SwapCtx(first_image["mixed"]), JoinY(w_proj, 1), JoinY(w_fc1, 0))
    )
    first_image["mixed"] = first_image["mixed"][:1] + list(got)
    got, (full_down,), (full_proj,) = do_fwd(
        0,
        Together(
            1,
            SwapCtx(second_image["mixed"]),
            JoinY(w_fc2, 1),
            GatherTp(own_proj, (0, 8, "end")),
        ),
    )
    full_proj = full_proj.reshape(width, width)
    second_image["mixed"] = second_image["mixed"][:1] + list(got)
    (first_image["heads"],), (cots,) = do_fwd(
        1,
        Together(
            2,
            SpreadHeads(first_image["attn"], (0, 7, "end", "end")),
            GatherTp(grads_in, (0, 13, "end")),
        ),
    )
    ((second_image["heads"],),) = do_mlp(
        0, Together(7, SpreadHeads(second_image["attn"], (0, 2, "end", "end")))
    )
    ((first_image["branch"], first_image["grad_middle"]),) = do_mlp(
        1,
        Together(
            3, ReduceTp(*first_image["backward"], first_image["cot"], (0, 1, "end", "end", "end"))
        ),
    )
    do_gattn(0)
    up_total = do_wgrad("act2", "grad_pre")
    down_total = do_wgrad("cot", "hidden")
    (branch, exact, *second_image["grads"]), (grad_down,), (up_low,) = do_bwd(
        0,
        Together(
            4,
            ReduceTp(
                *second_image["backward"], second_image["cot"], (0, 1, 9, 10, "end"), own_proj
            ),
            GradsZThenY(down_total, (0, 5, 13, "end")),
            GradsY(up_total, (0, 11, "end")),
        ),
    )
    second_image["branch"], second_image["grad_middle"] = branch, exact
    proj_total = do_wgrad("branch", "joined")
    (grad_up,), got, (total_0,), (total_1,) = do_bwd(
        1,
        Together(
            5,
            GradsZ(up_low, (0, 6, "end", "end")),
            SwapCtx(first_image["grad_mixed"]),
            ReduceShare(*first_image["forward"], (0, 1, 6, "end")),
            ReduceShare(*second_image["forward"], (6, 7, 12, "end")),
        ),
    )
    first_image["grad_mixed"] = first_image["grad_mixed"][:1] + list(got)
    for st, total in zip(state, (total_0, total_1)):
        st["output"] = (st["middle"] + total).astype(bf16)
    def pair(parts):
        return halves(jnp.sum(sum(parts), axis=2))

    early = pair([st["sums2"] for st in state]).reshape(-1, 128)
    early = jnp.pad(early, ((0, 32 - early.shape[0]), (0, 0)))
    tables = jnp.concatenate([sum(st["dtab"] for st in state), early], axis=0)
    total_0, total_1, grad_qkv, small, grad_proj = tail_call(
        *ordered(
            (
                tuple(first_image["grad_mixed"]),
                first_image["full"],
                first_image["act1"],
                gain1,
                own_qkv,
                other_qkv,
                tables,
                tuple(second_image["grad_mixed"]),
                second_image["full"],
                second_image["act1"],
                proj_total,
            )
        ),
        hd,
        6,
    )
    token[0] = small
    outputs = [st["output"] for st in state]
    input_grads = [st["grad_middle"] + t for st, t in zip(state, (total_0, total_1))]
    grad_qkv = grad_qkv.reshape(half // 4, 3, heads * hd)

    norms2 = small[256 : 256 + 2 * width // 128].reshape(2, width)
    norms1 = jnp.stack(
        [small[288 + 16 * n : 288 + 16 * n + width // 128].reshape(width) for n in range(2)]
    )
    norms = jnp.concatenate([norms1, norms2], axis=0)
    tabs = small[:256]
    rows_grad = jnp.dot(hot_rows.T, tabs[:127, :hd], precision=highest)
    cols_grad = jnp.dot(hot_cols.T, tabs[129:256, :hd][::-1], precision=highest)
    return (
        jnp.swapaxes(jnp.stack(outputs), 1, 2),
        jnp.swapaxes(jnp.stack(input_grads), 1, 2),
        norms[0],
        norms[1],
        grad_qkv,
        rows_grad,
        cols_grad,
        grad_proj.T,
        norms[2],
        norms[3],
        grad_up,
        grad_down.T,
    )


def per_device(*args):
    block_input, w_proj, table_rows, index_rows = args[0], args[7], args[5], args[12]
    heads = w_proj.shape[0] // table_rows.shape[1]
    fits = (
        lax.axis_size("tp") == 4
        and lax.axis_size("ctx") == 4
        and lax.axis_size("fsdp") == 2
        and heads == 4
        and index_rows.shape[0] == 64
        and table_rows.shape[1] == 80
        and block_input.shape[1] % 512 == 0
        and block_input.shape[0] == 2
    )
    return fast_device(*args) if fits else plain_device(*args)


def solution(mesh):
    in_specs = (
        P("fsdp", "ctx", "tp"),
        P("fsdp", "ctx", "tp"),
        P(),
        P(),
        P("fsdp", None, "tp"),
        P(),
        P(),
        P("tp", "fsdp"),
        P(),
        P(),
        P("fsdp", "tp"),
        P("tp", "fsdp"),
        P(),
        P(),
    )
    out_specs = (
        P("fsdp", "ctx", "tp"),
        P("fsdp", "ctx", "tp"),
        P(),
        P(),
        P(("fsdp", "ctx"), None, "tp"),
        P(),
        P(),
        P("tp", ("fsdp", "ctx")),
        P(),
        P(),
        P(("fsdp", "ctx"), "tp"),
        P("tp", ("fsdp", "ctx")),
    )
    return jax.shard_map(
        per_device, mesh=mesh, in_specs=in_specs, out_specs=out_specs, check_vma=False
    )
```

```python
import functools
import math

import jax
import jax.numpy as jnp
from jax import lax
from jax.experimental import pallas as pl
from jax.experimental.pallas import tpu as pltpu
from jax.sharding import PartitionSpec as P

MICRO = 2


epsilon = 1e-06
highest = lax.Precision.HIGHEST
block_rows = 512
lowest = -1e30


def layer_norm(values, gain_vec, shift_vec):
    center = values - jnp.mean(values, axis=-1, keepdims=True)
    inv_std = lax.rsqrt(jnp.mean(center * center, axis=-1, keepdims=True) + epsilon)
    normed = center * inv_std
    return (normed * gain_vec + shift_vec, normed, inv_std)


def norm_back(upstream, normed, inv_std, gain_vec):
    scaled = upstream * gain_vec
    inner = (
        scaled
        - jnp.mean(scaled, axis=-1, keepdims=True)
        - normed * jnp.mean(scaled * normed, axis=-1, keepdims=True)
    )
    return inner * inv_std


def gelu_pair(values):
    normal_cdf = 0.5 * (1.0 + lax.erf(values * 0.7071067811865476))
    normal_pdf = jnp.exp(-0.5 * values * values) * 0.3989422804014327
    return (values * normal_cdf, normal_cdf + values * normal_pdf)


def rel_terms(queries, band_table, cols_table, grid_side):
    shape_in = queries.shape
    shaped = queries.astype(jnp.float32).reshape(
        shape_in[0], shape_in[1] // grid_side, grid_side, shape_in[2], shape_in[3]
    )
    rows_term = jnp.einsum("byxhc,ykc->byxhk", shaped, band_table, precision=highest)
    cols_term = jnp.einsum("byxhc,xkc->byxhk", shaped, cols_table, precision=highest)
    return (
        rows_term.reshape(shape_in[:3] + (grid_side,)),
        cols_term.reshape(shape_in[:3] + (grid_side,)),
    )


def key_bias(rows_term, cols_term, first_key, key_count, grid_side):
    picked = lax.dynamic_slice_in_dim(rows_term, first_key // grid_side, key_count // grid_side, 3)
    joined = picked[..., :, None] + cols_term[..., None, :]
    return joined.reshape(picked.shape[:3] + (key_count,))


def bias_back(grad_logits, first_key, key_count, grid_side):
    split = grad_logits.reshape(grad_logits.shape[:3] + (key_count // grid_side, grid_side))
    empty = jnp.zeros(grad_logits.shape[:3] + (grid_side,), jnp.float32)
    rows_part = lax.dynamic_update_slice_in_dim(
        empty, jnp.sum(split, axis=4), first_key // grid_side, 3
    )
    return (rows_part, jnp.sum(split, axis=3))


def scores_of(queries, key_blk, rows_term, cols_term, first_key, score_scale, grid_side):
    raw_dots = jnp.einsum("brhc,bkhc->bhrk", queries, key_blk, preferred_element_type=jnp.float32)
    return raw_dots * score_scale + key_bias(
        rows_term, cols_term, first_key, key_blk.shape[1], grid_side
    )


def plain_device(
    block_input,
    cotangent,
    norm1_gain,
    norm1_shift,
    w_qkv,
    table_rows,
    table_cols,
    w_proj,
    norm2_gain,
    norm2_shift,
    w_fc1,
    w_fc2,
    index_rows,
    index_cols,
):
    grid_side = index_rows.shape[0]
    table_len = table_rows.shape[0]
    head_dim = table_rows.shape[1]
    model_width = norm1_gain.shape[0]
    band_len = block_input.shape[1]
    band_grid = band_len // grid_side
    local_heads = w_proj.shape[0] // head_dim
    hidden_local = w_fc1.shape[1]
    per_micro = block_input.shape[0] // MICRO
    score_scale = head_dim ** (-0.5)
    ctx_place = lax.axis_index("ctx")
    whole_seq = band_len * lax.axis_size("ctx")
    levels = jnp.arange(table_len, dtype=jnp.int32)
    hot_rows = (index_rows.reshape(-1)[:, None] == levels[None, :]).astype(jnp.float32)
    hot_cols = (index_cols.reshape(-1)[:, None] == levels[None, :]).astype(jnp.float32)
    rows_table = jnp.dot(hot_rows, table_rows.astype(jnp.float32), precision=highest).reshape(
        grid_side, grid_side, head_dim
    )
    cols_table = jnp.dot(hot_cols, table_cols.astype(jnp.float32), precision=highest).reshape(
        grid_side, grid_side, head_dim
    )
    band_table = lax.dynamic_slice_in_dim(rows_table, ctx_place * band_grid, band_grid, 0)
    band_hot = lax.dynamic_slice_in_dim(
        hot_rows.reshape(grid_side, grid_side, table_len), ctx_place * band_grid, band_grid, 0
    )
    cols_hot = hot_cols.reshape(grid_side, grid_side, table_len)
    over_rows = (((0,), (0,)), ((), ()))
    over_cols = (((1,), (1,)), ((), ()))
    qkv_width = 3 * local_heads * head_dim
    grad_qkv = jnp.zeros((model_width, qkv_width), jnp.float32)
    grad_proj = jnp.zeros((local_heads * head_dim, model_width), jnp.float32)
    grad_up = jnp.zeros((model_width, hidden_local), jnp.float32)
    grad_down = jnp.zeros((hidden_local, model_width), jnp.float32)
    gain_one = jnp.zeros((model_width,), jnp.float32)
    shift_one = jnp.zeros((model_width,), jnp.float32)
    gain_two = jnp.zeros((model_width,), jnp.float32)
    shift_two = jnp.zeros((model_width,), jnp.float32)
    grad_rows_tab = jnp.zeros((table_len, head_dim), jnp.float32)
    grad_cols_tab = jnp.zeros((table_len, head_dim), jnp.float32)
    outputs = []
    input_grads = []
    for micro_step in range(MICRO):
        input_part = block_input[micro_step * per_micro : (micro_step + 1) * per_micro]
        grad_part = cotangent[micro_step * per_micro : (micro_step + 1) * per_micro]
        images = input_part.shape[0]
        tokens = images * band_len
        full_qkv, full_proj, full_up, full_down = (
            lax.all_gather(w_qkv, "fsdp", axis=0, tiled=True),
            lax.all_gather(w_proj, "fsdp", axis=1, tiled=True),
            lax.all_gather(w_fc1, "fsdp", axis=0, tiled=True),
            lax.all_gather(w_fc2, "fsdp", axis=1, tiled=True),
        )
        flat_qkv = full_qkv.reshape(model_width, qkv_width)
        input_full, grad_out_full = (
            lax.all_gather(input_part, "tp", axis=2, tiled=True),
            lax.all_gather(grad_part, "tp", axis=2, tiled=True),
        )
        normed_in, normed1, inv_std1 = layer_norm(
            input_full.astype(jnp.float32), norm1_gain, norm1_shift
        )
        first_act = normed_in.astype(jnp.bfloat16).reshape(tokens, model_width)
        mixed_qkv = jnp.dot(first_act, flat_qkv, preferred_element_type=jnp.float32).astype(
            jnp.bfloat16
        )
        mixed_qkv = mixed_qkv.reshape(images, band_len, 3, local_heads, head_dim)
        queries = mixed_qkv[:, :, 0]
        key_part = mixed_qkv[:, :, 1]
        value_part = mixed_qkv[:, :, 2]
        rows_term, cols_term = rel_terms(queries, band_table, cols_table, grid_side)
        rows_swap = jnp.transpose(rows_term, (0, 2, 1, 3))
        cols_swap = jnp.transpose(cols_term, (0, 2, 1, 3))
        fold_init = (
            jnp.full((images, local_heads, band_len), lowest, jnp.float32),
            jnp.zeros((images, local_heads, band_len), jnp.float32),
            jnp.zeros((images, local_heads, band_len, head_dim), jnp.float32),
        )
        key_piece = lax.all_gather(key_part, "ctx", axis=1, tiled=True)
        value_piece = lax.all_gather(value_part, "ctx", axis=1, tiled=True)
        piece_len = key_piece.shape[1]
        sub_len = math.gcd(piece_len, block_rows)

        def forward_advance(block_idx, state):
            running, denom_sum, acc_out = state
            offset = block_idx * sub_len
            key_blk = lax.dynamic_slice_in_dim(key_piece, offset, sub_len, 1)
            value_blk = lax.dynamic_slice_in_dim(value_piece, offset, sub_len, 1)
            logits = scores_of(
                queries, key_blk, rows_swap, cols_swap, offset, score_scale, grid_side
            )
            new_peak = jnp.maximum(running, jnp.max(logits, axis=-1))
            rescale = jnp.exp(running - new_peak)
            weights = jnp.exp(logits - new_peak[..., None])
            denom_sum = denom_sum * rescale + jnp.sum(weights, axis=-1)
            acc_out = acc_out * rescale[..., None] + jnp.einsum(
                "bhrk,bkhc->bhrc",
                weights.astype(jnp.bfloat16),
                value_blk,
                preferred_element_type=jnp.float32,
            )
            return (new_peak, denom_sum, acc_out)

        peak_all, denom_all, acc_all = lax.fori_loop(
            0, piece_len // sub_len, forward_advance, fold_init
        )
        attn_exact = jnp.transpose(acc_all / denom_all[..., None], (0, 2, 1, 3))
        log_total = peak_all + jnp.log(denom_all)
        attn_low = attn_exact.astype(jnp.bfloat16).reshape(tokens, local_heads * head_dim)
        attn_branch = jnp.dot(attn_low, full_proj, preferred_element_type=jnp.float32).reshape(
            images, band_len, model_width
        )
        attn_share = lax.psum_scatter(
            attn_branch.astype(jnp.bfloat16), "tp", scatter_dimension=2, tiled=True
        ).astype(jnp.float32)
        middle_share = input_part.astype(jnp.float32) + attn_share
        middle_full = lax.all_gather(
            middle_share.astype(jnp.bfloat16), "tp", axis=2, tiled=True
        ).astype(middle_share.dtype)
        normed_mid, normed2, inv_std2 = layer_norm(middle_full, norm2_gain, norm2_shift)
        second_act = normed_mid.astype(jnp.bfloat16).reshape(tokens, model_width)
        pre_act = jnp.dot(second_act, full_up, preferred_element_type=jnp.float32)
        gelu_out, gelu_slope = gelu_pair(pre_act)
        hidden_low = gelu_out.astype(jnp.bfloat16)
        mlp_branch = jnp.dot(hidden_low, full_down, preferred_element_type=jnp.float32).reshape(
            images, band_len, model_width
        )
        mlp_share = lax.psum_scatter(
            mlp_branch.astype(jnp.bfloat16), "tp", scatter_dimension=2, tiled=True
        ).astype(jnp.float32)
        outputs.append((middle_share + mlp_share).astype(jnp.bfloat16))
        grad_out_flat = grad_out_full.reshape(tokens, model_width)
        grad_down = grad_down + lax.dot_general(
            hidden_low, grad_out_flat, over_rows, preferred_element_type=jnp.float32
        )
        grad_hidden = lax.dot_general(
            grad_out_flat, full_down, over_cols, preferred_element_type=jnp.float32
        )
        grad_pre = (grad_hidden * gelu_slope).astype(jnp.bfloat16)
        grad_up = grad_up + lax.dot_general(
            second_act, grad_pre, over_rows, preferred_element_type=jnp.float32
        )
        grad_second = lax.dot_general(
            grad_pre, full_up, over_cols, preferred_element_type=jnp.float32
        ).reshape(images, band_len, model_width)
        gain_two = gain_two + jnp.sum(grad_second * normed2, axis=(0, 1))
        shift_two = shift_two + jnp.sum(grad_second, axis=(0, 1))
        grad_middle = grad_part.astype(jnp.float32) + lax.psum_scatter(
            norm_back(grad_second, normed2, inv_std2, norm2_gain).astype(jnp.bfloat16),
            "tp",
            scatter_dimension=2,
            tiled=True,
        ).astype(jnp.float32)
        grad_branch = lax.all_gather(
            grad_middle.astype(jnp.bfloat16), "tp", axis=2, tiled=True
        ).reshape(tokens, model_width)
        grad_proj = grad_proj + lax.dot_general(
            attn_low, grad_branch, over_rows, preferred_element_type=jnp.float32
        )
        grad_attn = lax.dot_general(
            grad_branch, full_proj, over_cols, preferred_element_type=jnp.float32
        ).astype(jnp.bfloat16)
        grad_attn = grad_attn.reshape(images, band_len, local_heads, head_dim)
        delta_rows = jnp.sum(grad_attn.astype(jnp.float32) * attn_exact, axis=-1)
        delta_swap = jnp.transpose(delta_rows, (0, 2, 1))
        query_zero = jnp.zeros((images, local_heads, band_len, head_dim), jnp.float32)
        rel_zero = jnp.zeros((images, local_heads, band_len, grid_side), jnp.float32)
        whole_zero = jnp.zeros((images, whole_seq, local_heads, head_dim), jnp.float32)
        back_init = (query_zero, rel_zero, rel_zero, whole_zero, whole_zero)
        back_key_piece = lax.all_gather(key_part, "ctx", axis=1, tiled=True)
        back_value_piece = lax.all_gather(value_part, "ctx", axis=1, tiled=True)
        back_piece_len = back_key_piece.shape[1]
        back_sub_len = math.gcd(back_piece_len, block_rows)

        def back_advance(block_idx, state):
            offset = block_idx * back_sub_len
            key_blk = lax.dynamic_slice_in_dim(back_key_piece, offset, back_sub_len, 1)
            value_blk = lax.dynamic_slice_in_dim(back_value_piece, offset, back_sub_len, 1)
            logits = scores_of(
                queries, key_blk, rows_swap, cols_swap, offset, score_scale, grid_side
            )
            probs = jnp.exp(logits - log_total[..., None])
            grad_probs = jnp.einsum(
                "brhc,bkhc->bhrk", grad_attn, value_blk, preferred_element_type=jnp.float32
            )
            grad_logits = (probs * (grad_probs - delta_swap[..., None])).astype(jnp.bfloat16)
            grad_query = state[0] + jnp.einsum(
                "bhrk,bkhc->bhrc", grad_logits, key_blk, preferred_element_type=jnp.float32
            )
            add_rows, add_cols = bias_back(
                grad_logits.astype(jnp.float32), offset, back_sub_len, grid_side
            )
            grad_key_blk = (
                jnp.einsum(
                    "bhrk,brhc->bkhc", grad_logits, queries, preferred_element_type=jnp.float32
                )
                * score_scale
            )
            grad_value_blk = jnp.einsum(
                "bhrk,brhc->bkhc",
                probs.astype(jnp.bfloat16),
                grad_attn,
                preferred_element_type=jnp.float32,
            )
            keys_acc = lax.dynamic_update_slice_in_dim(
                state[3],
                lax.dynamic_slice_in_dim(state[3], offset, back_sub_len, 1) + grad_key_blk,
                offset,
                1,
            )
            values_acc = lax.dynamic_update_slice_in_dim(
                state[4],
                lax.dynamic_slice_in_dim(state[4], offset, back_sub_len, 1) + grad_value_blk,
                offset,
                1,
            )
            return (grad_query, state[1] + add_rows, state[2] + add_cols, keys_acc, values_acc)

        folded = lax.fori_loop(0, back_piece_len // back_sub_len, back_advance, back_init)
        grad_keys, grad_values = (
            lax.psum_scatter(
                folded[3].astype(jnp.bfloat16), "ctx", scatter_dimension=1, tiled=True
            ).astype(jnp.float32),
            lax.psum_scatter(
                folded[4].astype(jnp.bfloat16), "ctx", scatter_dimension=1, tiled=True
            ).astype(jnp.float32),
        )
        grad_query = jnp.transpose(folded[0] * score_scale, (0, 2, 1, 3))
        grad_rel_rows = jnp.transpose(folded[1], (0, 2, 1, 3)).reshape(
            images, band_grid, grid_side, local_heads, grid_side
        )
        grad_rel_cols = jnp.transpose(folded[2], (0, 2, 1, 3)).reshape(
            images, band_grid, grid_side, local_heads, grid_side
        )
        query_grid = queries.astype(jnp.float32).reshape(
            images, band_grid, grid_side, local_heads, head_dim
        )
        rel_query = jnp.einsum(
            "byxhk,ykc->byxhc", grad_rel_rows, band_table, precision=highest
        ) + jnp.einsum("byxhk,xkc->byxhc", grad_rel_cols, cols_table, precision=highest)
        grad_query = grad_query + rel_query.reshape(images, band_len, local_heads, head_dim)
        band_rows_grad = jnp.einsum(
            "byxhk,byxhc->ykc", grad_rel_rows, query_grid, precision=highest
        )
        cols_grad = jnp.einsum("byxhk,byxhc->xkc", grad_rel_cols, query_grid, precision=highest)
        grad_rows_tab = grad_rows_tab + jnp.einsum(
            "ykt,ykc->tc", band_hot, band_rows_grad, precision=highest
        )
        grad_cols_tab = grad_cols_tab + jnp.einsum(
            "xkt,xkc->tc", cols_hot, cols_grad, precision=highest
        )
        grad_mixed = (
            jnp.stack((grad_query, grad_keys, grad_values), axis=2)
            .astype(jnp.bfloat16)
            .reshape(tokens, qkv_width)
        )
        grad_qkv = grad_qkv + lax.dot_general(
            first_act, grad_mixed, over_rows, preferred_element_type=jnp.float32
        )
        grad_first = lax.dot_general(
            grad_mixed, flat_qkv, over_cols, preferred_element_type=jnp.float32
        ).reshape(images, band_len, model_width)
        gain_one = gain_one + jnp.sum(grad_first * normed1, axis=(0, 1))
        shift_one = shift_one + jnp.sum(grad_first, axis=(0, 1))
        input_grads.append(
            grad_middle
            + lax.psum_scatter(
                norm_back(grad_first, normed1, inv_std1, norm1_gain).astype(jnp.bfloat16),
                "tp",
                scatter_dimension=2,
                tiled=True,
            ).astype(jnp.float32)
        )
    owned_grads = (
        lax.psum_scatter(
            grad_qkv.reshape(model_width, 3, local_heads * head_dim).astype(jnp.bfloat16),
            ("fsdp", "ctx"),
            scatter_dimension=0,
            tiled=True,
        ).astype(jnp.float32),
        lax.psum_scatter(
            grad_proj.astype(jnp.bfloat16), ("fsdp", "ctx"), scatter_dimension=1, tiled=True
        ).astype(jnp.float32),
        lax.psum_scatter(
            grad_up.astype(jnp.bfloat16), ("fsdp", "ctx"), scatter_dimension=0, tiled=True
        ).astype(jnp.float32),
        lax.psum_scatter(
            grad_down.astype(jnp.bfloat16), ("fsdp", "ctx"), scatter_dimension=1, tiled=True
        ).astype(jnp.float32),
    )
    small_sums = lax.psum(
        (gain_one, shift_one, grad_rows_tab, grad_cols_tab, gain_two, shift_two),
        ("fsdp", "ctx", "tp"),
    )
    return (
        jnp.concatenate(outputs, axis=0),
        jnp.concatenate(input_grads, axis=0),
        small_sums[0],
        small_sums[1],
        owned_grads[0],
        small_sums[2],
        small_sums[3],
        owned_grads[1],
        small_sums[4],
        small_sums[5],
        owned_grads[2],
        owned_grads[3],
    )


f32 = jnp.float32
bf16 = jnp.bfloat16
LOG2E = 1.4426950408889634
NN = (((1,), (0,)), ((), ()))
NT = (((1,), (1,)), ((), ()))
TN = (((0,), (0,)), ((), ()))
VMEM_BYTES = 56 << 20


def mm(lhs, rhs, dims=NN):
    return lax.dot_general(lhs, rhs, dims, preferred_element_type=f32)


def pxor(value, axis, bit):
    size = lax.axis_size(axis)
    return lax.ppermute(value, axis, [(i, i ^ bit) for i in range(size)])


def after(values, done):
    return lax.optimization_barrier((values, done))[0]


def gather_tp(share):
    from_x = pxor(share, "tp", 2)
    from_core = pxor(share, "tp", 1)
    return [share, from_core, from_x, pxor(from_x, "tp", 1)]


def swap_ctx(pieces):
    return [pieces[0]] + [pxor(pieces[s], "ctx", s) for s in range(1, len(pieces))]


def gelu_parts(x):
    size = jnp.abs(x)
    t = 1.0 / (1.0 + 0.23164190 * size)
    poly = jnp.full_like(t, 0.5307027145)
    for coef in (-0.726576013, 0.7107068705, -0.142248368, 0.127414796):
        poly = poly * t + coef
    bell = jnp.exp2((-0.5 * LOG2E) * (x * x))
    tail = poly * t * bell
    cdf = jnp.where(x >= 0.0, 1.0 - tail, tail)
    return cdf, bell * 0.3989422804014327


ROWS = 64
ANY = pl.BlockSpec(memory_space=pl.ANY)
MESH = pl.DeviceIdType.MESH


def xor4(a, b):
    high = lax.rem(lax.div(a, 2) + lax.div(b, 2), 2)
    return 2 * high + lax.rem(lax.rem(a, 2) + lax.rem(b, 2), 2)


def spots():
    t, y = lax.axis_index("tp"), lax.axis_index("fsdp")
    return xor4(t, 2 * y), lax.axis_index("ctx")


def peer(axis, bit):
    return {axis: xor4(lax.axis_index(axis), bit)}


def greet(peers):
    barrier = pltpu.get_barrier_semaphore()
    for device in peers:
        pl.semaphore_signal(barrier, inc=1, device_id=device, device_id_type=MESH)
    pl.semaphore_wait(barrier, len(peers))


def remote(source, target, sems, slot, device):
    send, recv = sems
    return pltpu.make_async_remote_copy(
        src_ref=source,
        dst_ref=target,
        send_sem=send.at[slot],
        recv_sem=recv.at[slot],
        device_id=device,
        device_id_type=MESH,
    )


def dma(count=1):
    return pltpu.SemaphoreType.DMA((count,))


def start_all(copies):
    for copy in copies:
        copy.start()


def wait_all(copies):
    for copy in copies:
        copy.wait()


def add_rows(rows, body, step=32):
    def advance(n, carry):
        body(pl.ds(pl.multiple_of(n * step, step), step))
        return carry

    lax.fori_loop(0, rows // step, advance, 0, unroll=2 if rows % (2 * step) == 0 else 1)


CTX_PEERS = (("ctx", 1), ("ctx", 2), ("ctx", 3))
TP_PEERS = (("tp", 1), ("tp", 2))
Y_PEERS = (("fsdp", 1),)


class Quiet:
    ins, out_shape, scratch, peers = (), (), (), ()
    ident = None

    def steps(self, ins, outs, scratch):
        return {}


class Together:
    def __init__(self, ident, *backs):
        self.backs, self.ident = backs, ident
        self.ins = sum((tuple(b.ins) for b in backs), ())
        self.out_shape = sum((list(b.out_shape) for b in backs), [])
        self.scratch = sum((list(b.scratch) for b in backs), [])
        self.peers = tuple(dict.fromkeys(sum((tuple(b.peers) for b in backs), ())))

    def split(self, outs):
        groups = []
        for b in self.backs:
            group, outs = take(outs, len(b.out_shape))
            groups.append(group)
        return groups

    def steps(self, ins, outs, scratch):
        table = {0: [lambda: greet([peer(*p) for p in self.peers])]}
        for b in self.backs:
            mine_in, ins = take(ins, len(b.ins))
            mine_out, outs = take(outs, len(b.out_shape))
            mine_scratch, scratch = take(scratch, len(b.scratch))
            for point, step in b.steps(mine_in, mine_out, mine_scratch):
                table.setdefault(point, []).append(step)

        def chain(fns):
            def run():
                for fn in fns:
                    fn()

            return run

        return {point: chain(fns) for point, fns in table.items()}


class SwapCtx:
    peers = CTX_PEERS

    def __init__(self, pieces, begin=0, end="end"):
        self.ins, self.points = tuple(pieces[1:]), (begin, end)
        self.out_shape = [(p.shape, bf16) for p in self.ins]
        self.scratch = [dma(3), dma(3)]

    def steps(self, ins, outs, scratch):
        def copies():
            return [remote(ins[s], outs[s], scratch, s, peer("ctx", s + 1)) for s in (2, 1, 0)]

        return zip(self.points, (lambda: start_all(copies()), lambda: wait_all(copies())))


class JoinY:
    peers = Y_PEERS

    def __init__(self, own, axis, begin=0, end="end"):
        self.ins, self.axis, self.points = (own,), axis, (begin, end)
        shape = list(own.shape)
        shape[axis] *= 2
        self.out_shape = [(tuple(shape), bf16)]
        self.scratch = [dma(1), dma(1), dma(1)]

    def steps(self, ins, outs, scratch):
        (own,), (full,) = ins, outs
        half = own.shape[self.axis]
        low, high = pl.ds(0, half), pl.ds(half, half)

        def at(part):
            return full.at[part] if self.axis == 0 else full.at[:, part]

        def copies():
            return [
                remote(own, at(high), scratch[:2], 0, peer("fsdp", 1)),
                pltpu.make_async_copy(own, at(low), scratch[2].at[0]),
            ]

        return zip(self.points, (lambda: start_all(copies()), lambda: wait_all(copies())))


class GatherTp:
    peers = TP_PEERS

    def __init__(self, own, points):
        self.ins, self.points = (own,), points
        self.out_shape = [((4,) + own.shape, bf16)]
        self.scratch = [dma(3), dma(3), dma(1)]

    def steps(self, ins, outs, scratch):
        (own,), (full,) = ins, outs
        sems, local_sem = scratch[:2], scratch[2]

        def local():
            return pltpu.make_async_copy(own, full.at[0], local_sem.at[0])

        def to_x():
            return remote(own, full.at[2], sems, 0, peer("tp", 2))

        def to_core():
            return remote(own, full.at[1], sems, 1, peer("tp", 1))

        def onward():
            return remote(full.at[2], full.at[3], sems, 2, peer("tp", 1))

        def forward():
            to_x().wait()
            onward().start()

        return zip(
            self.points,
            (
                lambda: start_all([to_x(), to_core(), local()]),
                forward,
                lambda: wait_all([to_core(), onward(), local()]),
            ),
        )


class SpreadHeads:
    peers = CTX_PEERS + TP_PEERS

    def __init__(self, pieces, points):
        self.ins, self.points = tuple(pieces), points
        self.out_shape = [((4, 4) + pieces[0].shape, bf16)]
        self.scratch = [dma(6), dma(6), dma(1)]

    def steps(self, ins, outs, scratch):
        (out,) = outs
        sems, local_sem = scratch[:2], scratch[2]

        def arrivals():
            copies = [remote(ins[s], out.at[0, s], sems, s - 1, peer("ctx", s)) for s in range(1, 4)]
            return copies + [pltpu.make_async_copy(ins[0], out.at[0, 0], local_sem.at[0])]

        def to_x():
            return remote(out.at[0], out.at[2], sems, 3, peer("tp", 2))

        def to_core():
            return remote(out.at[0], out.at[1], sems, 4, peer("tp", 1))

        def onward():
            return remote(out.at[2], out.at[3], sems, 5, peer("tp", 1))

        def forward():
            wait_all(arrivals())
            start_all([to_x(), to_core()])

        def final():
            to_x().wait()
            onward().start()

        return zip(
            self.points,
            (
                lambda: start_all(arrivals()),
                forward,
                final,
                lambda: wait_all([to_core(), onward()]),
            ),
        )


class ReduceTp:
    peers = TP_PEERS

    def __init__(self, keep, send, cot, points, weight=None):
        self.ins, self.points = (keep, send, cot), points
        rows, tokens = keep.shape
        self.heads = weight is not None
        self.out_shape = [((2 * rows, tokens), bf16), ((rows // 2, tokens), f32)]
        self.scratch = [pltpu.VMEM(keep.shape, bf16)] * 4 + [
            pltpu.VMEM((2 * rows, tokens), bf16),
            pltpu.VMEM((rows // 2, tokens), f32),
            dma(8),
            dma(8),
            dma(7),
        ]
        if self.heads:
            self.ins += (weight,)
            hd = weight.shape[0] // 4
            self.out_shape += [((hd, tokens), bf16)] * 4
            self.scratch += [pltpu.VMEM(weight.shape, bf16), pltpu.VMEM((4, hd, tokens), bf16)]
            self.peers = TP_PEERS + CTX_PEERS

    def steps(self, ins, outs, scratch):
        keep, send, cot = ins[:3]
        full_out, exact_out = outs[:2]
        mine, from_core, from_x, grads, full, exact = scratch[:6]
        sems, local_sem = scratch[6:8], scratch[8]
        rows = mine.shape[0]
        half = rows // 2
        spot, z = spots()
        core = lax.rem(spot, 2)

        def rows_of(n, which):
            return pl.ds(pl.multiple_of((2 * n + which) * half, half), half)

        def core_copy():
            return remote(send, from_core, sems, 0, peer("tp", 1))

        def x_copy():
            return remote(mine, from_x, sems, 1, peer("tp", 2))

        def back_copies():
            return [
                remote(full.at[rows_of(n, core)], full.at[rows_of(n, core)], sems, 2 * n + 2, peer("tp", 1))
                for n in range(2)
            ]

        def loads():
            copies = [pltpu.make_async_copy(keep, mine, local_sem.at[0])]
            for n in range(2):
                copies.append(
                    pltpu.make_async_copy(
                        cot.at[rows_of(n, core)],
                        grads.at[n * half : (n + 1) * half],
                        local_sem.at[n + 1],
                    )
                )
            if self.heads:
                copies.append(pltpu.make_async_copy(ins[3], scratch[9], local_sem.at[5]))
            return copies

        def store_exact():
            return pltpu.make_async_copy(exact, exact_out, local_sem.at[4])

        def store_full():
            return pltpu.make_async_copy(full, full_out, local_sem.at[3])

        def begin():
            core_copy().start()
            start_all(loads())

        def add_core():
            wait_all(loads())
            core_copy().wait()

            def add(at):
                mine[at] = (mine[at].astype(f32) + from_core[at].astype(f32)).astype(bf16)

            add_rows(rows, add)
            x_copy().start()

        def add_x():
            x_copy().wait()
            step = 32
            for part in range(2):

                def add(n, carry, part=part):
                    at = pl.ds(pl.multiple_of(part * half + n * step, step), step)
                    total = mine[at].astype(f32) + from_x[at].astype(f32) + grads[at].astype(f32)
                    to = (2 * part + core) * half + n * step
                    full[pl.ds(pl.multiple_of(to, step), step)] = total.astype(bf16)

                    @pl.when(lax.div(spot, 2) == part)
                    def _():
                        exact[pl.ds(pl.multiple_of(n * step, step), step)] = total

                    return carry

                lax.fori_loop(0, half // step, add, 0)
            start_all(back_copies())
            store_exact().start()

        def swaps():
            parts = scratch[10]
            return [
                remote(parts.at[xor4(z, s)], outs[2 + s], sems, 4 + s, peer("ctx", s))
                for s in (1, 2, 3)
            ]

        def local_head():
            return pltpu.make_async_copy(scratch[10].at[z], outs[2], local_sem.at[6])

        def spread_heads():
            wait_all(back_copies())
            store_full().start()
            if self.heads:
                weight, parts = scratch[9], scratch[10]
                tokens = full.shape[1]
                step = 256
                for n in range(tokens // step):
                    at = slice(n * step, (n + 1) * step)
                    product = mm(weight[...], full[:, at]).astype(bf16)
                    parts[:, :, at] = product.reshape(parts.shape[0], parts.shape[1], step)
                start_all(swaps() + [local_head()])

        def end():
            wait_all([store_exact(), store_full()])
            if self.heads:
                wait_all(swaps() + [local_head()])

        return zip(self.points, (begin, add_core, add_x, spread_heads, end))


class ReduceShare:
    peers = TP_PEERS

    def __init__(self, keep, send, points):
        self.ins, self.points = (keep, send), points
        rows, tokens = keep.shape
        self.out_shape = [((rows // 2, tokens), f32)]
        self.scratch = [pltpu.VMEM(keep.shape, bf16)] * 2 + [
            pltpu.VMEM((rows // 2, tokens), bf16),
            pltpu.VMEM((rows // 2, tokens), f32),
            dma(2),
            dma(2),
            dma(2),
        ]

    def steps(self, ins, outs, scratch):
        keep, send = ins
        mine, from_core, from_x, exact = scratch[:4]
        sems, local_sem = scratch[4:6], scratch[6]
        half = exact.shape[0]
        spot, _ = spots()
        first = lax.div(spot, 2) * half
        second = half - first

        def core_copy():
            return remote(send, from_core, sems, 0, peer("tp", 1))

        def x_copy():
            source = mine.at[pl.ds(pl.multiple_of(second, half), half)]
            return remote(source, from_x, sems, 1, peer("tp", 2))

        def load():
            return pltpu.make_async_copy(keep, mine, local_sem.at[0])

        def store():
            return pltpu.make_async_copy(exact, outs[0], local_sem.at[1])

        def add_core():
            load().wait()
            core_copy().wait()

            def add(at):
                mine[at] = (mine[at].astype(f32) + from_core[at].astype(f32)).astype(bf16)

            add_rows(2 * half, add)
            x_copy().start()

        def add_x():
            x_copy().wait()

            def add(n, carry):
                at = pl.ds(pl.multiple_of(n * 16, 16), 16)
                own = pl.ds(pl.multiple_of(first + n * 16, 16), 16)
                exact[at] = mine[own].astype(f32) + from_x[at].astype(f32)
                return carry

            lax.fori_loop(0, half // 16, add, 0)
            store().start()

        return zip(
            self.points,
            (
                lambda: start_all([core_copy(), load()]),
                add_core,
                add_x,
                lambda: store().wait(),
            ),
        )


class GradsY:
    peers = Y_PEERS

    def __init__(self, total, points):
        self.ins, self.points = (total,), points
        half = (total.shape[0] // 2, total.shape[1])
        self.out_shape = [(half, bf16)]
        self.scratch = [pltpu.VMEM(half, bf16)] * 2 + [dma(1), dma(1), dma(2)]

    def steps(self, ins, outs, scratch):
        (total,) = ins
        mine, got = scratch[:2]
        sems, local_sem = scratch[2:4], scratch[4]
        half = mine.shape[0]

        def across():
            return remote(total.at[half:], got, sems, 0, peer("fsdp", 1))

        def load():
            return pltpu.make_async_copy(total.at[:half], mine, local_sem.at[0])

        def store():
            return pltpu.make_async_copy(mine, outs[0], local_sem.at[1])

        def add_y():
            load().wait()
            across().wait()

            def add(at):
                mine[at] = (mine[at].astype(f32) + got[at].astype(f32)).astype(bf16)

            add_rows(half, add)
            store().start()

        return zip(
            self.points,
            (lambda: start_all([across(), load()]), add_y, lambda: store().wait()),
        )


class GradsZ:
    peers = (("ctx", 1), ("ctx", 2))

    def __init__(self, low, points):
        self.ins, self.points = (low,), points
        rows, cols = low.shape[0] // 4, low.shape[1]
        self.out_shape = [((rows, cols), f32)]
        self.scratch = [
            pltpu.VMEM((5, rows, cols), bf16),
            pltpu.VMEM((rows, cols), f32),
            dma(3),
            dma(3),
            dma(3),
        ]

    def steps(self, ins, outs, scratch):
        (low,) = ins
        buf, exact = scratch[:2]
        sems, local_sem = scratch[2:4], scratch[4]
        rows = exact.shape[0]
        _, z = spots()

        def chunk(s):
            return low.at[pl.ds(pl.multiple_of(xor4(z, s) * rows, 16), rows)]

        def near():
            return [
                remote(chunk(s), buf.at[2 + n], sems, n, peer("ctx", 1)) for n, s in enumerate((1, 3))
            ]

        def far():
            return remote(buf.at[1], buf.at[4], sems, 2, peer("ctx", 2))

        def loads():
            return [
                pltpu.make_async_copy(chunk(s), buf.at[n], local_sem.at[n])
                for n, s in enumerate((0, 2))
            ]

        def store():
            return pltpu.make_async_copy(exact, outs[0], local_sem.at[2])

        def add_near():
            wait_all(loads() + near())

            def add(at):
                buf[1, at] = (buf[1, at].astype(f32) + buf[3, at].astype(f32)).astype(bf16)

            add_rows(rows, add)
            far().start()

        def add_far():
            far().wait()

            def add(at):
                exact[at] = (buf[0, at].astype(f32) + buf[2, at].astype(f32)) + buf[4, at].astype(f32)

            add_rows(rows, add)
            store().start()

        return zip(
            self.points,
            (lambda: start_all(near() + loads()), add_near, add_far, lambda: store().wait()),
        )


class GradsZThenY:
    peers = (("ctx", 1), ("ctx", 2)) + Y_PEERS

    def __init__(self, total, points):
        self.ins, self.points = (total,), points
        rows, cols = total.shape[0] // 8, total.shape[1]
        self.out_shape = [((rows, cols), f32)]
        self.scratch = [
            pltpu.VMEM((2, 5, rows, cols), bf16),
            pltpu.VMEM((rows, cols), bf16),
            pltpu.VMEM((rows, cols), f32),
            dma(7),
            dma(7),
            dma(5),
        ]

    def steps(self, ins, outs, scratch):
        (total,) = ins
        buf, from_y, exact = scratch[:3]
        sems, local_sem = scratch[3:5], scratch[5]
        rows = exact.shape[0]
        _, z = spots()

        def chunk(n, s):
            return total.at[pl.ds(pl.multiple_of((4 * n + xor4(z, s)) * rows, 16), rows)]

        def near(n):
            return [
                remote(chunk(n, s), buf.at[n, 2 + k], sems, 2 * n + k, peer("ctx", 1))
                for k, s in enumerate((1, 3))
            ]

        def far(n):
            return remote(buf.at[n, 1], buf.at[n, 4], sems, 4 + n, peer("ctx", 2))

        def to_y():
            return remote(buf.at[1, 0], from_y, sems, 6, peer("fsdp", 1))

        def loads():
            return [
                pltpu.make_async_copy(chunk(n, s), buf.at[n, k], local_sem.at[2 * n + k])
                for n in range(2)
                for k, s in enumerate((0, 2))
            ]

        def store():
            return pltpu.make_async_copy(exact, outs[0], local_sem.at[4])

        def begin():
            start_all(near(1) + loads())

        def add_near(n):
            wait_all(near(n))

            def add(at):
                buf[n, 1, at] = (buf[n, 1, at].astype(f32) + buf[n, 3, at].astype(f32)).astype(bf16)

            add_rows(rows, add)
            far(n).start()

        def summed(n, at):
            return (buf[n, 0, at].astype(f32) + buf[n, 2, at].astype(f32)) + buf[n, 4, at].astype(f32)

        def second():
            wait_all(loads())
            add_near(1)
            start_all(near(0))

        def third():
            add_near(0)
            far(1).wait()

            def add(at):
                buf[1, 0, at] = summed(1, at).astype(bf16)

            add_rows(rows, add)
            to_y().start()

        def end():
            to_y().wait()
            far(0).wait()

            def add(at):
                exact[at] = summed(0, at) + from_y[at].astype(f32)

            add_rows(rows, add)
            store().start()
            store().wait()

        return zip(self.points, (begin, second, third, end))


def take(refs, count):
    return refs[:count], refs[count:]


def run_step(steps, index, last=None):
    for point, step in steps.items():
        if point != "end":
            pl.when(index == point)(step)
    if last is not None and "end" in steps:
        pl.when(last)(steps["end"])


def assemble(place, pieces, full):
    count = len(pieces)
    share = pieces[0].shape[-2]
    for mine in range(count):

        @pl.when(place == mine)
        def _(mine=mine):
            for a in range(count):
                piece = pieces[a ^ mine]
                value = piece[0] if len(piece.shape) == 3 else piece[...]
                full[a * share : (a + 1) * share, :] = value


def spread(parts, place, keep_ref, send_ref):
    core = lax.rem(place, 2)
    share = parts.shape[1]
    for n in range(2):
        keep_ref[n * share : (n + 1) * share] = parts[2 * n + core]
        send_ref[n * share : (n + 1) * share] = parts[2 * n + 1 - core]


def over_rows_of(count, body, init, unroll=2):
    def advance(n, carry):
        return body(pl.ds(pl.multiple_of(n * ROWS, ROWS), ROWS), carry)

    return lax.fori_loop(0, count // ROWS, advance, init, unroll=unroll)


def fold8(value):
    return jnp.sum(value.reshape(value.shape[0] // 8, 8, value.shape[1]), axis=0)


def wide(value, lanes):
    return jnp.concatenate([value] * (lanes // 128), axis=1)


def moments(full):
    rows, lanes = full.shape
    zero = jnp.zeros((8, lanes), f32)
    total = over_rows_of(rows, lambda at, c: c + fold8(full[at].astype(f32)), zero)
    mean = jnp.sum(total, axis=0, keepdims=True) * (1.0 / rows)

    def square(at, c):
        center = full[at].astype(f32) - mean
        return c + fold8(center * center)

    total = over_rows_of(rows, square, zero)
    var = jnp.sum(total, axis=0, keepdims=True) * (1.0 / rows)
    return mean, lax.rsqrt(var + epsilon)


def normalize(full, act, gain, shift):
    mean, inv_std = moments(full)
    lanes = full.shape[1]

    def write(at, carry):
        normed = (full[at].astype(f32) - mean) * inv_std
        act[at] = (normed * wide(gain[at], lanes) + wide(shift[at], lanes)).astype(bf16)
        return carry

    over_rows_of(full.shape[0], write, 0)
    return mean, inv_std


def lane_sums(value):
    total = value[:, 0:128]
    for n in range(1, value.shape[1] // 128):
        total += value[:, n * 128 : (n + 1) * 128]
    return total


CHUNK = 256
SUB = 32


def subs(first):
    for r in range(CHUNK // SUB):
        yield slice(r * SUB, (r + 1) * SUB), slice(first + r * SUB, first + (r + 1) * SUB)


def gather_chunk(state, up_all, first, full, mean, inv_std, gain, sums, upstream):
    plain, mixed = state
    lanes = up_all.shape[1]
    for part, to in subs(first):
        up = up_all[part]
        upstream[to] = up
        both = up * ((full[to].astype(f32) - mean) * inv_std)
        g = wide(gain[to], lanes)
        sums[0, to] += lane_sums(both)
        sums[1, to] += lane_sums(up)
        plain += fold8(up * g)
        mixed += fold8(both * g)
    return plain, mixed


def finish_stats(state, width):
    plain, mixed = state
    scale = 1.0 / width
    return (
        jnp.sum(plain, axis=0, keepdims=True) * scale,
        jnp.sum(mixed, axis=0, keepdims=True) * scale,
    )


def write_chunk(parts, first, upstream, full, mean, inv_std, gain, stats):
    plain, mixed = stats
    share = parts.shape[1]
    lanes = upstream.shape[1]
    for _, to in subs(first):
        normed = (full[to].astype(f32) - mean) * inv_std
        result = (upstream[to] * wide(gain[to], lanes) - plain - normed * mixed) * inv_std
        at = to.start % share
        parts[to.start // share, at : at + SUB] = result.astype(bf16)


def normalize_chunk(full, act, first, mean, inv_std, gain, shift):
    lanes = full.shape[1]
    for _, to in subs(first):
        normed = (full[to].astype(f32) - mean) * inv_std
        act[to] = (normed * wide(gain[to], lanes) + wide(shift[to], lanes)).astype(bf16)


def spread_rows(value, parts, first):
    share = parts.shape[1]
    for part, to in subs(first):
        at = to.start % share
        parts[to.start // share, at : at + SUB] = value[part].astype(bf16)


def whole_spec(shape):
    return pl.BlockSpec(shape, lambda *_: (0,) * len(shape))


def cols_spec(height, block):
    return pl.BlockSpec((height, block), lambda i, *_: (0, i))


def image_spec(image, height, block):
    return pl.BlockSpec((1, height, block), lambda i, *_: (image, 0, i))


def fixed_spec(shape):
    return pl.BlockSpec(shape, lambda *_: (0,) * len(shape), pipeline_mode=pl.Buffered(1))


def call(body, grid, in_specs, out_specs, out_shape, scratch, name, args, back=Quiet(), vmem=48):
    count = len(out_shape)

    def kernel(*refs):
        ins, refs = take(refs, len(args))
        back_ins, refs = take(refs, len(back.ins))
        outs, refs = take(refs, count)
        back_outs, refs = take(refs, len(back.out_shape))
        own, back_scratch = take(refs, len(scratch))
        body(back.steps(back_ins, back_outs, back_scratch), *ins, *outs, *own)

    shapes = list(out_shape) + list(back.out_shape)
    params = dict(vmem_limit_bytes=vmem << 20)
    if back.ident is not None:
        params.update(collective_id=back.ident, has_side_effects=True)
    out = pl.pallas_call(
        kernel,
        grid=grid,
        in_specs=list(in_specs) + [ANY] * len(back.ins),
        out_specs=list(out_specs) + [ANY] * len(back.out_shape),
        scratch_shapes=list(scratch) + list(back.scratch),
        out_shape=[jax.ShapeDtypeStruct(s, d) for s, d in shapes],
        compiler_params=pltpu.CompilerParams(**params),
        cost_estimate=pl.CostEstimate(flops=1 << 20, bytes_accessed=1 << 16, transcendentals=0),
        name=name,
    )(*args, *back.ins)
    return out if back.ident is None else (out[:count], back.split(out[count:]))


def qkv_kernel(steps, *refs):
    run_step(steps, pl.program_id(0))
    pieces, (gain, shift, own, other), (full, act), outs, mixed = (
        refs[:4],
        refs[4:8],
        refs[8:10],
        refs[10:14],
        refs[14],
    )
    spot, z = spots()
    assemble(spot, pieces, full)
    normalize(full, act, gain, shift)
    half = own.shape[1]
    product = mm(own[...], act[0:half]) + mm(other[...], act[half:])
    mixed[...] = product.astype(bf16).reshape(mixed.shape)
    rows = mixed.shape[1]
    for s in range(4):
        head = xor4(z, s)
        for k, part in enumerate((1, 2, 0)):
            outs[s][k * rows : (k + 1) * rows] = mixed[part * 4 + head]
    pl.when(pl.program_id(0) == pl.num_programs(0) - 1)(steps.get("end", lambda: None))


def qkv_call(image, pieces, gain, shift, own, other, hd, back, name):
    _, share, tokens = pieces[0].shape
    width = gain.shape[0]
    total = own.shape[0]
    block = 256
    return call(
        qkv_kernel,
        (tokens // block,),
        [image_spec(image, share, block)] * 4
        + [fixed_spec(gain.shape)] * 2
        + [fixed_spec(own.shape)] * 2,
        [cols_spec(width, block)] * 2 + [cols_spec(3 * hd, block)] * 4,
        [((width, tokens), bf16)] * 2 + [((3 * hd, tokens), bf16)] * 4,
        [pltpu.VMEM((total // hd, hd, block), bf16)],
        name,
        (*pieces, gain, shift, own, other),
        back,
        vmem=24,
    )


def mlp_kernel(steps, heads, full, cots, *refs):
    gain, shift, proj, up, down = refs[:5]
    act2, cot, hidden, grad_pre, keep_f, send_f, keep_b, send_b, sums, mid_own, joined = refs[5:16]
    mixed, mid, upstream, parts, parts_f = refs[16:21]
    step_at = pl.program_id(0)
    run_step(steps, step_at)
    spot, z = spots()
    for r in range(4):
        for s in range(4):
            mixed[r, xor4(z, s)] = heads[r, s]
    joined[...] = mixed[0].reshape(joined.shape)
    assemble(spot, [cots.at[r, 0] for r in range(4)], cot)
    width, lanes = mid.shape
    hid = hidden.shape[0]
    attn = mixed[...].reshape(width, lanes)
    zero = jnp.zeros((8, lanes), f32)

    @pl.when(step_at == 0)
    def _():
        sums[...] = jnp.zeros_like(sums)

    total = zero
    for first in range(0, width, CHUNK):
        product = mm(proj[:, first : first + CHUNK], attn, TN)
        for part, to in subs(first):
            value = product[part] + full[to].astype(f32)
            mid[to] = value
            total += fold8(value)
    mean = jnp.sum(total, axis=0, keepdims=True) * (1.0 / width)
    share = mid_own.shape[0]
    mid_own[...] = mid[pl.ds(pl.multiple_of(spot * share, share), share)]
    total = zero
    for first in range(0, width, SUB):
        center = mid[first : first + SUB] - mean
        total += fold8(center * center)
    inv_std = lax.rsqrt(jnp.sum(total, axis=0, keepdims=True) * (1.0 / width) + epsilon)
    for first in range(0, width, CHUNK):
        upstream[first : first + CHUNK] = mm(down[first : first + CHUNK], cot[...])
        normalize_chunk(mid, act2, first, mean, inv_std, gain, shift)
    for first in range(0, hid, CHUNK):
        pre_all = mm(up[:, first : first + CHUNK], act2[...], TN)
        for part, to in subs(first):
            pre = pre_all[part]
            cdf, density = gelu_parts(pre)
            hidden[to] = (pre * cdf).astype(bf16)
            grad_pre[to] = (upstream[to] * (cdf + pre * density)).astype(bf16)
    state = (zero, zero)
    for first in range(0, width, CHUNK):
        up_all = mm(up[first : first + CHUNK], grad_pre[...])
        state = gather_chunk(state, up_all, first, mid, mean, inv_std, gain, sums, upstream)
    stats = finish_stats(state, width)
    for first in range(0, width, CHUNK):
        spread_rows(mm(down[:, first : first + CHUNK], hidden[...], TN), parts_f, first)
        write_chunk(parts, first, upstream, mid, mean, inv_std, gain, stats)
    spread(parts_f, spot, keep_f, send_f)
    spread(parts, spot, keep_b, send_b)
    pl.when(step_at == pl.num_programs(0) - 1)(steps.get("end", lambda: None))


def mlp_call(image, heads, full, cots, gain, shift, proj, up, down, back):
    width, tokens = full.shape
    hid = up.shape[1]
    share = width // 4
    hd = heads.shape[2]
    block = 256
    half = width // 2
    return call(
        mlp_kernel,
        (tokens // block,),
        [
            pl.BlockSpec((4, 4, hd, block), lambda i: (0, 0, 0, i)),
            cols_spec(width, block),
        ]
        + [pl.BlockSpec((4, 1, share, block), lambda i: (0, image, 0, i))]
        + [fixed_spec(gain.shape)] * 2
        + [fixed_spec(proj.shape), fixed_spec(up.shape), fixed_spec(down.shape)],
        [cols_spec(width, block)] * 2
        + [cols_spec(hid, block)] * 2
        + [cols_spec(half, block)] * 4
        + [whole_spec((2, width, 128)), cols_spec(share, block), cols_spec(4 * hd, block)],
        [((width, tokens), bf16)] * 2
        + [((hid, tokens), bf16)] * 2
        + [((half, tokens), bf16)] * 4
        + [((2, width, 128), f32), ((share, tokens), f32), ((4 * hd, tokens), bf16)],
        [
            pltpu.VMEM((4, 4, hd, block), bf16),
            pltpu.VMEM((width, block), f32),
            pltpu.VMEM((width, block), f32),
            pltpu.VMEM((4, share, block), bf16),
            pltpu.VMEM((4, share, block), bf16),
        ],
        "mlp%d" % image,
        (heads, full, cots, gain, shift, proj, up, down),
        back,
    )


def gattn_kernel(_, full, weight, *refs):
    outs, mixed = refs[:4], refs[4]
    _, z = spots()
    mixed[...] = mm(weight[...], full[...]).astype(bf16).reshape(mixed.shape)
    for s in range(4):
        outs[s][...] = mixed[xor4(z, s)]


def gattn_call(full, weight, hd):
    width, tokens = full.shape
    total = weight.shape[0]
    block = 256
    return call(
        gattn_kernel,
        (tokens // block,),
        [cols_spec(width, block), fixed_spec(weight.shape)],
        [cols_spec(hd, block)] * 4,
        [((hd, tokens), bf16)] * 4,
        [pltpu.VMEM((total // hd, hd, block), bf16)],
        "gattn",
        (full, weight),
        vmem=20,
    )


def gin_block(joined, full, gain, own, other, sums, upstream, parts):
    half = own.shape[1]
    width, lanes = full.shape
    mean, inv_std = moments(full)
    zero = jnp.zeros((8, lanes), f32)
    state = (zero, zero)
    step = 128
    for first in range(0, width, CHUNK):
        ups = []
        for n in range(first, first + CHUNK, step):
            weight = own if n < half else other
            ups.append(mm(weight[:, n % half : n % half + step], joined, TN))
        up_all = jnp.concatenate(ups, axis=0)
        state = gather_chunk(state, up_all, first, full, mean, inv_std, gain, sums, upstream)
    stats = finish_stats(state, width)
    for first in range(0, width, CHUNK):
        write_chunk(parts, first, upstream, full, mean, inv_std, gain, stats)


def tail_kernel(_, *refs):
    pieces, (full_0, act_0, gain, own, other, small_in), refs = refs[:4], refs[4:10], refs[10:]
    sends, (full_any, act_any, proj_any), refs = refs[:4], refs[4:7], refs[7:]
    (out_0, out_1, out_w, out_small, out_p), refs = refs[:5], refs[5:]
    (mixed, got, full_1, act_1, total, low, upstream, parts, block, sums), refs = refs[:10], refs[10:]
    (keep, send, from_core, from_x, exact, from_y, from_z, exact_w, small, hops), refs = (
        refs[:10],
        refs[10:],
    )
    (mine_p, got_p, from_p, exact_p), refs = refs[:4], refs[4:]
    send_sem, recv_sem, local_sem = refs
    sems = (send_sem, recv_sem)
    spot, z = spots()
    core = lax.rem(spot, 2)
    tokens = mixed.shape[2]
    rows = mixed.shape[1]
    width = full_0.shape[0]
    half = width // 2
    share = half // 2
    lanes = block.shape[1]
    chunk = half // 4

    greet([peer(*p) for p in CTX_PEERS + TP_PEERS + Y_PEERS])

    def swaps():
        return [remote(sends[s], got.at[s], sems, s - 1, peer("ctx", s)) for s in (3, 2, 1)]

    def loads():
        return [
            pltpu.make_async_copy(sends[0], got.at[0], local_sem.at[0]),
            pltpu.make_async_copy(full_any, full_1, local_sem.at[1]),
            pltpu.make_async_copy(act_any, act_1, local_sem.at[2]),
        ]

    def proj_y():
        return remote(proj_any.at[half:], got_p, sems, 19, peer("fsdp", 1))

    def proj_load():
        return pltpu.make_async_copy(proj_any.at[:half], mine_p, local_sem.at[7])

    def proj_z(s):
        source = mine_p.at[pl.ds(pl.multiple_of(xor4(z, s) * chunk, 16), chunk)]
        return remote(source, from_p.at[s], sems, 19 + s, peer("ctx", s))

    start_all(swaps() + loads() + [proj_y(), proj_load()])
    sums[...] = jnp.zeros_like(sums)

    def join(source):
        for s in range(4):
            head = xor4(z, s)
            for k, part in enumerate((1, 2, 0)):
                mixed[part * 4 + head] = source(s)[k * rows : (k + 1) * rows]

    def all_blocks(full, image):
        def advance(b, carry):
            at = pl.ds(pl.multiple_of(b * lanes, lanes), lanes)
            block[...] = full[:, at]
            joined = mixed[:, :, at].reshape(mixed.shape[0] * rows, lanes)
            gin_block(joined, block, gain, own, other, sums, upstream, parts)
            for n in range(2):
                to = slice(n * share, (n + 1) * share)
                keep[image, to, at] = parts[2 * n + core]
                send[image, to, at] = parts[2 * n + 1 - core]
            return carry

        lax.fori_loop(0, tokens // lanes, advance, 0)

    def core_copy(image):
        return remote(send.at[image], from_core.at[image], sems, 3 + image, peer("tp", 1))

    first = lax.div(spot, 2) * share
    second = share - first

    def x_copy(image):
        source = keep.at[image, pl.ds(pl.multiple_of(second, share), share)]
        return remote(source, from_x.at[image], sems, 5 + image, peer("tp", 2))

    def add_core(image):
        core_copy(image).wait()

        def add(at):
            keep[image, at] = (
                keep[image, at].astype(f32) + from_core[image, at].astype(f32)
            ).astype(bf16)

        add_rows(half, add)
        x_copy(image).start()

    def add_x(image):
        x_copy(image).wait()

        def add(n, carry):
            at = pl.ds(pl.multiple_of(n * 16, 16), 16)
            mine = pl.ds(pl.multiple_of(first + n * 16, 16), 16)
            exact[image, at] = keep[image, mine].astype(f32) + from_x[image, at].astype(f32)
            return carry

        lax.fori_loop(0, share // 16, add, 0)

    def out_copy(image, out):
        return pltpu.make_async_copy(exact.at[image], out, local_sem.at[3 + image])

    def y_copy(s):
        place = pl.multiple_of(half + xor4(z, s) * chunk, 16)
        return remote(low.at[pl.ds(place, chunk)], from_y.at[s], sems, 7 + s, peer("fsdp", 1))

    def z_copy(s):
        return remote(from_y.at[s], from_z.at[s], sems, 10 + s, peer("ctx", s))

    def product(act, at):
        return mm(act[at], mixed[...].reshape(mixed.shape[0] * rows, tokens), NT)

    step = 128

    def weight_first(n, carry):
        at = pl.ds(pl.multiple_of(n * step, step), step)
        total[at] = product(act_0, at)
        return carry

    def weight_second(n, carry):
        at = pl.ds(pl.multiple_of(n * step, step), step)
        low[at] = (total[at] + product(act_1, at)).astype(bf16)
        return carry

    join(lambda s: pieces[s])
    all_blocks(full_0, 0)
    core_copy(0).start()
    lax.fori_loop(0, width // step, weight_first, 0)
    add_core(0)
    wait_all([proj_load(), proj_y()])

    def add_p(at):
        mine_p[at] = (mine_p[at].astype(f32) + got_p[at].astype(f32)).astype(bf16)

    add_rows(half, add_p)
    wait_all(swaps() + loads())
    start_all([proj_z(s) for s in (3, 2, 1)])
    join(lambda s: got.at[s])
    lax.fori_loop(half // step, width // step, weight_second, 0)
    start_all([y_copy(s) for s in (3, 2, 1, 0)])
    lax.fori_loop(0, half // step, weight_second, 0)
    add_x(0)
    out_copy(0, out_0).start()
    all_blocks(full_1, 1)
    core_copy(1).start()
    small[0:288] = small_in[...]
    y = lax.axis_index("fsdp")
    for n in range(2):
        line = jnp.sum(jnp.transpose(sums[n]), axis=0, keepdims=True)
        line = jnp.where(y == 0, line, jnp.concatenate([line[:, half:], line[:, :half]], axis=1))
        for k in range(width // 128):
            small[288 + n * 16 + k : 289 + n * 16 + k] = line[:, k * 128 : (k + 1) * 128]
    def hop(k, axis, bit):
        return remote(small, hops.at[k], sems, 14 + k, peer(axis, bit))

    route = TP_PEERS + CTX_PEERS[:2] + Y_PEERS

    def hop_end(k):
        hop(k, *route[k]).wait()
        small[...] += hops[k]

    hop(0, *route[0]).start()
    for n, s in enumerate((3, 2, 1)):
        y_copy(s).wait()

        def add(at, s=s):
            mine = low[pl.ds(pl.multiple_of(xor4(z, s) * chunk + at.start, 16), at.size)]
            from_y[s, at] = (from_y[s, at].astype(f32) + mine.astype(f32)).astype(bf16)

        add_rows(chunk, add)
        z_copy(s).start()
        hop_end(n)
        hop(n + 1, *route[n + 1]).start()
        if n == 0:
            add_core(1)
    hop_end(3)
    hop(4, *route[4]).start()
    wait_all([proj_z(s) for s in (3, 2, 1)])

    def last_p(at):
        mine = mine_p[pl.ds(pl.multiple_of(z * chunk + at.start, 16), at.size)].astype(f32)
        exact_p[at] = (mine + from_p[1, at].astype(f32)) + (
            from_p[2, at].astype(f32) + from_p[3, at].astype(f32)
        )

    add_rows(chunk, last_p)
    add_x(1)
    out_copy(1, out_1).start()
    y_copy(0).wait()
    hop_end(4)
    wait_all([z_copy(s) for s in (3, 2, 1)])

    def add_last(at):
        mine = low[pl.ds(pl.multiple_of(z * chunk + at.start, 16), at.size)].astype(f32)
        exact_w[at] = ((mine + from_y[0, at].astype(f32)) + from_z[1, at].astype(f32)) + (
            from_z[2, at].astype(f32) + from_z[3, at].astype(f32)
        )

    add_rows(chunk, add_last)
    lasts = [
        pltpu.make_async_copy(exact_w, out_w, local_sem.at[5]),
        pltpu.make_async_copy(small, out_small, local_sem.at[6]),
        pltpu.make_async_copy(exact_p, out_p, local_sem.at[8]),
    ]
    start_all(lasts)
    wait_all(lasts + [out_copy(0, out_0), out_copy(1, out_1)])


def tail_call(pieces, full_0, act_0, gain, own, other, small, sends, full_1, act_1, proj, hd, ident):
    part_rows, tokens = pieces[0].shape
    width = gain.shape[0]
    total = own.shape[0]
    half = width // 2
    share = half // 2
    block = 256
    ins = (*pieces, full_0, act_0, gain, own, other, small)
    anys = (*sends, full_1, act_1, proj)
    cols = proj.shape[1]
    scratch = [
        pltpu.VMEM((total // hd, hd, tokens), bf16),
        pltpu.VMEM((4, part_rows, tokens), bf16),
        pltpu.VMEM((width, tokens), bf16),
        pltpu.VMEM((width, tokens), bf16),
        pltpu.VMEM((width, total), f32),
        pltpu.VMEM((width, total), bf16),
        pltpu.VMEM((width, block), f32),
        pltpu.VMEM((4, share, block), bf16),
        pltpu.VMEM((width, block), bf16),
        pltpu.VMEM((2, width, 128), f32),
        pltpu.VMEM((2, half, tokens), bf16),
        pltpu.VMEM((2, half, tokens), bf16),
        pltpu.VMEM((2, half, tokens), bf16),
        pltpu.VMEM((2, share, tokens), bf16),
        pltpu.VMEM((2, share, tokens), f32),
        pltpu.VMEM((4, half // 4, total), bf16),
        pltpu.VMEM((4, half // 4, total), bf16),
        pltpu.VMEM((half // 4, total), f32),
        pltpu.VMEM((320, 128), f32),
        pltpu.VMEM((5, 320, 128), f32),
        pltpu.VMEM((half, cols), bf16),
        pltpu.VMEM((half, cols), bf16),
        pltpu.VMEM((4, half // 4, cols), bf16),
        pltpu.VMEM((half // 4, cols), f32),
        dma(23),
        dma(23),
        dma(9),
    ]
    return pl.pallas_call(
        functools.partial(tail_kernel, None),
        in_specs=[pl.BlockSpec(memory_space=pltpu.VMEM)] * len(ins) + [ANY] * len(anys),
        out_specs=[ANY] * 5,
        scratch_shapes=scratch,
        out_shape=[
            jax.ShapeDtypeStruct((share, tokens), f32),
            jax.ShapeDtypeStruct((share, tokens), f32),
            jax.ShapeDtypeStruct((half // 4, total), f32),
            jax.ShapeDtypeStruct((320, 128), f32),
            jax.ShapeDtypeStruct((half // 4, cols), f32),
        ],
        compiler_params=pltpu.CompilerParams(
            vmem_limit_bytes=60 << 20, collective_id=ident, has_side_effects=True
        ),
        cost_estimate=pl.CostEstimate(flops=1 << 20, bytes_accessed=1 << 16, transcendentals=0),
        name="tail",
    )(*ins, *anys)


def band_start(place, chunk, size, band):
    return xor4(place, lax.div(chunk * size, band)) * band + lax.rem(chunk * size, band)


def fwd_kernel(dims, steps, *refs):
    hd, side, scale = dims
    _, place = spots()
    pieces, table = refs[:4], refs[4]
    outs, kvq, exact, lse, qa = refs[5:9], refs[9], refs[10], refs[11], refs[12]
    ka, va, low = refs[13:16]
    band = pieces[0].shape[1]
    seq = kvq.shape[1]
    step = 512
    bq, bk = band, 1024
    for s in range(4):
        kvq[:, s * band : (s + 1) * band] = pieces[s][...]
    lane = lax.broadcasted_iota(jnp.int32, (step, 128), 1)
    row = lax.broadcasted_iota(jnp.int32, (step, 128), 0)
    lane_side = lax.broadcasted_iota(jnp.int32, (side, 128), 1)
    row16 = lax.broadcasted_iota(jnp.int32, (16, step), 0)
    pad = jnp.zeros((128 - hd, step), bf16)

    def prepare(c, carry):
        at = pl.ds(pl.multiple_of(c * step, step), step)
        start = band_start(place, c, step, band)
        keys = jnp.transpose(jnp.concatenate([kvq[0:hd, at], pad], axis=0).astype(f32))
        ka[at, 0:128] = keys.astype(bf16)
        pos = row + start
        want = jnp.where(lane < side, lax.div(pos, side), lax.rem(pos, side) + side)
        ka[at, 128:256] = jnp.where(want == lane, 1.0, 0.0).astype(bf16)
        va[0:hd, at] = kvq[hd : 2 * hd, at]
        va[hd : hd + 16, at] = jnp.where(row16 == 0, 1.0, 0.0).astype(bf16)
        queries = jnp.concatenate([kvq[2 * hd : 3 * hd, at], pad], axis=0)
        qa[0:128, at] = (queries.astype(f32) * (scale * LOG2E)).astype(bf16)
        terms = lax.dot_general(queries, table[...], (((0,), (1,)), ((), ())), preferred_element_type=f32)
        parts = []
        for r in range(step // side):
            y = lax.div(start, side) + r
            by_row = terms[r * side : (r + 1) * side, 0:128]
            by_col = terms[r * side : (r + 1) * side, 128:256]
            by_row = pltpu.roll(by_row, lax.rem(side + 1 + y, 128), 1)
            by_col = pltpu.roll(by_col, 1, 1, stride=1, stride_axis=0)
            parts.append(jnp.where(lane_side < side, by_row, by_col))
        rel = jnp.concatenate(parts, axis=0) * LOG2E
        qa[128:256, at] = jnp.transpose(rel).astype(bf16)
        return carry

    lax.fori_loop(0, seq // step, prepare, 0)

    def queries_loop(i, carry):
        at = pl.ds(pl.multiple_of(i * bq, bq), bq)
        q_block = qa[:, at]

        def keys_loop(j, state):
            peak, total = state
            run_step(steps, i * (seq // bk) + j)
            keys = pl.ds(pl.multiple_of(j * bk, bk), bk)
            logits = mm(ka[keys, :], q_block)
            new_peak = jnp.maximum(peak, jnp.max(logits, axis=0, keepdims=True))
            weights = jnp.exp2(logits - new_peak).astype(bf16)
            total = total * jnp.exp2(peak - new_peak) + mm(va[:, keys], weights)
            return new_peak, total

        peak, total = lax.fori_loop(
            0,
            seq // bk,
            keys_loop,
            (jnp.full((1, bq), lowest, f32), jnp.zeros((hd + 16, bq), f32)),
        )
        denom = total[hd : hd + 1]
        value = total[0:hd] / denom
        exact[:, at] = value
        low[:, at] = value.astype(bf16)
        lse[:, at] = jnp.broadcast_to(peak + jnp.log2(denom), (8, bq))
        return carry

    lax.fori_loop(0, seq // bq, queries_loop, 0)
    for s in range(4):
        outs[s][...] = low[:, s * band : (s + 1) * band]
    steps.get("end", lambda: None)()


def fwd_call(pieces, table, hd, side, back, name):
    rows, band = pieces[0].shape
    seq = 4 * band
    return call(
        functools.partial(fwd_kernel, (hd, side, hd ** (-0.5))),
        (1,),
        [fixed_spec((rows, band))] * 4 + [fixed_spec(table.shape)],
        [fixed_spec((hd, band))] * 4
        + [fixed_spec((rows, seq)), fixed_spec((hd, seq)), fixed_spec((8, seq)), fixed_spec((256, seq))],
        [((hd, band), bf16)] * 4
        + [((rows, seq), bf16), ((hd, seq), f32), ((8, seq), f32), ((256, seq), bf16)],
        [
            pltpu.VMEM((seq, 256), bf16),
            pltpu.VMEM((hd + 16, seq), bf16),
            pltpu.VMEM((hd, seq), bf16),
        ],
        name,
        (*pieces, table),
        back,
        vmem=36,
    )


def split3(value):
    high = value.astype(bf16).astype(f32)
    rest = value - high
    mid = rest.astype(bf16).astype(f32)
    return high, mid, rest - mid


def bwd_kernel(dims, steps, *refs):
    hd, side, scale = dims
    _, place = spots()
    grads, kvq, qa_in, exact, lse, table = refs[:4], refs[4], refs[5], refs[6], refs[7], refs[8]
    outs, dtab = refs[9:13], refs[13]
    ka, kt, va, qa, da, qn, dn, dk, dv, res = refs[14:24]
    band = grads[0].shape[1]
    seq = kvq.shape[1]
    step = 512
    bq, bk = band, 1024
    for s in range(4):
        da[0:hd, s * band : (s + 1) * band] = grads[s][...]
    lane = lax.broadcasted_iota(jnp.int32, (step, 128), 1)
    row = lax.broadcasted_iota(jnp.int32, (step, 128), 0)
    lane_side = lax.broadcasted_iota(jnp.int32, (side, 128), 1)
    extra = lax.broadcasted_iota(jnp.int32, (128 - hd, step), 0)
    pad = jnp.zeros((128 - hd, step), bf16)
    ones = (lane >= hd) & (lane < hd + 3)

    def turned(value):
        return jnp.transpose(jnp.concatenate([value, pad], axis=0).astype(f32))

    def special(value):
        high, mid, rest = split3(value)
        picked = jnp.where(extra == 0, high, jnp.where(extra == 1, mid, jnp.where(extra == 2, rest, 0.0)))
        return picked.astype(bf16)

    def prepare(c, carry):
        at = pl.ds(pl.multiple_of(c * step, step), step)
        start = band_start(place, c, step, band)
        k_part = kvq[0:hd, at]
        q_part = kvq[2 * hd : 3 * hd, at]
        kt[0:128, at] = jnp.concatenate([k_part, pad], axis=0)
        ka[at, 0:128] = jnp.where(ones, 1.0, turned(k_part)).astype(bf16)
        pos = row + start
        want = jnp.where(lane < side, lax.div(pos, side), lax.rem(pos, side) + side)
        ka[at, 128:256] = jnp.where(want == lane, 1.0, 0.0).astype(bf16)
        want = jnp.where(lane < side, lax.div(pos, side), 2 * side - 1 - lax.rem(pos, side))
        kt[128:256, at] = jnp.transpose(jnp.where(want == lane, 1.0, 0.0)).astype(bf16)
        va[at, :] = jnp.where(ones, 1.0, turned(kvq[hd : 2 * hd, at])).astype(bf16)
        dk[at, :] = jnp.zeros((step, 128), f32)
        dv[at, :] = jnp.zeros((step, 128), f32)
        d_part = da[0:hd, at]
        qn[at, :] = turned(q_part).astype(bf16)
        dn[at, :] = turned(d_part).astype(bf16)
        delta = jnp.sum(d_part.astype(f32) * exact[:, at], axis=0, keepdims=True)
        qa[0:hd, at] = qa_in[0:hd, at]
        qa[hd:128, at] = special(-lse[0:1, at])
        qa[128:256, at] = qa_in[128:256, at]
        da[hd:128, at] = special(-delta)
        return carry

    lax.fori_loop(0, seq // step, prepare, 0)
    dtab[...] = jnp.zeros_like(dtab)

    def queries_loop(i, carry):
        at = pl.ds(pl.multiple_of(i * bq, bq), bq)
        qa_i, da_i, qn_i, dn_i = qa[:, at], da[:, at], qn[at, :], dn[at, :]

        def keys_loop(j, total):
            run_step(steps, i * (seq // bk) + j)
            keys = pl.ds(pl.multiple_of(j * bk, bk), bk)
            probs = jnp.exp2(mm(ka[keys, :], qa_i))
            grad_logits = (probs * mm(va[keys, :], da_i)).astype(bf16)
            dv[keys, :] += mm(probs.astype(bf16), dn_i)
            dk[keys, :] += mm(grad_logits, qn_i)
            return total + mm(kt[:, keys], grad_logits)

        total = lax.fori_loop(0, seq // bk, keys_loop, jnp.zeros((256, bq), f32))
        rel = jnp.transpose(total[128:256])
        start = band_start(place, i, bq, band)
        parts = []
        for r in range(bq // side):
            y = lax.div(start, side) + r
            block = rel[r * side : (r + 1) * side]
            by_row = jnp.where(lane_side < side, block, 0.0)
            by_col = jnp.where(lane_side < side, 0.0, block)
            by_row = pltpu.roll(by_row, lax.rem(side + 127 - y, 128), 1)
            by_col = pltpu.roll(by_col, side + 1, 1, stride=1, stride_axis=0)
            parts.append(jnp.concatenate([by_row, by_col], axis=1))
        moved = jnp.concatenate(parts, axis=0).astype(bf16)
        dq = total[0:128] * scale + lax.dot_general(
            table[...], moved, (((0,), (1,)), ((), ())), preferred_element_type=f32
        )
        res[2 * hd : 3 * hd, at] = dq[0:hd].astype(bf16)
        dtab[...] += mm(moved, qn_i, TN)
        return carry

    lax.fori_loop(0, seq // bq, queries_loop, 0)

    def finish(c, carry):
        at = pl.ds(pl.multiple_of(c * step, step), step)
        res[0:hd, at] = jnp.transpose(dk[at, :] * scale)[0:hd].astype(bf16)
        res[hd : 2 * hd, at] = jnp.transpose(dv[at, :])[0:hd].astype(bf16)
        return carry

    lax.fori_loop(0, seq // step, finish, 0)
    for s in range(4):
        outs[s][...] = res[:, s * band : (s + 1) * band]
    steps.get("end", lambda: None)()


def bwd_call(grads, kvq, qa, exact, lse, table, hd, side, back, name):
    rows, seq = kvq.shape
    band = seq // 4
    return call(
        functools.partial(bwd_kernel, (hd, side, hd ** (-0.5))),
        (1,),
        [fixed_spec((hd, band))] * 4
        + [fixed_spec(a.shape) for a in (kvq, qa, exact, lse, table)],
        [fixed_spec((rows, band))] * 4 + [fixed_spec((256, 128))],
        [((rows, band), bf16)] * 4 + [((256, 128), f32)],
        [
            pltpu.VMEM((seq, 256), bf16),
            pltpu.VMEM((256, seq), bf16),
            pltpu.VMEM((seq, 128), bf16),
            pltpu.VMEM((256, seq), bf16),
            pltpu.VMEM((128, seq), bf16),
            pltpu.VMEM((seq, 128), bf16),
            pltpu.VMEM((seq, 128), bf16),
            pltpu.VMEM((seq, 128), f32),
            pltpu.VMEM((seq, 128), f32),
            pltpu.VMEM((rows, seq), bf16),
        ],
        name,
        (*grads, kvq, qa, exact, lse, table),
        back,
        vmem=60,
    )


def offset_rows(index, table):
    side = index.shape[0]
    picks = jnp.concatenate([index[::-1, 0], index[0, 1:]])
    hot = (picks[:, None] == jnp.arange(table.shape[0], dtype=jnp.int32)[None, :]).astype(f32)
    rows = jnp.dot(hot, table.astype(f32), precision=highest)
    return hot, jnp.pad(rows, ((0, 1), (0, 128 - table.shape[1]))).astype(bf16)


def fast_device(
    block_input,
    cotangent,
    norm1_gain,
    norm1_shift,
    w_qkv,
    table_rows,
    table_cols,
    w_proj,
    norm2_gain,
    norm2_shift,
    w_fc1,
    w_fc2,
    index_rows,
    index_cols,
):
    images, band_len, share = block_input.shape
    hd = table_rows.shape[1]
    side = index_rows.shape[0]
    width = norm1_gain.shape[0]
    half = width // 2
    heads = w_proj.shape[0] // hd
    t = lax.axis_index("tp")
    z = lax.axis_index("ctx")
    y = lax.axis_index("fsdp")
    spot = t ^ (2 * y)
    first = lax.div(spot, 2) == 0

    def halves(vector):
        return jnp.where(y == 0, vector, jnp.roll(vector, half, axis=-1))

    def lanes(vector):
        return jnp.broadcast_to(halves(vector)[:, None], (width, 128))

    gain1, shift1 = lanes(norm1_gain), lanes(norm1_shift)
    gain2, shift2 = lanes(norm2_gain), lanes(norm2_shift)

    tokens_in = jnp.swapaxes(block_input, 1, 2)
    grads_in = jnp.swapaxes(cotangent, 1, 2)
    own_qkv = jnp.transpose(w_qkv, (1, 2, 0)).reshape(3 * heads * hd, half)
    other_qkv = pxor(own_qkv, "fsdp", 1)
    inputs = tuple(gather_tp(tokens_in))
    hot_rows, shifted_rows = offset_rows(index_rows, table_rows)
    hot_cols, shifted_cols = offset_rows(index_cols, table_cols)
    table = jnp.concatenate([shifted_rows, shifted_cols], axis=0)
    back_table = jnp.concatenate(
        [shifted_rows, jnp.zeros((1, 128), bf16), shifted_cols[:127][::-1]], axis=0
    )

    def reduce_tp(keep, send):
        got = keep.astype(f32) + pxor(send, "tp", 1).astype(f32)
        mine = jnp.where(first, got[:share], got[share:])
        other = jnp.where(first, got[share:], got[:share]).astype(bf16)
        return mine + pxor(other, "tp", 2).astype(f32)

    state = [{} for _ in range(images)]
    token = [None]

    def ordered(values):
        return values if token[0] is None else after(values, token[0])

    def do_qkv(m, back):
        st = state[m]
        pieces = ordered(inputs)
        out = qkv_call(m, pieces, gain1, shift1, own_qkv, other_qkv, hd, back, "qkv%d" % m)
        out, extra = out if back.ident is not None else (out, ())
        st["full"], st["act1"], *st["mixed"] = out
        token[0] = st["mixed"][0]
        return extra

    def do_fwd(m, back):
        st = state[m]
        pieces = ordered(tuple(st["mixed"]))
        out, extra = fwd_call(pieces, table, hd, side, back, "attn_fwd%d" % m)
        *st["attn"], st["kvq"], st["exact"], st["lse"], st["qa"] = out
        token[0] = st["lse"]
        return extra

    def do_mlp(m, back):
        st = state[m]
        heads_all = ordered(st["heads"])
        out, extra = mlp_call(
            m, heads_all, st["full"], cots, gain2, shift2, full_proj, full_up, full_down, back
        )
        st["act2"], st["cot"], st["hidden"], st["grad_pre"] = out[:4]
        st["forward"], st["backward"] = out[4:6], out[6:8]
        st["sums2"], st["middle"], st["joined"] = out[8:]
        token[0] = out[8]
        return extra

    def do_gattn(m):
        st = state[m]
        branch = ordered(st["branch"])
        grads = gattn_call(branch, own_proj, hd)
        token[0] = grads[0]
        st["grads"] = swap_ctx(grads)

    def do_bwd(m, back):
        st = state[m]
        pieces = ordered(tuple(st["grads"]))
        out, extra = bwd_call(
            pieces,
            st["kvq"],
            st["qa"],
            st["exact"],
            st["lse"],
            back_table,
            hd,
            side,
            back,
            "attn_bwd%d" % m,
        )
        *st["grad_mixed"], st["dtab"] = out
        token[0] = st["dtab"]
        return extra

    def do_wgrad(left, right):
        parts = [state[m][left] for m in range(images)], [state[m][right] for m in range(images)]
        lefts, rights = ordered((tuple(parts[0]), tuple(parts[1])))
        total = sum(mm(a, b, NT) for a, b in zip(lefts, rights)).astype(bf16)
        token[0] = total
        return total

    first_image, second_image = state
    do_qkv(0, Quiet())
    got, (own_proj,), (cots,) = do_qkv(
        1,
        Together(
            0,
            SwapCtx(first_image["mixed"]),
            JoinY(w_proj, 1),
            GatherTp(grads_in, (0, 3, "end")),
        ),
    )
    first_image["mixed"] = first_image["mixed"][:1] + list(got)
    got, (full_up,), (full_proj,) = do_fwd(
        0,
        Together(
            1,
            SwapCtx(second_image["mixed"]),
            JoinY(w_fc1, 0),
            GatherTp(own_proj, (0, 10, "end")),
        ),
    )
    full_proj = full_proj.reshape(width, width)
    second_image["mixed"] = second_image["mixed"][:1] + list(got)
    (first_image["heads"],), (full_down,) = do_fwd(
        1,
        Together(
            2,
            SpreadHeads(first_image["attn"], (0, 8, "end", "end")),
            JoinY(w_fc2, 1),
        ),
    )
    ((second_image["heads"],),) = do_mlp(
        0, Together(7, SpreadHeads(second_image["attn"], (0, 2, "end", "end")))
    )
    ((first_image["branch"], first_image["grad_middle"]),) = do_mlp(
        1,
        Together(
            3, ReduceTp(*first_image["backward"], first_image["cot"], (0, 0, "end", "end", "end"))
        ),
    )
    do_gattn(0)
    up_total = do_wgrad("act2", "grad_pre")
    hid = full_down.shape[0]
    split = hid * 3 // 4
    for st in state:
        st["hidden_a"], st["hidden_b"] = st["hidden"][:split], st["hidden"][split:]
    down_total = do_wgrad("cot", "hidden_a")
    down_rest = do_wgrad("cot", "hidden_b")
    (branch, exact, *second_image["grads"]), (grad_down,), (up_low,) = do_bwd(
        0,
        Together(
            4,
            ReduceTp(
                *second_image["backward"], second_image["cot"], (0, 1, 10, 11, "end"), own_proj
            ),
            GradsZThenY(down_total, (0, 4, 10, "end")),
            GradsY(up_total, (0, 13, "end")),
        ),
    )
    second_image["branch"], second_image["grad_middle"] = branch, exact
    proj_total = do_wgrad("branch", "joined")
    (grad_up,), got, (total_0,), (total_1,) = do_bwd(
        1,
        Together(
            5,
            GradsZ(up_low, (0, 11, "end", "end")),
            SwapCtx(first_image["grad_mixed"]),
            ReduceShare(*first_image["forward"], (0, 1, 6, "end")),
            ReduceShare(*second_image["forward"], (6, 7, 12, "end")),
        ),
    )
    first_image["grad_mixed"] = first_image["grad_mixed"][:1] + list(got)
    for st, total in zip(state, (total_0, total_1)):
        st["output"] = (st["middle"] + total).astype(bf16)
    def pair(parts):
        return halves(jnp.sum(sum(parts), axis=2))

    early = pair([st["sums2"] for st in state]).reshape(-1, 128)
    early = jnp.pad(early, ((0, 32 - early.shape[0]), (0, 0)))
    tables = jnp.concatenate([sum(st["dtab"] for st in state), early], axis=0)
    total_0, total_1, grad_qkv, small, grad_rest = tail_call(
        *ordered(
            (
                tuple(first_image["grad_mixed"]),
                first_image["full"],
                first_image["act1"],
                gain1,
                own_qkv,
                other_qkv,
                tables,
                tuple(second_image["grad_mixed"]),
                second_image["full"],
                second_image["act1"],
                jnp.concatenate([proj_total, down_rest], axis=1),
            )
        ),
        hd,
        6,
    )
    token[0] = small
    outputs = [st["output"] for st in state]
    input_grads = [st["grad_middle"] + t for st, t in zip(state, (total_0, total_1))]
    grad_qkv = grad_qkv.reshape(half // 4, 3, heads * hd)

    norms2 = small[256 : 256 + 2 * width // 128].reshape(2, width)
    norms1 = jnp.stack(
        [small[288 + 16 * n : 288 + 16 * n + width // 128].reshape(width) for n in range(2)]
    )
    norms = jnp.concatenate([norms1, norms2], axis=0)
    tabs = small[:256]
    rows_grad = jnp.dot(hot_rows.T, tabs[:127, :hd], precision=highest)
    cols_grad = jnp.dot(hot_cols.T, tabs[129:256, :hd][::-1], precision=highest)
    return (
        jnp.swapaxes(jnp.stack(outputs), 1, 2),
        jnp.swapaxes(jnp.stack(input_grads), 1, 2),
        norms[0],
        norms[1],
        grad_qkv,
        rows_grad,
        cols_grad,
        grad_rest[:, : heads * hd].T,
        norms[2],
        norms[3],
        grad_up,
        jnp.concatenate([grad_down, grad_rest[:, heads * hd :]], axis=1).T,
    )


def per_device(*args):
    block_input, w_proj, table_rows, index_rows = args[0], args[7], args[5], args[12]
    heads = w_proj.shape[0] // table_rows.shape[1]
    fits = (
        lax.axis_size("tp") == 4
        and lax.axis_size("ctx") == 4
        and lax.axis_size("fsdp") == 2
        and heads == 4
        and index_rows.shape[0] == 64
        and table_rows.shape[1] == 80
        and block_input.shape[1] % 512 == 0
        and block_input.shape[0] == 2
    )
    return fast_device(*args) if fits else plain_device(*args)


def solution(mesh):
    in_specs = (
        P("fsdp", "ctx", "tp"),
        P("fsdp", "ctx", "tp"),
        P(),
        P(),
        P("fsdp", None, "tp"),
        P(),
        P(),
        P("tp", "fsdp"),
        P(),
        P(),
        P("fsdp", "tp"),
        P("tp", "fsdp"),
        P(),
        P(),
    )
    out_specs = (
        P("fsdp", "ctx", "tp"),
        P("fsdp", "ctx", "tp"),
        P(),
        P(),
        P(("fsdp", "ctx"), None, "tp"),
        P(),
        P(),
        P("tp", ("fsdp", "ctx")),
        P(),
        P(),
        P(("fsdp", "ctx"), "tp"),
        P("tp", ("fsdp", "ctx")),
    )
    return jax.shard_map(
        per_device, mesh=mesh, in_specs=in_specs, out_specs=out_specs, check_vma=False
    )
```

```python
import functools
import math

import jax
import jax.numpy as jnp
from jax import lax
from jax.experimental import pallas as pl
from jax.experimental.pallas import tpu as pltpu
from jax.sharding import PartitionSpec as P

MICRO = 2


epsilon = 1e-06
highest = lax.Precision.HIGHEST
block_rows = 512
lowest = -1e30


def layer_norm(values, gain_vec, shift_vec):
    center = values - jnp.mean(values, axis=-1, keepdims=True)
    inv_std = lax.rsqrt(jnp.mean(center * center, axis=-1, keepdims=True) + epsilon)
    normed = center * inv_std
    return (normed * gain_vec + shift_vec, normed, inv_std)


def norm_back(upstream, normed, inv_std, gain_vec):
    scaled = upstream * gain_vec
    inner = (
        scaled
        - jnp.mean(scaled, axis=-1, keepdims=True)
        - normed * jnp.mean(scaled * normed, axis=-1, keepdims=True)
    )
    return inner * inv_std


def gelu_pair(values):
    normal_cdf = 0.5 * (1.0 + lax.erf(values * 0.7071067811865476))
    normal_pdf = jnp.exp(-0.5 * values * values) * 0.3989422804014327
    return (values * normal_cdf, normal_cdf + values * normal_pdf)


def rel_terms(queries, band_table, cols_table, grid_side):
    shape_in = queries.shape
    shaped = queries.astype(jnp.float32).reshape(
        shape_in[0], shape_in[1] // grid_side, grid_side, shape_in[2], shape_in[3]
    )
    rows_term = jnp.einsum("byxhc,ykc->byxhk", shaped, band_table, precision=highest)
    cols_term = jnp.einsum("byxhc,xkc->byxhk", shaped, cols_table, precision=highest)
    return (
        rows_term.reshape(shape_in[:3] + (grid_side,)),
        cols_term.reshape(shape_in[:3] + (grid_side,)),
    )


def key_bias(rows_term, cols_term, first_key, key_count, grid_side):
    picked = lax.dynamic_slice_in_dim(rows_term, first_key // grid_side, key_count // grid_side, 3)
    joined = picked[..., :, None] + cols_term[..., None, :]
    return joined.reshape(picked.shape[:3] + (key_count,))


def bias_back(grad_logits, first_key, key_count, grid_side):
    split = grad_logits.reshape(grad_logits.shape[:3] + (key_count // grid_side, grid_side))
    empty = jnp.zeros(grad_logits.shape[:3] + (grid_side,), jnp.float32)
    rows_part = lax.dynamic_update_slice_in_dim(
        empty, jnp.sum(split, axis=4), first_key // grid_side, 3
    )
    return (rows_part, jnp.sum(split, axis=3))


def scores_of(queries, key_blk, rows_term, cols_term, first_key, score_scale, grid_side):
    raw_dots = jnp.einsum("brhc,bkhc->bhrk", queries, key_blk, preferred_element_type=jnp.float32)
    return raw_dots * score_scale + key_bias(
        rows_term, cols_term, first_key, key_blk.shape[1], grid_side
    )


def plain_device(
    block_input,
    cotangent,
    norm1_gain,
    norm1_shift,
    w_qkv,
    table_rows,
    table_cols,
    w_proj,
    norm2_gain,
    norm2_shift,
    w_fc1,
    w_fc2,
    index_rows,
    index_cols,
):
    grid_side = index_rows.shape[0]
    table_len = table_rows.shape[0]
    head_dim = table_rows.shape[1]
    model_width = norm1_gain.shape[0]
    band_len = block_input.shape[1]
    band_grid = band_len // grid_side
    local_heads = w_proj.shape[0] // head_dim
    hidden_local = w_fc1.shape[1]
    per_micro = block_input.shape[0] // MICRO
    score_scale = head_dim ** (-0.5)
    ctx_place = lax.axis_index("ctx")
    whole_seq = band_len * lax.axis_size("ctx")
    levels = jnp.arange(table_len, dtype=jnp.int32)
    hot_rows = (index_rows.reshape(-1)[:, None] == levels[None, :]).astype(jnp.float32)
    hot_cols = (index_cols.reshape(-1)[:, None] == levels[None, :]).astype(jnp.float32)
    rows_table = jnp.dot(hot_rows, table_rows.astype(jnp.float32), precision=highest).reshape(
        grid_side, grid_side, head_dim
    )
    cols_table = jnp.dot(hot_cols, table_cols.astype(jnp.float32), precision=highest).reshape(
        grid_side, grid_side, head_dim
    )
    band_table = lax.dynamic_slice_in_dim(rows_table, ctx_place * band_grid, band_grid, 0)
    band_hot = lax.dynamic_slice_in_dim(
        hot_rows.reshape(grid_side, grid_side, table_len), ctx_place * band_grid, band_grid, 0
    )
    cols_hot = hot_cols.reshape(grid_side, grid_side, table_len)
    over_rows = (((0,), (0,)), ((), ()))
    over_cols = (((1,), (1,)), ((), ()))
    qkv_width = 3 * local_heads * head_dim
    grad_qkv = jnp.zeros((model_width, qkv_width), jnp.float32)
    grad_proj = jnp.zeros((local_heads * head_dim, model_width), jnp.float32)
    grad_up = jnp.zeros((model_width, hidden_local), jnp.float32)
    grad_down = jnp.zeros((hidden_local, model_width), jnp.float32)
    gain_one = jnp.zeros((model_width,), jnp.float32)
    shift_one = jnp.zeros((model_width,), jnp.float32)
    gain_two = jnp.zeros((model_width,), jnp.float32)
    shift_two = jnp.zeros((model_width,), jnp.float32)
    grad_rows_tab = jnp.zeros((table_len, head_dim), jnp.float32)
    grad_cols_tab = jnp.zeros((table_len, head_dim), jnp.float32)
    outputs = []
    input_grads = []
    for micro_step in range(MICRO):
        input_part = block_input[micro_step * per_micro : (micro_step + 1) * per_micro]
        grad_part = cotangent[micro_step * per_micro : (micro_step + 1) * per_micro]
        images = input_part.shape[0]
        tokens = images * band_len
        full_qkv, full_proj, full_up, full_down = (
            lax.all_gather(w_qkv, "fsdp", axis=0, tiled=True),
            lax.all_gather(w_proj, "fsdp", axis=1, tiled=True),
            lax.all_gather(w_fc1, "fsdp", axis=0, tiled=True),
            lax.all_gather(w_fc2, "fsdp", axis=1, tiled=True),
        )
        flat_qkv = full_qkv.reshape(model_width, qkv_width)
        input_full, grad_out_full = (
            lax.all_gather(input_part, "tp", axis=2, tiled=True),
            lax.all_gather(grad_part, "tp", axis=2, tiled=True),
        )
        normed_in, normed1, inv_std1 = layer_norm(
            input_full.astype(jnp.float32), norm1_gain, norm1_shift
        )
        first_act = normed_in.astype(jnp.bfloat16).reshape(tokens, model_width)
        mixed_qkv = jnp.dot(first_act, flat_qkv, preferred_element_type=jnp.float32).astype(
            jnp.bfloat16
        )
        mixed_qkv = mixed_qkv.reshape(images, band_len, 3, local_heads, head_dim)
        queries = mixed_qkv[:, :, 0]
        key_part = mixed_qkv[:, :, 1]
        value_part = mixed_qkv[:, :, 2]
        rows_term, cols_term = rel_terms(queries, band_table, cols_table, grid_side)
        rows_swap = jnp.transpose(rows_term, (0, 2, 1, 3))
        cols_swap = jnp.transpose(cols_term, (0, 2, 1, 3))
        fold_init = (
            jnp.full((images, local_heads, band_len), lowest, jnp.float32),
            jnp.zeros((images, local_heads, band_len), jnp.float32),
            jnp.zeros((images, local_heads, band_len, head_dim), jnp.float32),
        )
        key_piece = lax.all_gather(key_part, "ctx", axis=1, tiled=True)
        value_piece = lax.all_gather(value_part, "ctx", axis=1, tiled=True)
        piece_len = key_piece.shape[1]
        sub_len = math.gcd(piece_len, block_rows)

        def forward_advance(block_idx, state):
            running, denom_sum, acc_out = state
            offset = block_idx * sub_len
            key_blk = lax.dynamic_slice_in_dim(key_piece, offset, sub_len, 1)
            value_blk = lax.dynamic_slice_in_dim(value_piece, offset, sub_len, 1)
            logits = scores_of(
                queries, key_blk, rows_swap, cols_swap, offset, score_scale, grid_side
            )
            new_peak = jnp.maximum(running, jnp.max(logits, axis=-1))
            rescale = jnp.exp(running - new_peak)
            weights = jnp.exp(logits - new_peak[..., None])
            denom_sum = denom_sum * rescale + jnp.sum(weights, axis=-1)
            acc_out = acc_out * rescale[..., None] + jnp.einsum(
                "bhrk,bkhc->bhrc",
                weights.astype(jnp.bfloat16),
                value_blk,
                preferred_element_type=jnp.float32,
            )
            return (new_peak, denom_sum, acc_out)

        peak_all, denom_all, acc_all = lax.fori_loop(
            0, piece_len // sub_len, forward_advance, fold_init
        )
        attn_exact = jnp.transpose(acc_all / denom_all[..., None], (0, 2, 1, 3))
        log_total = peak_all + jnp.log(denom_all)
        attn_low = attn_exact.astype(jnp.bfloat16).reshape(tokens, local_heads * head_dim)
        attn_branch = jnp.dot(attn_low, full_proj, preferred_element_type=jnp.float32).reshape(
            images, band_len, model_width
        )
        attn_share = lax.psum_scatter(
            attn_branch.astype(jnp.bfloat16), "tp", scatter_dimension=2, tiled=True
        ).astype(jnp.float32)
        middle_share = input_part.astype(jnp.float32) + attn_share
        middle_full = lax.all_gather(
            middle_share.astype(jnp.bfloat16), "tp", axis=2, tiled=True
        ).astype(middle_share.dtype)
        normed_mid, normed2, inv_std2 = layer_norm(middle_full, norm2_gain, norm2_shift)
        second_act = normed_mid.astype(jnp.bfloat16).reshape(tokens, model_width)
        pre_act = jnp.dot(second_act, full_up, preferred_element_type=jnp.float32)
        gelu_out, gelu_slope = gelu_pair(pre_act)
        hidden_low = gelu_out.astype(jnp.bfloat16)
        mlp_branch = jnp.dot(hidden_low, full_down, preferred_element_type=jnp.float32).reshape(
            images, band_len, model_width
        )
        mlp_share = lax.psum_scatter(
            mlp_branch.astype(jnp.bfloat16), "tp", scatter_dimension=2, tiled=True
        ).astype(jnp.float32)
        outputs.append((middle_share + mlp_share).astype(jnp.bfloat16))
        grad_out_flat = grad_out_full.reshape(tokens, model_width)
        grad_down = grad_down + lax.dot_general(
            hidden_low, grad_out_flat, over_rows, preferred_element_type=jnp.float32
        )
        grad_hidden = lax.dot_general(
            grad_out_flat, full_down, over_cols, preferred_element_type=jnp.float32
        )
        grad_pre = (grad_hidden * gelu_slope).astype(jnp.bfloat16)
        grad_up = grad_up + lax.dot_general(
            second_act, grad_pre, over_rows, preferred_element_type=jnp.float32
        )
        grad_second = lax.dot_general(
            grad_pre, full_up, over_cols, preferred_element_type=jnp.float32
        ).reshape(images, band_len, model_width)
        gain_two = gain_two + jnp.sum(grad_second * normed2, axis=(0, 1))
        shift_two = shift_two + jnp.sum(grad_second, axis=(0, 1))
        grad_middle = grad_part.astype(jnp.float32) + lax.psum_scatter(
            norm_back(grad_second, normed2, inv_std2, norm2_gain).astype(jnp.bfloat16),
            "tp",
            scatter_dimension=2,
            tiled=True,
        ).astype(jnp.float32)
        grad_branch = lax.all_gather(
            grad_middle.astype(jnp.bfloat16), "tp", axis=2, tiled=True
        ).reshape(tokens, model_width)
        grad_proj = grad_proj + lax.dot_general(
            attn_low, grad_branch, over_rows, preferred_element_type=jnp.float32
        )
        grad_attn = lax.dot_general(
            grad_branch, full_proj, over_cols, preferred_element_type=jnp.float32
        ).astype(jnp.bfloat16)
        grad_attn = grad_attn.reshape(images, band_len, local_heads, head_dim)
        delta_rows = jnp.sum(grad_attn.astype(jnp.float32) * attn_exact, axis=-1)
        delta_swap = jnp.transpose(delta_rows, (0, 2, 1))
        query_zero = jnp.zeros((images, local_heads, band_len, head_dim), jnp.float32)
        rel_zero = jnp.zeros((images, local_heads, band_len, grid_side), jnp.float32)
        whole_zero = jnp.zeros((images, whole_seq, local_heads, head_dim), jnp.float32)
        back_init = (query_zero, rel_zero, rel_zero, whole_zero, whole_zero)
        back_key_piece = lax.all_gather(key_part, "ctx", axis=1, tiled=True)
        back_value_piece = lax.all_gather(value_part, "ctx", axis=1, tiled=True)
        back_piece_len = back_key_piece.shape[1]
        back_sub_len = math.gcd(back_piece_len, block_rows)

        def back_advance(block_idx, state):
            offset = block_idx * back_sub_len
            key_blk = lax.dynamic_slice_in_dim(back_key_piece, offset, back_sub_len, 1)
            value_blk = lax.dynamic_slice_in_dim(back_value_piece, offset, back_sub_len, 1)
            logits = scores_of(
                queries, key_blk, rows_swap, cols_swap, offset, score_scale, grid_side
            )
            probs = jnp.exp(logits - log_total[..., None])
            grad_probs = jnp.einsum(
                "brhc,bkhc->bhrk", grad_attn, value_blk, preferred_element_type=jnp.float32
            )
            grad_logits = (probs * (grad_probs - delta_swap[..., None])).astype(jnp.bfloat16)
            grad_query = state[0] + jnp.einsum(
                "bhrk,bkhc->bhrc", grad_logits, key_blk, preferred_element_type=jnp.float32
            )
            add_rows, add_cols = bias_back(
                grad_logits.astype(jnp.float32), offset, back_sub_len, grid_side
            )
            grad_key_blk = (
                jnp.einsum(
                    "bhrk,brhc->bkhc", grad_logits, queries, preferred_element_type=jnp.float32
                )
                * score_scale
            )
            grad_value_blk = jnp.einsum(
                "bhrk,brhc->bkhc",
                probs.astype(jnp.bfloat16),
                grad_attn,
                preferred_element_type=jnp.float32,
            )
            keys_acc = lax.dynamic_update_slice_in_dim(
                state[3],
                lax.dynamic_slice_in_dim(state[3], offset, back_sub_len, 1) + grad_key_blk,
                offset,
                1,
            )
            values_acc = lax.dynamic_update_slice_in_dim(
                state[4],
                lax.dynamic_slice_in_dim(state[4], offset, back_sub_len, 1) + grad_value_blk,
                offset,
                1,
            )
            return (grad_query, state[1] + add_rows, state[2] + add_cols, keys_acc, values_acc)

        folded = lax.fori_loop(0, back_piece_len // back_sub_len, back_advance, back_init)
        grad_keys, grad_values = (
            lax.psum_scatter(
                folded[3].astype(jnp.bfloat16), "ctx", scatter_dimension=1, tiled=True
            ).astype(jnp.float32),
            lax.psum_scatter(
                folded[4].astype(jnp.bfloat16), "ctx", scatter_dimension=1, tiled=True
            ).astype(jnp.float32),
        )
        grad_query = jnp.transpose(folded[0] * score_scale, (0, 2, 1, 3))
        grad_rel_rows = jnp.transpose(folded[1], (0, 2, 1, 3)).reshape(
            images, band_grid, grid_side, local_heads, grid_side
        )
        grad_rel_cols = jnp.transpose(folded[2], (0, 2, 1, 3)).reshape(
            images, band_grid, grid_side, local_heads, grid_side
        )
        query_grid = queries.astype(jnp.float32).reshape(
            images, band_grid, grid_side, local_heads, head_dim
        )
        rel_query = jnp.einsum(
            "byxhk,ykc->byxhc", grad_rel_rows, band_table, precision=highest
        ) + jnp.einsum("byxhk,xkc->byxhc", grad_rel_cols, cols_table, precision=highest)
        grad_query = grad_query + rel_query.reshape(images, band_len, local_heads, head_dim)
        band_rows_grad = jnp.einsum(
            "byxhk,byxhc->ykc", grad_rel_rows, query_grid, precision=highest
        )
        cols_grad = jnp.einsum("byxhk,byxhc->xkc", grad_rel_cols, query_grid, precision=highest)
        grad_rows_tab = grad_rows_tab + jnp.einsum(
            "ykt,ykc->tc", band_hot, band_rows_grad, precision=highest
        )
        grad_cols_tab = grad_cols_tab + jnp.einsum(
            "xkt,xkc->tc", cols_hot, cols_grad, precision=highest
        )
        grad_mixed = (
            jnp.stack((grad_query, grad_keys, grad_values), axis=2)
            .astype(jnp.bfloat16)
            .reshape(tokens, qkv_width)
        )
        grad_qkv = grad_qkv + lax.dot_general(
            first_act, grad_mixed, over_rows, preferred_element_type=jnp.float32
        )
        grad_first = lax.dot_general(
            grad_mixed, flat_qkv, over_cols, preferred_element_type=jnp.float32
        ).reshape(images, band_len, model_width)
        gain_one = gain_one + jnp.sum(grad_first * normed1, axis=(0, 1))
        shift_one = shift_one + jnp.sum(grad_first, axis=(0, 1))
        input_grads.append(
            grad_middle
            + lax.psum_scatter(
                norm_back(grad_first, normed1, inv_std1, norm1_gain).astype(jnp.bfloat16),
                "tp",
                scatter_dimension=2,
                tiled=True,
            ).astype(jnp.float32)
        )
    owned_grads = (
        lax.psum_scatter(
            grad_qkv.reshape(model_width, 3, local_heads * head_dim).astype(jnp.bfloat16),
            ("fsdp", "ctx"),
            scatter_dimension=0,
            tiled=True,
        ).astype(jnp.float32),
        lax.psum_scatter(
            grad_proj.astype(jnp.bfloat16), ("fsdp", "ctx"), scatter_dimension=1, tiled=True
        ).astype(jnp.float32),
        lax.psum_scatter(
            grad_up.astype(jnp.bfloat16), ("fsdp", "ctx"), scatter_dimension=0, tiled=True
        ).astype(jnp.float32),
        lax.psum_scatter(
            grad_down.astype(jnp.bfloat16), ("fsdp", "ctx"), scatter_dimension=1, tiled=True
        ).astype(jnp.float32),
    )
    small_sums = lax.psum(
        (gain_one, shift_one, grad_rows_tab, grad_cols_tab, gain_two, shift_two),
        ("fsdp", "ctx", "tp"),
    )
    return (
        jnp.concatenate(outputs, axis=0),
        jnp.concatenate(input_grads, axis=0),
        small_sums[0],
        small_sums[1],
        owned_grads[0],
        small_sums[2],
        small_sums[3],
        owned_grads[1],
        small_sums[4],
        small_sums[5],
        owned_grads[2],
        owned_grads[3],
    )


f32 = jnp.float32
bf16 = jnp.bfloat16
LOG2E = 1.4426950408889634
NN = (((1,), (0,)), ((), ()))
NT = (((1,), (1,)), ((), ()))
TN = (((0,), (0,)), ((), ()))
VMEM_BYTES = 56 << 20


def mm(lhs, rhs, dims=NN):
    return lax.dot_general(lhs, rhs, dims, preferred_element_type=f32)


def pxor(value, axis, bit):
    size = lax.axis_size(axis)
    return lax.ppermute(value, axis, [(i, i ^ bit) for i in range(size)])


def after(values, done):
    return lax.optimization_barrier((values, done))[0]


def gather_tp(share):
    from_x = pxor(share, "tp", 2)
    from_core = pxor(share, "tp", 1)
    return [share, from_core, from_x, pxor(from_x, "tp", 1)]


def swap_ctx(pieces):
    return [pieces[0]] + [pxor(pieces[s], "ctx", s) for s in range(1, len(pieces))]


def gelu_parts(x):
    size = jnp.abs(x)
    t = 1.0 / (1.0 + 0.23164190 * size)
    poly = jnp.full_like(t, 0.5307027145)
    for coef in (-0.726576013, 0.7107068705, -0.142248368, 0.127414796):
        poly = poly * t + coef
    bell = jnp.exp2((-0.5 * LOG2E) * (x * x))
    tail = poly * t * bell
    cdf = jnp.where(x >= 0.0, 1.0 - tail, tail)
    return cdf, bell * 0.3989422804014327


ROWS = 64
ANY = pl.BlockSpec(memory_space=pl.ANY)
MESH = pl.DeviceIdType.MESH


def xor4(a, b):
    high = lax.rem(lax.div(a, 2) + lax.div(b, 2), 2)
    return 2 * high + lax.rem(lax.rem(a, 2) + lax.rem(b, 2), 2)


def spots():
    t, y = lax.axis_index("tp"), lax.axis_index("fsdp")
    return xor4(t, 2 * y), lax.axis_index("ctx")


def peer(axis, bit):
    return {axis: xor4(lax.axis_index(axis), bit)}


def greet(peers):
    barrier = pltpu.get_barrier_semaphore()
    for device in peers:
        pl.semaphore_signal(barrier, inc=1, device_id=device, device_id_type=MESH)
    pl.semaphore_wait(barrier, len(peers))


def remote(source, target, sems, slot, device):
    send, recv = sems
    return pltpu.make_async_remote_copy(
        src_ref=source,
        dst_ref=target,
        send_sem=send.at[slot],
        recv_sem=recv.at[slot],
        device_id=device,
        device_id_type=MESH,
    )


def dma(count=1):
    return pltpu.SemaphoreType.DMA((count,))


def start_all(copies):
    for copy in copies:
        copy.start()


def wait_all(copies):
    for copy in copies:
        copy.wait()


def add_rows(rows, body, step=32):
    def advance(n, carry):
        body(pl.ds(pl.multiple_of(n * step, step), step))
        return carry

    lax.fori_loop(0, rows // step, advance, 0, unroll=2 if rows % (2 * step) == 0 else 1)


CTX_PEERS = (("ctx", 1), ("ctx", 2), ("ctx", 3))
TP_PEERS = (("tp", 1), ("tp", 2))
Y_PEERS = (("fsdp", 1),)


class Quiet:
    ins, out_shape, scratch, peers = (), (), (), ()
    ident = None

    def steps(self, ins, outs, scratch):
        return {}


class Together:
    def __init__(self, ident, *backs):
        self.backs, self.ident = backs, ident
        self.ins = sum((tuple(b.ins) for b in backs), ())
        self.out_shape = sum((list(b.out_shape) for b in backs), [])
        self.scratch = sum((list(b.scratch) for b in backs), [])
        self.peers = tuple(dict.fromkeys(sum((tuple(b.peers) for b in backs), ())))

    def split(self, outs):
        groups = []
        for b in self.backs:
            group, outs = take(outs, len(b.out_shape))
            groups.append(group)
        return groups

    def steps(self, ins, outs, scratch):
        table = {0: [lambda: greet([peer(*p) for p in self.peers])]}
        for b in self.backs:
            mine_in, ins = take(ins, len(b.ins))
            mine_out, outs = take(outs, len(b.out_shape))
            mine_scratch, scratch = take(scratch, len(b.scratch))
            for point, step in b.steps(mine_in, mine_out, mine_scratch):
                table.setdefault(point, []).append(step)

        def chain(fns):
            def run():
                for fn in fns:
                    fn()

            return run

        return {point: chain(fns) for point, fns in table.items()}


class SwapCtx:
    peers = CTX_PEERS

    def __init__(self, pieces, begin=0, end="end"):
        self.ins, self.points = tuple(pieces[1:]), (begin, end)
        self.out_shape = [(p.shape, bf16) for p in self.ins]
        self.scratch = [dma(3), dma(3)]

    def steps(self, ins, outs, scratch):
        def copies():
            return [remote(ins[s], outs[s], scratch, s, peer("ctx", s + 1)) for s in (2, 1, 0)]

        return zip(self.points, (lambda: start_all(copies()), lambda: wait_all(copies())))


class JoinY:
    peers = Y_PEERS

    def __init__(self, own, axis, begin=0, end="end"):
        self.ins, self.axis, self.points = (own,), axis, (begin, end)
        shape = list(own.shape)
        shape[axis] *= 2
        self.out_shape = [(tuple(shape), bf16)]
        self.scratch = [dma(1), dma(1), dma(1)]

    def steps(self, ins, outs, scratch):
        (own,), (full,) = ins, outs
        half = own.shape[self.axis]
        low, high = pl.ds(0, half), pl.ds(half, half)

        def at(part):
            return full.at[part] if self.axis == 0 else full.at[:, part]

        def copies():
            return [
                remote(own, at(high), scratch[:2], 0, peer("fsdp", 1)),
                pltpu.make_async_copy(own, at(low), scratch[2].at[0]),
            ]

        return zip(self.points, (lambda: start_all(copies()), lambda: wait_all(copies())))


class GatherTp:
    peers = TP_PEERS

    def __init__(self, own, points):
        self.ins, self.points = (own,), points
        self.out_shape = [((4,) + own.shape, bf16)]
        self.scratch = [dma(3), dma(3), dma(1)]

    def steps(self, ins, outs, scratch):
        (own,), (full,) = ins, outs
        sems, local_sem = scratch[:2], scratch[2]

        def local():
            return pltpu.make_async_copy(own, full.at[0], local_sem.at[0])

        def to_x():
            return remote(own, full.at[2], sems, 0, peer("tp", 2))

        def to_core():
            return remote(own, full.at[1], sems, 1, peer("tp", 1))

        def onward():
            return remote(full.at[2], full.at[3], sems, 2, peer("tp", 1))

        def forward():
            to_x().wait()
            onward().start()

        return zip(
            self.points,
            (
                lambda: start_all([to_x(), to_core(), local()]),
                forward,
                lambda: wait_all([to_core(), onward(), local()]),
            ),
        )


class SpreadHeads:
    peers = CTX_PEERS + TP_PEERS

    def __init__(self, pieces, points):
        self.ins, self.points = tuple(pieces), points
        self.out_shape = [((4, 4) + pieces[0].shape, bf16)]
        self.scratch = [dma(6), dma(6), dma(1)]

    def steps(self, ins, outs, scratch):
        (out,) = outs
        sems, local_sem = scratch[:2], scratch[2]

        def arrivals():
            copies = [remote(ins[s], out.at[0, s], sems, s - 1, peer("ctx", s)) for s in range(1, 4)]
            return copies + [pltpu.make_async_copy(ins[0], out.at[0, 0], local_sem.at[0])]

        def to_x():
            return remote(out.at[0], out.at[2], sems, 3, peer("tp", 2))

        def to_core():
            return remote(out.at[0], out.at[1], sems, 4, peer("tp", 1))

        def onward():
            return remote(out.at[2], out.at[3], sems, 5, peer("tp", 1))

        def forward():
            wait_all(arrivals())
            start_all([to_x(), to_core()])

        def final():
            to_x().wait()
            onward().start()

        return zip(
            self.points,
            (
                lambda: start_all(arrivals()),
                forward,
                final,
                lambda: wait_all([to_core(), onward()]),
            ),
        )


class ReduceTp:
    peers = TP_PEERS

    def __init__(self, keep, send, cot, points, weight=None):
        self.ins, self.points = (keep, send, cot), points
        rows, tokens = keep.shape
        self.heads = weight is not None
        self.out_shape = [((2 * rows, tokens), bf16), ((rows // 2, tokens), f32)]
        self.scratch = [pltpu.VMEM(keep.shape, bf16)] * 4 + [
            pltpu.VMEM((2 * rows, tokens), bf16),
            pltpu.VMEM((rows // 2, tokens), f32),
            dma(8),
            dma(8),
            dma(7),
        ]
        if self.heads:
            self.ins += (weight,)
            hd = weight.shape[0] // 4
            self.out_shape += [((hd, tokens), bf16)] * 4
            self.scratch += [pltpu.VMEM(weight.shape, bf16), pltpu.VMEM((4, hd, tokens), bf16)]
            self.peers = TP_PEERS + CTX_PEERS

    def steps(self, ins, outs, scratch):
        keep, send, cot = ins[:3]
        full_out, exact_out = outs[:2]
        mine, from_core, from_x, grads, full, exact = scratch[:6]
        sems, local_sem = scratch[6:8], scratch[8]
        rows = mine.shape[0]
        half = rows // 2
        spot, z = spots()
        core = lax.rem(spot, 2)

        def rows_of(n, which):
            return pl.ds(pl.multiple_of((2 * n + which) * half, half), half)

        def core_copy():
            return remote(send, from_core, sems, 0, peer("tp", 1))

        def x_copy():
            return remote(mine, from_x, sems, 1, peer("tp", 2))

        def back_copies():
            return [
                remote(full.at[rows_of(n, core)], full.at[rows_of(n, core)], sems, 2 * n + 2, peer("tp", 1))
                for n in range(2)
            ]

        def loads():
            copies = [pltpu.make_async_copy(keep, mine, local_sem.at[0])]
            for n in range(2):
                copies.append(
                    pltpu.make_async_copy(
                        cot.at[rows_of(n, core)],
                        grads.at[n * half : (n + 1) * half],
                        local_sem.at[n + 1],
                    )
                )
            if self.heads:
                copies.append(pltpu.make_async_copy(ins[3], scratch[9], local_sem.at[5]))
            return copies

        def store_exact():
            return pltpu.make_async_copy(exact, exact_out, local_sem.at[4])

        def store_full():
            return pltpu.make_async_copy(full, full_out, local_sem.at[3])

        def begin():
            core_copy().start()
            start_all(loads())

        def add_core():
            wait_all(loads())
            core_copy().wait()

            def add(at):
                mine[at] = (mine[at].astype(f32) + from_core[at].astype(f32)).astype(bf16)

            add_rows(rows, add)
            x_copy().start()

        def add_x():
            x_copy().wait()
            step = 32
            for part in range(2):

                def add(n, carry, part=part):
                    at = pl.ds(pl.multiple_of(part * half + n * step, step), step)
                    total = mine[at].astype(f32) + from_x[at].astype(f32) + grads[at].astype(f32)
                    to = (2 * part + core) * half + n * step
                    full[pl.ds(pl.multiple_of(to, step), step)] = total.astype(bf16)

                    @pl.when(lax.div(spot, 2) == part)
                    def _():
                        exact[pl.ds(pl.multiple_of(n * step, step), step)] = total

                    return carry

                lax.fori_loop(0, half // step, add, 0)
            start_all(back_copies())
            store_exact().start()

        def swaps():
            parts = scratch[10]
            return [
                remote(parts.at[xor4(z, s)], outs[2 + s], sems, 4 + s, peer("ctx", s))
                for s in (1, 2, 3)
            ]

        def local_head():
            return pltpu.make_async_copy(scratch[10].at[z], outs[2], local_sem.at[6])

        def spread_heads():
            wait_all(back_copies())
            store_full().start()
            if self.heads:
                weight, parts = scratch[9], scratch[10]
                tokens = full.shape[1]
                step = 256
                for n in range(tokens // step):
                    at = slice(n * step, (n + 1) * step)
                    product = mm(weight[...], full[:, at]).astype(bf16)
                    parts[:, :, at] = product.reshape(parts.shape[0], parts.shape[1], step)
                start_all(swaps() + [local_head()])

        def end():
            wait_all([store_exact(), store_full()])
            if self.heads:
                wait_all(swaps() + [local_head()])

        return zip(self.points, (begin, add_core, add_x, spread_heads, end))


class ReduceShare:
    peers = TP_PEERS

    def __init__(self, keep, send, points):
        self.ins, self.points = (keep, send), points
        rows, tokens = keep.shape
        self.out_shape = [((rows // 2, tokens), f32)]
        self.scratch = [pltpu.VMEM(keep.shape, bf16)] * 2 + [
            pltpu.VMEM((rows // 2, tokens), bf16),
            pltpu.VMEM((rows // 2, tokens), f32),
            dma(2),
            dma(2),
            dma(2),
        ]

    def steps(self, ins, outs, scratch):
        keep, send = ins
        mine, from_core, from_x, exact = scratch[:4]
        sems, local_sem = scratch[4:6], scratch[6]
        half = exact.shape[0]
        spot, _ = spots()
        first = lax.div(spot, 2) * half
        second = half - first

        def core_copy():
            return remote(send, from_core, sems, 0, peer("tp", 1))

        def x_copy():
            source = mine.at[pl.ds(pl.multiple_of(second, half), half)]
            return remote(source, from_x, sems, 1, peer("tp", 2))

        def load():
            return pltpu.make_async_copy(keep, mine, local_sem.at[0])

        def store():
            return pltpu.make_async_copy(exact, outs[0], local_sem.at[1])

        def add_core():
            load().wait()
            core_copy().wait()

            def add(at):
                mine[at] = (mine[at].astype(f32) + from_core[at].astype(f32)).astype(bf16)

            add_rows(2 * half, add)
            x_copy().start()

        def add_x():
            x_copy().wait()

            def add(n, carry):
                at = pl.ds(pl.multiple_of(n * 16, 16), 16)
                own = pl.ds(pl.multiple_of(first + n * 16, 16), 16)
                exact[at] = mine[own].astype(f32) + from_x[at].astype(f32)
                return carry

            lax.fori_loop(0, half // 16, add, 0)
            store().start()

        return zip(
            self.points,
            (
                lambda: start_all([core_copy(), load()]),
                add_core,
                add_x,
                lambda: store().wait(),
            ),
        )


class GradsY:
    peers = Y_PEERS

    def __init__(self, total, points):
        self.ins, self.points = (total,), points
        half = (total.shape[0] // 2, total.shape[1])
        self.out_shape = [(half, bf16)]
        self.scratch = [pltpu.VMEM(half, bf16)] * 2 + [dma(1), dma(1), dma(2)]

    def steps(self, ins, outs, scratch):
        (total,) = ins
        mine, got = scratch[:2]
        sems, local_sem = scratch[2:4], scratch[4]
        half = mine.shape[0]

        def across():
            return remote(total.at[half:], got, sems, 0, peer("fsdp", 1))

        def load():
            return pltpu.make_async_copy(total.at[:half], mine, local_sem.at[0])

        def store():
            return pltpu.make_async_copy(mine, outs[0], local_sem.at[1])

        def add_y():
            load().wait()
            across().wait()

            def add(at):
                mine[at] = (mine[at].astype(f32) + got[at].astype(f32)).astype(bf16)

            add_rows(half, add)
            store().start()

        return zip(
            self.points,
            (lambda: start_all([across(), load()]), add_y, lambda: store().wait()),
        )


class GradsZ:
    peers = (("ctx", 1), ("ctx", 2))

    def __init__(self, low, points):
        self.ins, self.points = (low,), points
        rows, cols = low.shape[0] // 4, low.shape[1]
        self.out_shape = [((rows, cols), f32)]
        self.scratch = [
            pltpu.VMEM((5, rows, cols), bf16),
            pltpu.VMEM((rows, cols), f32),
            dma(3),
            dma(3),
            dma(3),
        ]

    def steps(self, ins, outs, scratch):
        (low,) = ins
        buf, exact = scratch[:2]
        sems, local_sem = scratch[2:4], scratch[4]
        rows = exact.shape[0]
        _, z = spots()

        def chunk(s):
            return low.at[pl.ds(pl.multiple_of(xor4(z, s) * rows, 16), rows)]

        def near():
            return [
                remote(chunk(s), buf.at[2 + n], sems, n, peer("ctx", 1)) for n, s in enumerate((1, 3))
            ]

        def far():
            return remote(buf.at[1], buf.at[4], sems, 2, peer("ctx", 2))

        def loads():
            return [
                pltpu.make_async_copy(chunk(s), buf.at[n], local_sem.at[n])
                for n, s in enumerate((0, 2))
            ]

        def store():
            return pltpu.make_async_copy(exact, outs[0], local_sem.at[2])

        def add_near():
            wait_all(loads() + near())

            def add(at):
                buf[1, at] = (buf[1, at].astype(f32) + buf[3, at].astype(f32)).astype(bf16)

            add_rows(rows, add)
            far().start()

        def add_far():
            far().wait()

            def add(at):
                exact[at] = (buf[0, at].astype(f32) + buf[2, at].astype(f32)) + buf[4, at].astype(f32)

            add_rows(rows, add)
            store().start()

        return zip(
            self.points,
            (lambda: start_all(near() + loads()), add_near, add_far, lambda: store().wait()),
        )


class GradsZThenY:
    peers = (("ctx", 1), ("ctx", 2)) + Y_PEERS

    def __init__(self, total, points):
        self.ins, self.points = (total,), points
        rows, cols = total.shape[0] // 8, total.shape[1]
        self.out_shape = [((rows, cols), f32)]
        self.scratch = [
            pltpu.VMEM((2, 5, rows, cols), bf16),
            pltpu.VMEM((rows, cols), bf16),
            pltpu.VMEM((rows, cols), f32),
            dma(7),
            dma(7),
            dma(5),
        ]

    def steps(self, ins, outs, scratch):
        (total,) = ins
        buf, from_y, exact = scratch[:3]
        sems, local_sem = scratch[3:5], scratch[5]
        rows = exact.shape[0]
        _, z = spots()

        def chunk(n, s):
            return total.at[pl.ds(pl.multiple_of((4 * n + xor4(z, s)) * rows, 16), rows)]

        def near(n):
            return [
                remote(chunk(n, s), buf.at[n, 2 + k], sems, 2 * n + k, peer("ctx", 1))
                for k, s in enumerate((1, 3))
            ]

        def far(n):
            return remote(buf.at[n, 1], buf.at[n, 4], sems, 4 + n, peer("ctx", 2))

        def to_y():
            return remote(buf.at[1, 0], from_y, sems, 6, peer("fsdp", 1))

        def loads():
            return [
                pltpu.make_async_copy(chunk(n, s), buf.at[n, k], local_sem.at[2 * n + k])
                for n in range(2)
                for k, s in enumerate((0, 2))
            ]

        def store():
            return pltpu.make_async_copy(exact, outs[0], local_sem.at[4])

        def begin():
            start_all(near(1) + loads())

        def add_near(n):
            wait_all(near(n))

            def add(at):
                buf[n, 1, at] = (buf[n, 1, at].astype(f32) + buf[n, 3, at].astype(f32)).astype(bf16)

            add_rows(rows, add)
            far(n).start()

        def summed(n, at):
            return (buf[n, 0, at].astype(f32) + buf[n, 2, at].astype(f32)) + buf[n, 4, at].astype(f32)

        def second():
            wait_all(loads())
            add_near(1)
            start_all(near(0))

        def third():
            add_near(0)
            far(1).wait()

            def add(at):
                buf[1, 0, at] = summed(1, at).astype(bf16)

            add_rows(rows, add)
            to_y().start()

        def end():
            to_y().wait()
            far(0).wait()

            def add(at):
                exact[at] = summed(0, at) + from_y[at].astype(f32)

            add_rows(rows, add)
            store().start()
            store().wait()

        return zip(self.points, (begin, second, third, end))


def take(refs, count):
    return refs[:count], refs[count:]


def run_step(steps, index, last=None):
    for point, step in steps.items():
        if point != "end":
            pl.when(index == point)(step)
    if last is not None and "end" in steps:
        pl.when(last)(steps["end"])


def assemble(place, pieces, full):
    count = len(pieces)
    share = pieces[0].shape[-2]
    for mine in range(count):

        @pl.when(place == mine)
        def _(mine=mine):
            for a in range(count):
                piece = pieces[a ^ mine]
                value = piece[0] if len(piece.shape) == 3 else piece[...]
                full[a * share : (a + 1) * share, :] = value


def spread(parts, place, keep_ref, send_ref):
    core = lax.rem(place, 2)
    share = parts.shape[1]
    for n in range(2):
        keep_ref[n * share : (n + 1) * share] = parts[2 * n + core]
        send_ref[n * share : (n + 1) * share] = parts[2 * n + 1 - core]


def over_rows_of(count, body, init, unroll=2):
    def advance(n, carry):
        return body(pl.ds(pl.multiple_of(n * ROWS, ROWS), ROWS), carry)

    return lax.fori_loop(0, count // ROWS, advance, init, unroll=unroll)


def fold8(value):
    return jnp.sum(value.reshape(value.shape[0] // 8, 8, value.shape[1]), axis=0)


def wide(value, lanes):
    return jnp.concatenate([value] * (lanes // 128), axis=1)


def moments(full):
    rows, lanes = full.shape
    zero = jnp.zeros((8, lanes), f32)
    total = over_rows_of(rows, lambda at, c: c + fold8(full[at].astype(f32)), zero)
    mean = jnp.sum(total, axis=0, keepdims=True) * (1.0 / rows)

    def square(at, c):
        center = full[at].astype(f32) - mean
        return c + fold8(center * center)

    total = over_rows_of(rows, square, zero)
    var = jnp.sum(total, axis=0, keepdims=True) * (1.0 / rows)
    return mean, lax.rsqrt(var + epsilon)


def normalize(full, act, gain, shift):
    mean, inv_std = moments(full)
    lanes = full.shape[1]

    def write(at, carry):
        normed = (full[at].astype(f32) - mean) * inv_std
        act[at] = (normed * wide(gain[at], lanes) + wide(shift[at], lanes)).astype(bf16)
        return carry

    over_rows_of(full.shape[0], write, 0)
    return mean, inv_std


def lane_sums(value):
    total = value[:, 0:128]
    for n in range(1, value.shape[1] // 128):
        total += value[:, n * 128 : (n + 1) * 128]
    return total


CHUNK = 256
SUB = 32


def subs(first):
    for r in range(CHUNK // SUB):
        yield slice(r * SUB, (r + 1) * SUB), slice(first + r * SUB, first + (r + 1) * SUB)


def gather_chunk(state, up_all, first, full, mean, inv_std, gain, sums, upstream):
    plain, mixed = state
    lanes = up_all.shape[1]
    for part, to in subs(first):
        up = up_all[part]
        upstream[to] = up
        both = up * ((full[to].astype(f32) - mean) * inv_std)
        g = wide(gain[to], lanes)
        sums[0, to] += lane_sums(both)
        sums[1, to] += lane_sums(up)
        plain += fold8(up * g)
        mixed += fold8(both * g)
    return plain, mixed


def finish_stats(state, width):
    plain, mixed = state
    scale = 1.0 / width
    return (
        jnp.sum(plain, axis=0, keepdims=True) * scale,
        jnp.sum(mixed, axis=0, keepdims=True) * scale,
    )


def write_chunk(parts, first, upstream, full, mean, inv_std, gain, stats):
    plain, mixed = stats
    share = parts.shape[1]
    lanes = upstream.shape[1]
    for _, to in subs(first):
        normed = (full[to].astype(f32) - mean) * inv_std
        result = (upstream[to] * wide(gain[to], lanes) - plain - normed * mixed) * inv_std
        at = to.start % share
        parts[to.start // share, at : at + SUB] = result.astype(bf16)


def normalize_chunk(full, act, first, mean, inv_std, gain, shift):
    lanes = full.shape[1]
    for _, to in subs(first):
        normed = (full[to].astype(f32) - mean) * inv_std
        act[to] = (normed * wide(gain[to], lanes) + wide(shift[to], lanes)).astype(bf16)


def spread_rows(value, parts, first):
    share = parts.shape[1]
    for part, to in subs(first):
        at = to.start % share
        parts[to.start // share, at : at + SUB] = value[part].astype(bf16)


def whole_spec(shape):
    return pl.BlockSpec(shape, lambda *_: (0,) * len(shape))


def cols_spec(height, block):
    return pl.BlockSpec((height, block), lambda i, *_: (0, i))


def image_spec(image, height, block):
    return pl.BlockSpec((1, height, block), lambda i, *_: (image, 0, i))


def fixed_spec(shape):
    return pl.BlockSpec(shape, lambda *_: (0,) * len(shape), pipeline_mode=pl.Buffered(1))


def call(body, grid, in_specs, out_specs, out_shape, scratch, name, args, back=Quiet(), vmem=48):
    count = len(out_shape)

    def kernel(*refs):
        ins, refs = take(refs, len(args))
        back_ins, refs = take(refs, len(back.ins))
        outs, refs = take(refs, count)
        back_outs, refs = take(refs, len(back.out_shape))
        own, back_scratch = take(refs, len(scratch))
        body(back.steps(back_ins, back_outs, back_scratch), *ins, *outs, *own)

    shapes = list(out_shape) + list(back.out_shape)
    params = dict(vmem_limit_bytes=vmem << 20)
    if back.ident is not None:
        params.update(collective_id=back.ident, has_side_effects=True)
    out = pl.pallas_call(
        kernel,
        grid=grid,
        in_specs=list(in_specs) + [ANY] * len(back.ins),
        out_specs=list(out_specs) + [ANY] * len(back.out_shape),
        scratch_shapes=list(scratch) + list(back.scratch),
        out_shape=[jax.ShapeDtypeStruct(s, d) for s, d in shapes],
        compiler_params=pltpu.CompilerParams(**params),
        cost_estimate=pl.CostEstimate(flops=1 << 20, bytes_accessed=1 << 16, transcendentals=0),
        name=name,
    )(*args, *back.ins)
    return out if back.ident is None else (out[:count], back.split(out[count:]))


def qkv_kernel(steps, *refs):
    run_step(steps, pl.program_id(0))
    pieces, (gain, shift, own, other), (full, act), outs, mixed = (
        refs[:4],
        refs[4:8],
        refs[8:10],
        refs[10:14],
        refs[14],
    )
    spot, z = spots()
    assemble(spot, pieces, full)
    normalize(full, act, gain, shift)
    half = own.shape[1]
    product = mm(own[...], act[0:half]) + mm(other[...], act[half:])
    mixed[...] = product.astype(bf16).reshape(mixed.shape)
    rows = mixed.shape[1]
    for s in range(4):
        head = xor4(z, s)
        for k, part in enumerate((1, 2, 0)):
            outs[s][k * rows : (k + 1) * rows] = mixed[part * 4 + head]
    pl.when(pl.program_id(0) == pl.num_programs(0) - 1)(steps.get("end", lambda: None))


def qkv_call(image, pieces, gain, shift, own, other, hd, back, name):
    _, share, tokens = pieces[0].shape
    width = gain.shape[0]
    total = own.shape[0]
    block = 256
    return call(
        qkv_kernel,
        (tokens // block,),
        [image_spec(image, share, block)] * 4
        + [fixed_spec(gain.shape)] * 2
        + [fixed_spec(own.shape)] * 2,
        [cols_spec(width, block)] * 2 + [cols_spec(3 * hd, block)] * 4,
        [((width, tokens), bf16)] * 2 + [((3 * hd, tokens), bf16)] * 4,
        [pltpu.VMEM((total // hd, hd, block), bf16)],
        name,
        (*pieces, gain, shift, own, other),
        back,
        vmem=24,
    )


def mlp_kernel(steps, heads, full, cots, *refs):
    gain, shift, proj, up, down = refs[:5]
    act2, cot, hidden, grad_pre, keep_f, send_f, keep_b, send_b, sums, mid_own, joined = refs[5:16]
    mixed, mid, upstream, parts, parts_f = refs[16:21]
    step_at = pl.program_id(0)
    run_step(steps, step_at)
    spot, z = spots()
    for r in range(4):
        for s in range(4):
            mixed[r, xor4(z, s)] = heads[r, s]
    joined[...] = mixed[0].reshape(joined.shape)
    assemble(spot, [cots.at[r, 0] for r in range(4)], cot)
    width, lanes = mid.shape
    hid = hidden.shape[0]
    attn = mixed[...].reshape(width, lanes)
    zero = jnp.zeros((8, lanes), f32)

    @pl.when(step_at == 0)
    def _():
        sums[...] = jnp.zeros_like(sums)

    total = zero
    for first in range(0, width, CHUNK):
        product = mm(proj[:, first : first + CHUNK], attn, TN)
        for part, to in subs(first):
            value = product[part] + full[to].astype(f32)
            mid[to] = value
            total += fold8(value)
    mean = jnp.sum(total, axis=0, keepdims=True) * (1.0 / width)
    share = mid_own.shape[0]
    mid_own[...] = mid[pl.ds(pl.multiple_of(spot * share, share), share)]
    total = zero
    for first in range(0, width, SUB):
        center = mid[first : first + SUB] - mean
        total += fold8(center * center)
    inv_std = lax.rsqrt(jnp.sum(total, axis=0, keepdims=True) * (1.0 / width) + epsilon)
    for first in range(0, width, CHUNK):
        upstream[first : first + CHUNK] = mm(down[first : first + CHUNK], cot[...])
        normalize_chunk(mid, act2, first, mean, inv_std, gain, shift)
    for first in range(0, hid, CHUNK):
        pre_all = mm(up[:, first : first + CHUNK], act2[...], TN)
        for part, to in subs(first):
            pre = pre_all[part]
            cdf, density = gelu_parts(pre)
            hidden[to] = (pre * cdf).astype(bf16)
            grad_pre[to] = (upstream[to] * (cdf + pre * density)).astype(bf16)
    state = (zero, zero)
    for first in range(0, width, CHUNK):
        up_all = mm(up[first : first + CHUNK], grad_pre[...])
        state = gather_chunk(state, up_all, first, mid, mean, inv_std, gain, sums, upstream)
    stats = finish_stats(state, width)
    for first in range(0, width, CHUNK):
        spread_rows(mm(down[:, first : first + CHUNK], hidden[...], TN), parts_f, first)
        write_chunk(parts, first, upstream, mid, mean, inv_std, gain, stats)
    spread(parts_f, spot, keep_f, send_f)
    spread(parts, spot, keep_b, send_b)
    pl.when(step_at == pl.num_programs(0) - 1)(steps.get("end", lambda: None))


def mlp_call(image, heads, full, cots, gain, shift, proj, up, down, back):
    width, tokens = full.shape
    hid = up.shape[1]
    share = width // 4
    hd = heads.shape[2]
    block = 256
    half = width // 2
    return call(
        mlp_kernel,
        (tokens // block,),
        [
            pl.BlockSpec((4, 4, hd, block), lambda i: (0, 0, 0, i)),
            cols_spec(width, block),
        ]
        + [pl.BlockSpec((4, 1, share, block), lambda i: (0, image, 0, i))]
        + [fixed_spec(gain.shape)] * 2
        + [fixed_spec(proj.shape), fixed_spec(up.shape), fixed_spec(down.shape)],
        [cols_spec(width, block)] * 2
        + [cols_spec(hid, block)] * 2
        + [cols_spec(half, block)] * 4
        + [whole_spec((2, width, 128)), cols_spec(share, block), cols_spec(4 * hd, block)],
        [((width, tokens), bf16)] * 2
        + [((hid, tokens), bf16)] * 2
        + [((half, tokens), bf16)] * 4
        + [((2, width, 128), f32), ((share, tokens), f32), ((4 * hd, tokens), bf16)],
        [
            pltpu.VMEM((4, 4, hd, block), bf16),
            pltpu.VMEM((width, block), f32),
            pltpu.VMEM((width, block), f32),
            pltpu.VMEM((4, share, block), bf16),
            pltpu.VMEM((4, share, block), bf16),
        ],
        "mlp%d" % image,
        (heads, full, cots, gain, shift, proj, up, down),
        back,
    )


def gattn_kernel(_, full, weight, *refs):
    outs, mixed = refs[:4], refs[4]
    _, z = spots()
    mixed[...] = mm(weight[...], full[...]).astype(bf16).reshape(mixed.shape)
    for s in range(4):
        outs[s][...] = mixed[xor4(z, s)]


def gattn_call(full, weight, hd):
    width, tokens = full.shape
    total = weight.shape[0]
    block = 256
    return call(
        gattn_kernel,
        (tokens // block,),
        [cols_spec(width, block), fixed_spec(weight.shape)],
        [cols_spec(hd, block)] * 4,
        [((hd, tokens), bf16)] * 4,
        [pltpu.VMEM((total // hd, hd, block), bf16)],
        "gattn",
        (full, weight),
        vmem=20,
    )


def gin_block(joined, full, gain, own, other, sums, upstream, parts):
    half = own.shape[1]
    width, lanes = full.shape
    mean, inv_std = moments(full)
    zero = jnp.zeros((8, lanes), f32)
    state = (zero, zero)
    step = 128
    for first in range(0, width, CHUNK):
        ups = []
        for n in range(first, first + CHUNK, step):
            weight = own if n < half else other
            ups.append(mm(weight[:, n % half : n % half + step], joined, TN))
        up_all = jnp.concatenate(ups, axis=0)
        state = gather_chunk(state, up_all, first, full, mean, inv_std, gain, sums, upstream)
    stats = finish_stats(state, width)
    for first in range(0, width, CHUNK):
        write_chunk(parts, first, upstream, full, mean, inv_std, gain, stats)


def tail_kernel(_, *refs):
    pieces, (full_0, act_0, gain, own, other, small_in), refs = refs[:4], refs[4:10], refs[10:]
    sends, (full_any, act_any, proj_any), refs = refs[:4], refs[4:7], refs[7:]
    (out_0, out_1, out_w, out_small, out_p), refs = refs[:5], refs[5:]
    (mixed, got, full_1, act_1, total, low, upstream, parts, block, sums), refs = refs[:10], refs[10:]
    (keep, send, from_core, from_x, exact, from_y, from_z, exact_w, small, hops), refs = (
        refs[:10],
        refs[10:],
    )
    (mine_p, got_p, from_p, exact_p), refs = refs[:4], refs[4:]
    send_sem, recv_sem, local_sem = refs
    sems = (send_sem, recv_sem)
    spot, z = spots()
    core = lax.rem(spot, 2)
    tokens = mixed.shape[2]
    rows = mixed.shape[1]
    width = full_0.shape[0]
    half = width // 2
    share = half // 2
    lanes = block.shape[1]
    chunk = half // 4

    greet([peer(*p) for p in CTX_PEERS + TP_PEERS + Y_PEERS])

    def swaps():
        return [remote(sends[s], got.at[s], sems, s - 1, peer("ctx", s)) for s in (3, 2, 1)]

    def loads():
        return [
            pltpu.make_async_copy(sends[0], got.at[0], local_sem.at[0]),
            pltpu.make_async_copy(full_any, full_1, local_sem.at[1]),
            pltpu.make_async_copy(act_any, act_1, local_sem.at[2]),
        ]

    def proj_y():
        return remote(proj_any.at[half:], got_p, sems, 19, peer("fsdp", 1))

    def proj_load():
        return pltpu.make_async_copy(proj_any.at[:half], mine_p, local_sem.at[7])

    def proj_z(s):
        source = mine_p.at[pl.ds(pl.multiple_of(xor4(z, s) * chunk, 16), chunk)]
        return remote(source, from_p.at[s], sems, 19 + s, peer("ctx", s))

    start_all(swaps() + loads() + [proj_y(), proj_load()])
    sums[...] = jnp.zeros_like(sums)

    def join(source):
        for s in range(4):
            head = xor4(z, s)
            for k, part in enumerate((1, 2, 0)):
                mixed[part * 4 + head] = source(s)[k * rows : (k + 1) * rows]

    def all_blocks(full, image):
        def advance(b, carry):
            at = pl.ds(pl.multiple_of(b * lanes, lanes), lanes)
            block[...] = full[:, at]
            joined = mixed[:, :, at].reshape(mixed.shape[0] * rows, lanes)
            gin_block(joined, block, gain, own, other, sums, upstream, parts)
            for n in range(2):
                to = slice(n * share, (n + 1) * share)
                keep[image, to, at] = parts[2 * n + core]
                send[image, to, at] = parts[2 * n + 1 - core]
            return carry

        lax.fori_loop(0, tokens // lanes, advance, 0)

    def core_copy(image):
        return remote(send.at[image], from_core.at[image], sems, 3 + image, peer("tp", 1))

    first = lax.div(spot, 2) * share
    second = share - first

    def x_copy(image):
        source = keep.at[image, pl.ds(pl.multiple_of(second, share), share)]
        return remote(source, from_x.at[image], sems, 5 + image, peer("tp", 2))

    def add_core(image):
        core_copy(image).wait()

        def add(at):
            keep[image, at] = (
                keep[image, at].astype(f32) + from_core[image, at].astype(f32)
            ).astype(bf16)

        add_rows(half, add)
        x_copy(image).start()

    def add_x(image):
        x_copy(image).wait()

        def add(n, carry):
            at = pl.ds(pl.multiple_of(n * 16, 16), 16)
            mine = pl.ds(pl.multiple_of(first + n * 16, 16), 16)
            exact[image, at] = keep[image, mine].astype(f32) + from_x[image, at].astype(f32)
            return carry

        lax.fori_loop(0, share // 16, add, 0)

    def out_copy(image, out):
        return pltpu.make_async_copy(exact.at[image], out, local_sem.at[3 + image])

    def y_copy(s):
        place = pl.multiple_of(half + xor4(z, s) * chunk, 16)
        return remote(low.at[pl.ds(place, chunk)], from_y.at[s], sems, 7 + s, peer("fsdp", 1))

    def z_copy(s):
        return remote(from_y.at[s], from_z.at[s], sems, 10 + s, peer("ctx", s))

    def product(act, at):
        return mm(act[at], mixed[...].reshape(mixed.shape[0] * rows, tokens), NT)

    step = 128

    def weight_first(n, carry):
        at = pl.ds(pl.multiple_of(n * step, step), step)
        total[at] = product(act_0, at)
        return carry

    def weight_second(n, carry):
        at = pl.ds(pl.multiple_of(n * step, step), step)
        low[at] = (total[at] + product(act_1, at)).astype(bf16)
        return carry

    join(lambda s: pieces[s])
    all_blocks(full_0, 0)
    core_copy(0).start()
    lax.fori_loop(0, width // step, weight_first, 0)
    add_core(0)
    wait_all([proj_load(), proj_y()])

    def add_p(at):
        mine_p[at] = (mine_p[at].astype(f32) + got_p[at].astype(f32)).astype(bf16)

    add_rows(half, add_p)
    wait_all(swaps() + loads())
    start_all([proj_z(s) for s in (3, 2, 1)])
    join(lambda s: got.at[s])
    lax.fori_loop(half // step, width // step, weight_second, 0)
    start_all([y_copy(s) for s in (3, 2, 1, 0)])
    lax.fori_loop(0, half // step, weight_second, 0)
    add_x(0)
    out_copy(0, out_0).start()
    all_blocks(full_1, 1)
    core_copy(1).start()
    small[0:288] = small_in[...]
    y = lax.axis_index("fsdp")
    for n in range(2):
        line = jnp.sum(jnp.transpose(sums[n]), axis=0, keepdims=True)
        line = jnp.where(y == 0, line, jnp.concatenate([line[:, half:], line[:, :half]], axis=1))
        for k in range(width // 128):
            small[288 + n * 16 + k : 289 + n * 16 + k] = line[:, k * 128 : (k + 1) * 128]
    def hop(k, axis, bit):
        return remote(small, hops.at[k], sems, 14 + k, peer(axis, bit))

    route = TP_PEERS + CTX_PEERS[:2] + Y_PEERS

    def hop_end(k):
        hop(k, *route[k]).wait()
        small[...] += hops[k]

    hop(0, *route[0]).start()
    for n, s in enumerate((3, 2, 1)):
        y_copy(s).wait()

        def add(at, s=s):
            mine = low[pl.ds(pl.multiple_of(xor4(z, s) * chunk + at.start, 16), at.size)]
            from_y[s, at] = (from_y[s, at].astype(f32) + mine.astype(f32)).astype(bf16)

        add_rows(chunk, add)
        z_copy(s).start()
        hop_end(n)
        hop(n + 1, *route[n + 1]).start()
        if n == 0:
            add_core(1)
    hop_end(3)
    hop(4, *route[4]).start()
    wait_all([proj_z(s) for s in (3, 2, 1)])

    def last_p(at):
        mine = mine_p[pl.ds(pl.multiple_of(z * chunk + at.start, 16), at.size)].astype(f32)
        exact_p[at] = (mine + from_p[1, at].astype(f32)) + (
            from_p[2, at].astype(f32) + from_p[3, at].astype(f32)
        )

    add_rows(chunk, last_p)
    add_x(1)
    out_copy(1, out_1).start()
    y_copy(0).wait()
    hop_end(4)
    wait_all([z_copy(s) for s in (3, 2, 1)])

    def add_last(at):
        mine = low[pl.ds(pl.multiple_of(z * chunk + at.start, 16), at.size)].astype(f32)
        exact_w[at] = ((mine + from_y[0, at].astype(f32)) + from_z[1, at].astype(f32)) + (
            from_z[2, at].astype(f32) + from_z[3, at].astype(f32)
        )

    add_rows(chunk, add_last)
    lasts = [
        pltpu.make_async_copy(exact_w, out_w, local_sem.at[5]),
        pltpu.make_async_copy(small, out_small, local_sem.at[6]),
        pltpu.make_async_copy(exact_p, out_p, local_sem.at[8]),
    ]
    start_all(lasts)
    wait_all(lasts + [out_copy(0, out_0), out_copy(1, out_1)])


def tail_call(pieces, full_0, act_0, gain, own, other, small, sends, full_1, act_1, proj, hd, ident):
    part_rows, tokens = pieces[0].shape
    width = gain.shape[0]
    total = own.shape[0]
    half = width // 2
    share = half // 2
    block = 256
    ins = (*pieces, full_0, act_0, gain, own, other, small)
    anys = (*sends, full_1, act_1, proj)
    cols = proj.shape[1]
    scratch = [
        pltpu.VMEM((total // hd, hd, tokens), bf16),
        pltpu.VMEM((4, part_rows, tokens), bf16),
        pltpu.VMEM((width, tokens), bf16),
        pltpu.VMEM((width, tokens), bf16),
        pltpu.VMEM((width, total), f32),
        pltpu.VMEM((width, total), bf16),
        pltpu.VMEM((width, block), f32),
        pltpu.VMEM((4, share, block), bf16),
        pltpu.VMEM((width, block), bf16),
        pltpu.VMEM((2, width, 128), f32),
        pltpu.VMEM((2, half, tokens), bf16),
        pltpu.VMEM((2, half, tokens), bf16),
        pltpu.VMEM((2, half, tokens), bf16),
        pltpu.VMEM((2, share, tokens), bf16),
        pltpu.VMEM((2, share, tokens), f32),
        pltpu.VMEM((4, half // 4, total), bf16),
        pltpu.VMEM((4, half // 4, total), bf16),
        pltpu.VMEM((half // 4, total), f32),
        pltpu.VMEM((320, 128), f32),
        pltpu.VMEM((5, 320, 128), f32),
        pltpu.VMEM((half, cols), bf16),
        pltpu.VMEM((half, cols), bf16),
        pltpu.VMEM((4, half // 4, cols), bf16),
        pltpu.VMEM((half // 4, cols), f32),
        dma(23),
        dma(23),
        dma(9),
    ]
    return pl.pallas_call(
        functools.partial(tail_kernel, None),
        in_specs=[pl.BlockSpec(memory_space=pltpu.VMEM)] * len(ins) + [ANY] * len(anys),
        out_specs=[ANY] * 5,
        scratch_shapes=scratch,
        out_shape=[
            jax.ShapeDtypeStruct((share, tokens), f32),
            jax.ShapeDtypeStruct((share, tokens), f32),
            jax.ShapeDtypeStruct((half // 4, total), f32),
            jax.ShapeDtypeStruct((320, 128), f32),
            jax.ShapeDtypeStruct((half // 4, cols), f32),
        ],
        compiler_params=pltpu.CompilerParams(
            vmem_limit_bytes=60 << 20, collective_id=ident, has_side_effects=True
        ),
        cost_estimate=pl.CostEstimate(flops=1 << 20, bytes_accessed=1 << 16, transcendentals=0),
        name="tail",
    )(*ins, *anys)


def band_start(place, chunk, size, band):
    return xor4(place, lax.div(chunk * size, band)) * band + lax.rem(chunk * size, band)


def fwd_kernel(dims, steps, *refs):
    hd, side, scale = dims
    _, place = spots()
    pieces, table = refs[:4], refs[4]
    outs, kvq, exact, lse, qa = refs[5:9], refs[9], refs[10], refs[11], refs[12]
    ka, va, low = refs[13:16]
    band = pieces[0].shape[1]
    seq = kvq.shape[1]
    step = 512
    bq, bk = band, 1024
    for s in range(4):
        kvq[:, s * band : (s + 1) * band] = pieces[s][...]
    lane = lax.broadcasted_iota(jnp.int32, (step, 128), 1)
    row = lax.broadcasted_iota(jnp.int32, (step, 128), 0)
    lane_side = lax.broadcasted_iota(jnp.int32, (side, 128), 1)
    row16 = lax.broadcasted_iota(jnp.int32, (16, step), 0)
    pad = jnp.zeros((128 - hd, step), bf16)

    def prepare(c, carry):
        at = pl.ds(pl.multiple_of(c * step, step), step)
        start = band_start(place, c, step, band)
        keys = jnp.transpose(jnp.concatenate([kvq[0:hd, at], pad], axis=0).astype(f32))
        ka[at, 0:128] = keys.astype(bf16)
        pos = row + start
        want = jnp.where(lane < side, lax.div(pos, side), lax.rem(pos, side) + side)
        ka[at, 128:256] = jnp.where(want == lane, 1.0, 0.0).astype(bf16)
        va[0:hd, at] = kvq[hd : 2 * hd, at]
        va[hd : hd + 16, at] = jnp.where(row16 == 0, 1.0, 0.0).astype(bf16)
        queries = jnp.concatenate([kvq[2 * hd : 3 * hd, at], pad], axis=0)
        qa[0:128, at] = (queries.astype(f32) * (scale * LOG2E)).astype(bf16)
        terms = lax.dot_general(queries, table[...], (((0,), (1,)), ((), ())), preferred_element_type=f32)
        parts = []
        for r in range(step // side):
            y = lax.div(start, side) + r
            by_row = terms[r * side : (r + 1) * side, 0:128]
            by_col = terms[r * side : (r + 1) * side, 128:256]
            by_row = pltpu.roll(by_row, lax.rem(side + 1 + y, 128), 1)
            by_col = pltpu.roll(by_col, 1, 1, stride=1, stride_axis=0)
            parts.append(jnp.where(lane_side < side, by_row, by_col))
        rel = jnp.concatenate(parts, axis=0) * LOG2E
        qa[128:256, at] = jnp.transpose(rel).astype(bf16)
        return carry

    lax.fori_loop(0, seq // step, prepare, 0)

    def queries_loop(i, carry):
        at = pl.ds(pl.multiple_of(i * bq, bq), bq)
        q_block = qa[:, at]

        def keys_loop(j, state):
            peak, total = state
            run_step(steps, i * (seq // bk) + j)
            keys = pl.ds(pl.multiple_of(j * bk, bk), bk)
            logits = mm(ka[keys, :], q_block)
            new_peak = jnp.maximum(peak, jnp.max(logits, axis=0, keepdims=True))
            weights = jnp.exp2(logits - new_peak).astype(bf16)
            total = total * jnp.exp2(peak - new_peak) + mm(va[:, keys], weights)
            return new_peak, total

        peak, total = lax.fori_loop(
            0,
            seq // bk,
            keys_loop,
            (jnp.full((1, bq), lowest, f32), jnp.zeros((hd + 16, bq), f32)),
        )
        denom = total[hd : hd + 1]
        value = total[0:hd] / denom
        exact[:, at] = value
        low[:, at] = value.astype(bf16)
        lse[:, at] = jnp.broadcast_to(peak + jnp.log2(denom), (8, bq))
        return carry

    lax.fori_loop(0, seq // bq, queries_loop, 0)
    for s in range(4):
        outs[s][...] = low[:, s * band : (s + 1) * band]
    steps.get("end", lambda: None)()


def fwd_call(pieces, table, hd, side, back, name):
    rows, band = pieces[0].shape
    seq = 4 * band
    return call(
        functools.partial(fwd_kernel, (hd, side, hd ** (-0.5))),
        (1,),
        [fixed_spec((rows, band))] * 4 + [fixed_spec(table.shape)],
        [fixed_spec((hd, band))] * 4
        + [fixed_spec((rows, seq)), fixed_spec((hd, seq)), fixed_spec((8, seq)), fixed_spec((256, seq))],
        [((hd, band), bf16)] * 4
        + [((rows, seq), bf16), ((hd, seq), f32), ((8, seq), f32), ((256, seq), bf16)],
        [
            pltpu.VMEM((seq, 256), bf16),
            pltpu.VMEM((hd + 16, seq), bf16),
            pltpu.VMEM((hd, seq), bf16),
        ],
        name,
        (*pieces, table),
        back,
        vmem=36,
    )


def split3(value):
    high = value.astype(bf16).astype(f32)
    rest = value - high
    mid = rest.astype(bf16).astype(f32)
    return high, mid, rest - mid


def bwd_kernel(dims, steps, *refs):
    hd, side, scale = dims
    _, place = spots()
    grads, kvq, qa_in, exact, lse, table = refs[:4], refs[4], refs[5], refs[6], refs[7], refs[8]
    outs, dtab = refs[9:13], refs[13]
    ka, kt, va, qa, da, qn, dn, dk, dv, res = refs[14:24]
    band = grads[0].shape[1]
    seq = kvq.shape[1]
    step = 512
    bq, bk = band, 1024
    for s in range(4):
        da[0:hd, s * band : (s + 1) * band] = grads[s][...]
    lane = lax.broadcasted_iota(jnp.int32, (step, 128), 1)
    row = lax.broadcasted_iota(jnp.int32, (step, 128), 0)
    lane_side = lax.broadcasted_iota(jnp.int32, (side, 128), 1)
    extra = lax.broadcasted_iota(jnp.int32, (128 - hd, step), 0)
    pad = jnp.zeros((128 - hd, step), bf16)
    ones = (lane >= hd) & (lane < hd + 3)

    def turned(value):
        return jnp.transpose(jnp.concatenate([value, pad], axis=0).astype(f32))

    def special(value):
        high, mid, rest = split3(value)
        picked = jnp.where(extra == 0, high, jnp.where(extra == 1, mid, jnp.where(extra == 2, rest, 0.0)))
        return picked.astype(bf16)

    def prepare(c, carry):
        at = pl.ds(pl.multiple_of(c * step, step), step)
        start = band_start(place, c, step, band)
        k_part = kvq[0:hd, at]
        q_part = kvq[2 * hd : 3 * hd, at]
        kt[0:128, at] = jnp.concatenate([k_part, pad], axis=0)
        ka[at, 0:128] = jnp.where(ones, 1.0, turned(k_part)).astype(bf16)
        pos = row + start
        want = jnp.where(lane < side, lax.div(pos, side), lax.rem(pos, side) + side)
        ka[at, 128:256] = jnp.where(want == lane, 1.0, 0.0).astype(bf16)
        want = jnp.where(lane < side, lax.div(pos, side), 2 * side - 1 - lax.rem(pos, side))
        kt[128:256, at] = jnp.transpose(jnp.where(want == lane, 1.0, 0.0)).astype(bf16)
        va[at, :] = jnp.where(ones, 1.0, turned(kvq[hd : 2 * hd, at])).astype(bf16)
        dk[at, :] = jnp.zeros((step, 128), f32)
        dv[at, :] = jnp.zeros((step, 128), f32)
        d_part = da[0:hd, at]
        qn[at, :] = turned(q_part).astype(bf16)
        dn[at, :] = turned(d_part).astype(bf16)
        delta = jnp.sum(d_part.astype(f32) * exact[:, at], axis=0, keepdims=True)
        qa[0:hd, at] = qa_in[0:hd, at]
        qa[hd:128, at] = special(-lse[0:1, at])
        qa[128:256, at] = qa_in[128:256, at]
        da[hd:128, at] = special(-delta)
        return carry

    lax.fori_loop(0, seq // step, prepare, 0)
    dtab[...] = jnp.zeros_like(dtab)

    def queries_loop(i, carry):
        at = pl.ds(pl.multiple_of(i * bq, bq), bq)
        qa_i, da_i, qn_i, dn_i = qa[:, at], da[:, at], qn[at, :], dn[at, :]

        def keys_loop(j, total):
            run_step(steps, i * (seq // bk) + j)
            keys = pl.ds(pl.multiple_of(j * bk, bk), bk)
            probs = jnp.exp2(mm(ka[keys, :], qa_i))
            grad_logits = (probs * mm(va[keys, :], da_i)).astype(bf16)
            dv[keys, :] += mm(probs.astype(bf16), dn_i)
            dk[keys, :] += mm(grad_logits, qn_i)
            return total + mm(kt[:, keys], grad_logits)

        total = lax.fori_loop(0, seq // bk, keys_loop, jnp.zeros((256, bq), f32))
        rel = jnp.transpose(total[128:256])
        start = band_start(place, i, bq, band)
        parts = []
        for r in range(bq // side):
            y = lax.div(start, side) + r
            block = rel[r * side : (r + 1) * side]
            by_row = jnp.where(lane_side < side, block, 0.0)
            by_col = jnp.where(lane_side < side, 0.0, block)
            by_row = pltpu.roll(by_row, lax.rem(side + 127 - y, 128), 1)
            by_col = pltpu.roll(by_col, side + 1, 1, stride=1, stride_axis=0)
            parts.append(jnp.concatenate([by_row, by_col], axis=1))
        moved = jnp.concatenate(parts, axis=0).astype(bf16)
        dq = total[0:128] * scale + lax.dot_general(
            table[...], moved, (((0,), (1,)), ((), ())), preferred_element_type=f32
        )
        res[2 * hd : 3 * hd, at] = dq[0:hd].astype(bf16)
        dtab[...] += mm(moved, qn_i, TN)
        return carry

    lax.fori_loop(0, seq // bq, queries_loop, 0)

    def finish(c, carry):
        at = pl.ds(pl.multiple_of(c * step, step), step)
        res[0:hd, at] = jnp.transpose(dk[at, :] * scale)[0:hd].astype(bf16)
        res[hd : 2 * hd, at] = jnp.transpose(dv[at, :])[0:hd].astype(bf16)
        return carry

    lax.fori_loop(0, seq // step, finish, 0)
    for s in range(4):
        outs[s][...] = res[:, s * band : (s + 1) * band]
    steps.get("end", lambda: None)()


def bwd_call(grads, kvq, qa, exact, lse, table, hd, side, back, name):
    rows, seq = kvq.shape
    band = seq // 4
    return call(
        functools.partial(bwd_kernel, (hd, side, hd ** (-0.5))),
        (1,),
        [fixed_spec((hd, band))] * 4
        + [fixed_spec(a.shape) for a in (kvq, qa, exact, lse, table)],
        [fixed_spec((rows, band))] * 4 + [fixed_spec((256, 128))],
        [((rows, band), bf16)] * 4 + [((256, 128), f32)],
        [
            pltpu.VMEM((seq, 256), bf16),
            pltpu.VMEM((256, seq), bf16),
            pltpu.VMEM((seq, 128), bf16),
            pltpu.VMEM((256, seq), bf16),
            pltpu.VMEM((128, seq), bf16),
            pltpu.VMEM((seq, 128), bf16),
            pltpu.VMEM((seq, 128), bf16),
            pltpu.VMEM((seq, 128), f32),
            pltpu.VMEM((seq, 128), f32),
            pltpu.VMEM((rows, seq), bf16),
        ],
        name,
        (*grads, kvq, qa, exact, lse, table),
        back,
        vmem=60,
    )


def offset_rows(index, table):
    side = index.shape[0]
    picks = jnp.concatenate([index[::-1, 0], index[0, 1:]])
    hot = (picks[:, None] == jnp.arange(table.shape[0], dtype=jnp.int32)[None, :]).astype(f32)
    rows = jnp.dot(hot, table.astype(f32), precision=highest)
    return hot, jnp.pad(rows, ((0, 1), (0, 128 - table.shape[1]))).astype(bf16)


def fast_device(
    block_input,
    cotangent,
    norm1_gain,
    norm1_shift,
    w_qkv,
    table_rows,
    table_cols,
    w_proj,
    norm2_gain,
    norm2_shift,
    w_fc1,
    w_fc2,
    index_rows,
    index_cols,
):
    images, band_len, share = block_input.shape
    hd = table_rows.shape[1]
    side = index_rows.shape[0]
    width = norm1_gain.shape[0]
    half = width // 2
    heads = w_proj.shape[0] // hd
    t = lax.axis_index("tp")
    z = lax.axis_index("ctx")
    y = lax.axis_index("fsdp")
    spot = t ^ (2 * y)
    first = lax.div(spot, 2) == 0

    def halves(vector):
        return jnp.where(y == 0, vector, jnp.roll(vector, half, axis=-1))

    def lanes(vector):
        return jnp.broadcast_to(halves(vector)[:, None], (width, 128))

    gain1, shift1 = lanes(norm1_gain), lanes(norm1_shift)
    gain2, shift2 = lanes(norm2_gain), lanes(norm2_shift)

    tokens_in = jnp.swapaxes(block_input, 1, 2)
    grads_in = jnp.swapaxes(cotangent, 1, 2)
    own_qkv = jnp.transpose(w_qkv, (1, 2, 0)).reshape(3 * heads * hd, half)
    other_qkv = pxor(own_qkv, "fsdp", 1)
    next_in = tokens_in[1:2]
    inputs = [gather_tp(tokens_in[0:1]), [next_in, pxor(next_in, "tp", 1), pxor(next_in, "tp", 2)]]
    hot_rows, shifted_rows = offset_rows(index_rows, table_rows)
    hot_cols, shifted_cols = offset_rows(index_cols, table_cols)
    table = jnp.concatenate([shifted_rows, shifted_cols], axis=0)
    back_table = jnp.concatenate(
        [shifted_rows, jnp.zeros((1, 128), bf16), shifted_cols[:127][::-1]], axis=0
    )

    def reduce_tp(keep, send):
        got = keep.astype(f32) + pxor(send, "tp", 1).astype(f32)
        mine = jnp.where(first, got[:share], got[share:])
        other = jnp.where(first, got[share:], got[:share]).astype(bf16)
        return mine + pxor(other, "tp", 2).astype(f32)

    state = [{} for _ in range(images)]
    token = [None]

    def ordered(values):
        return values if token[0] is None else after(values, token[0])

    def do_qkv(m, back):
        st = state[m]
        pieces = ordered(tuple(inputs[m]))
        out = qkv_call(0, pieces, gain1, shift1, own_qkv, other_qkv, hd, back, "qkv%d" % m)
        out, extra = out if back.ident is not None else (out, ())
        st["full"], st["act1"], *st["mixed"] = out
        token[0] = st["mixed"][0]
        return extra

    def do_fwd(m, back):
        st = state[m]
        pieces = ordered(tuple(st["mixed"]))
        out, extra = fwd_call(pieces, table, hd, side, back, "attn_fwd%d" % m)
        *st["attn"], st["kvq"], st["exact"], st["lse"], st["qa"] = out
        token[0] = st["lse"]
        return extra

    def do_mlp(m, back):
        st = state[m]
        heads_all = ordered(st["heads"])
        out, extra = mlp_call(
            m, heads_all, st["full"], cots, gain2, shift2, full_proj, full_up, full_down, back
        )
        st["act2"], st["cot"], st["hidden"], st["grad_pre"] = out[:4]
        st["forward"], st["backward"] = out[4:6], out[6:8]
        st["sums2"], st["middle"], st["joined"] = out[8:]
        token[0] = out[8]
        return extra

    def do_gattn(m):
        st = state[m]
        branch = ordered(st["branch"])
        grads = gattn_call(branch, own_proj, hd)
        token[0] = grads[0]
        st["grads"] = swap_ctx(grads)

    def do_bwd(m, back):
        st = state[m]
        pieces = ordered(tuple(st["grads"]))
        out, extra = bwd_call(
            pieces,
            st["kvq"],
            st["qa"],
            st["exact"],
            st["lse"],
            back_table,
            hd,
            side,
            back,
            "attn_bwd%d" % m,
        )
        *st["grad_mixed"], st["dtab"] = out
        token[0] = st["dtab"]
        return extra

    def do_wgrad(left, right):
        parts = [state[m][left] for m in range(images)], [state[m][right] for m in range(images)]
        lefts, rights = ordered((tuple(parts[0]), tuple(parts[1])))
        total = sum(mm(a, b, NT) for a, b in zip(lefts, rights)).astype(bf16)
        token[0] = total
        return total

    first_image, second_image = state
    do_qkv(0, Quiet())
    inputs[1].append(pxor(ordered(inputs[1][2]), "tp", 1))
    got, (own_proj,), (cots,) = do_qkv(
        1,
        Together(
            0,
            SwapCtx(first_image["mixed"]),
            JoinY(w_proj, 1),
            GatherTp(grads_in, (0, 3, "end")),
        ),
    )
    first_image["mixed"] = first_image["mixed"][:1] + list(got)
    got, (full_up,), (full_proj,) = do_fwd(
        0,
        Together(
            1,
            SwapCtx(second_image["mixed"]),
            JoinY(w_fc1, 0),
            GatherTp(own_proj, (0, 10, "end")),
        ),
    )
    full_proj = full_proj.reshape(width, width)
    second_image["mixed"] = second_image["mixed"][:1] + list(got)
    (first_image["heads"],), (full_down,) = do_fwd(
        1,
        Together(
            2,
            SpreadHeads(first_image["attn"], (0, 8, "end", "end")),
            JoinY(w_fc2, 1),
        ),
    )
    ((second_image["heads"],),) = do_mlp(
        0, Together(7, SpreadHeads(second_image["attn"], (0, 2, "end", "end")))
    )
    ((first_image["branch"], first_image["grad_middle"]),) = do_mlp(
        1,
        Together(
            3, ReduceTp(*first_image["backward"], first_image["cot"], (0, 0, "end", "end", "end"))
        ),
    )
    do_gattn(0)
    up_total = do_wgrad("act2", "grad_pre")
    hid = full_down.shape[0]
    split = hid * 3 // 4
    for st in state:
        st["hidden_a"], st["hidden_b"] = st["hidden"][:split], st["hidden"][split:]
    down_total = do_wgrad("cot", "hidden_a")
    down_rest = do_wgrad("cot", "hidden_b")
    (branch, exact, *second_image["grads"]), (grad_down,), (up_low,) = do_bwd(
        0,
        Together(
            4,
            ReduceTp(
                *second_image["backward"], second_image["cot"], (0, 1, 10, 11, "end"), own_proj
            ),
            GradsZThenY(down_total, (0, 4, 10, "end")),
            GradsY(up_total, (0, 13, "end")),
        ),
    )
    second_image["branch"], second_image["grad_middle"] = branch, exact
    proj_total = do_wgrad("branch", "joined")
    (grad_up,), got, (total_0,), (total_1,) = do_bwd(
        1,
        Together(
            5,
            GradsZ(up_low, (0, 11, "end", "end")),
            SwapCtx(first_image["grad_mixed"]),
            ReduceShare(*first_image["forward"], (0, 1, 6, "end")),
            ReduceShare(*second_image["forward"], (6, 7, 12, "end")),
        ),
    )
    first_image["grad_mixed"] = first_image["grad_mixed"][:1] + list(got)
    for st, total in zip(state, (total_0, total_1)):
        st["output"] = (st["middle"] + total).astype(bf16)
    def pair(parts):
        return halves(jnp.sum(sum(parts), axis=2))

    early = pair([st["sums2"] for st in state]).reshape(-1, 128)
    early = jnp.pad(early, ((0, 32 - early.shape[0]), (0, 0)))
    tables = jnp.concatenate([sum(st["dtab"] for st in state), early], axis=0)
    total_0, total_1, grad_qkv, small, grad_rest = tail_call(
        *ordered(
            (
                tuple(first_image["grad_mixed"]),
                first_image["full"],
                first_image["act1"],
                gain1,
                own_qkv,
                other_qkv,
                tables,
                tuple(second_image["grad_mixed"]),
                second_image["full"],
                second_image["act1"],
                jnp.concatenate([proj_total, down_rest], axis=1),
            )
        ),
        hd,
        6,
    )
    token[0] = small
    outputs = [st["output"] for st in state]
    input_grads = [st["grad_middle"] + t for st, t in zip(state, (total_0, total_1))]
    grad_qkv = grad_qkv.reshape(half // 4, 3, heads * hd)

    norms2 = small[256 : 256 + 2 * width // 128].reshape(2, width)
    norms1 = jnp.stack(
        [small[288 + 16 * n : 288 + 16 * n + width // 128].reshape(width) for n in range(2)]
    )
    norms = jnp.concatenate([norms1, norms2], axis=0)
    tabs = small[:256]
    rows_grad = jnp.dot(hot_rows.T, tabs[:127, :hd], precision=highest)
    cols_grad = jnp.dot(hot_cols.T, tabs[129:256, :hd][::-1], precision=highest)
    return (
        jnp.swapaxes(jnp.stack(outputs), 1, 2),
        jnp.swapaxes(jnp.stack(input_grads), 1, 2),
        norms[0],
        norms[1],
        grad_qkv,
        rows_grad,
        cols_grad,
        grad_rest[:, : heads * hd].T,
        norms[2],
        norms[3],
        grad_up,
        jnp.concatenate([grad_down, grad_rest[:, heads * hd :]], axis=1).T,
    )


def per_device(*args):
    block_input, w_proj, table_rows, index_rows = args[0], args[7], args[5], args[12]
    heads = w_proj.shape[0] // table_rows.shape[1]
    fits = (
        lax.axis_size("tp") == 4
        and lax.axis_size("ctx") == 4
        and lax.axis_size("fsdp") == 2
        and heads == 4
        and index_rows.shape[0] == 64
        and table_rows.shape[1] == 80
        and block_input.shape[1] % 512 == 0
        and block_input.shape[0] == 2
    )
    return fast_device(*args) if fits else plain_device(*args)


def solution(mesh):
    in_specs = (
        P("fsdp", "ctx", "tp"),
        P("fsdp", "ctx", "tp"),
        P(),
        P(),
        P("fsdp", None, "tp"),
        P(),
        P(),
        P("tp", "fsdp"),
        P(),
        P(),
        P("fsdp", "tp"),
        P("tp", "fsdp"),
        P(),
        P(),
    )
    out_specs = (
        P("fsdp", "ctx", "tp"),
        P("fsdp", "ctx", "tp"),
        P(),
        P(),
        P(("fsdp", "ctx"), None, "tp"),
        P(),
        P(),
        P("tp", ("fsdp", "ctx")),
        P(),
        P(),
        P(("fsdp", "ctx"), "tp"),
        P("tp", ("fsdp", "ctx")),
    )
    return jax.shard_map(
        per_device, mesh=mesh, in_specs=in_specs, out_specs=out_specs, check_vma=False
    )
```
